32 devices in a mesh: wide: 8 (over z, y), narrow: 4 (over x, core).
Axes of the slice: x: 2, y: 2, z: 4, core: 2. Of those that a mesh axis runs over, the one named last changes fastest.
Arguments:
- inputs: bfloat16 [2, 1024, 1024], P(None, 'wide', 'narrow'), may hold values from -6 to 6
- attn_gain: float32 [1024], P('narrow'), may hold values from 0.5 to 1.5
- query_key_value_weight: bfloat16 [1024, 3, 1024], P('wide', None, 'narrow'), may hold values from -0.1875 to 0.1875
- attention_out_weight: bfloat16 [1024, 1024], P('narrow', 'wide'), may hold values from -4 to 4
- mlp_gain: float32 [1024], P('narrow'), may hold values from 0.5 to 1.5
- feedforward_in_weight: bfloat16 [1024, 2, 2624], P('wide', None, 'narrow'), may hold values from -0.1875 to 0.1875
- feedforward_out_weight: bfloat16 [2624, 1024], P('narrow', 'wide'), may hold values from -0.125 to 0.125
- grad_out: bfloat16 [2, 1024, 1024], P(None, 'wide', 'narrow'), may hold values from -6 to 6
Outputs:
- outputs: bfloat16 [2, 1024, 1024], P(None, 'wide', 'narrow')
- grad_inputs: float32 [2, 1024, 1024], P(None, 'wide', 'narrow')
- grad_attn_gain: float32 [1024], P('narrow')
- grad_w_qkv: float32 [1024, 3, 1024], P('wide', None, 'narrow')
- grad_w_attn_out: float32 [1024, 1024], P('narrow', 'wide')
- grad_mlp_gain: float32 [1024], P('narrow')
- grad_w_in: float32 [1024, 2, 2624], P('wide', None, 'narrow')
- grad_w_mlp_out: float32 [2624, 1024], P('narrow', 'wide')
The draws below stay inside these ranges and needn't reach their ends.
All inputs are finite; a program needn't handle non-finite values.
Results may differ from the reference program's by a relative error of at most 0.014.
Values may be sent and summed in bfloat16 or wider, within the bound.
No kernel may reach another device: no remote copies, remote signals or barrier semaphores. Data moves between devices by JAX's collectives and lax.ppermute only.
A program may use at most 128 MiB of HBM per device.

```python
import jax
import jax.numpy as jnp
from jax import lax

D = 1024
HEADS = 16
HEAD_DIM = 64
FF = 2624
SEQS = 2
LENGTH = 1024


def block_scale(rng, dims, split, least, top_value):
    factor_of = 1.0
    for position, shards_of in split:
        heights = jax.random.uniform(jax.random.fold_in(jax.random.fold_in(rng, 6), position), (shards_of,), jnp.float32, least / len(split), top_value / len(split))
        factor_of = factor_of * jnp.repeat(jnp.exp(heights), dims[position] // shards_of).reshape((-1,) + (1,) * (len(dims) - 1 - position))
    return factor_of


def normal_values(rng, dims, spread, most, cuts=(), held_as=jnp.bfloat16):
    drawn = jax.random.normal(rng, dims, jnp.float32) * spread
    if len(cuts) > 0:
        drawn = block_scale(rng, dims, cuts, -0.22, 0.18) * drawn
    return jnp.clip(drawn, min=-most, max=most).astype(held_as)


def setup_inputs(seed: int = 0) -> dict:
    streams_of = jax.random.split(jax.random.key(seed), 9)
    return {
        "inputs": normal_values(streams_of[0], (SEQS, LENGTH, D), 1.0, 6.0, ((1, 8), (2, 4))),
        "attn_gain": jnp.clip(1.0 + 0.1 * jax.random.normal(streams_of[1], (D,), jnp.float32), 0.5, 1.5),
        "query_key_value_weight": normal_values(streams_of[2], (D, 3, D), D ** -0.5, 0.1875, ((0, 8), (2, 4))),
        "attention_out_weight": normal_values(streams_of[3], (D, D), (max(1, 2048 // LENGTH)) ** -0.5, 4.0, ((0, 4), (1, 8))),
        "mlp_gain": jnp.clip(1.0 + 0.1 * jax.random.normal(streams_of[4], (D,), jnp.float32), 0.5, 1.5),
        "feedforward_in_weight": normal_values(streams_of[5], (D, 2, FF), D ** -0.5, 0.1875, ((0, 8), (2, 4))),
        "feedforward_out_weight": normal_values(streams_of[6], (FF, D), FF ** -0.5, 0.125, ((0, 4), (1, 8))),
        "grad_out": normal_values(streams_of[7], (SEQS, LENGTH, D), 1.0, 6.0, ((1, 8), (2, 4))),
    }


@jax.custom_vjp
def low(v):
    return lax.optimization_barrier(v.astype(jnp.bfloat16)).astype(jnp.float32)

@jax.custom_vjp
def reduced_precision_back(v):
    return v

def low_keep(v):
    return (low(v), None)

def low_pass(kept, grad):
    return (grad,)

def back_keep(v):
    return (v, None)

def back_low(kept, grad):
    return (low(grad),)
low.defvjp(low_keep, low_pass)
reduced_precision_back.defvjp(back_keep, back_low)
highest_precision = lax.Precision.HIGHEST
eps_norm = 1e-05
rope_base = 160000.0

def layer_norm(resid, gain):
    average = lax.optimization_barrier(jnp.mean(resid, axis=-1, keepdims=True))
    variance = lax.optimization_barrier(jnp.mean(resid * resid, axis=-1, keepdims=True)) - average * average
    return (resid - average) * lax.rsqrt(variance + eps_norm) * gain

def rotary(tensor, positions):
    half_dim = tensor.shape[-1] // 2
    frequency = rope_base ** (-jnp.arange(half_dim).astype(jnp.float32) * 2.0 / tensor.shape[-1])
    angles = positions[:, None] * frequency[None, :]
    angles = jnp.concatenate([angles, angles], axis=-1)[:, None, :]
    rotated = jnp.concatenate([-tensor[..., half_dim:], tensor[..., :half_dim]], axis=-1)
    return tensor * jnp.cos(angles) + rotated * jnp.sin(angles)

def attend_one(items):
    query_rows, key_rows, value_rows = items
    score_scale = HEAD_DIM ** (-0.5)
    scores = reduced_precision_back(jnp.dot(query_rows, key_rows.T, precision=highest_precision, preferred_element_type=jnp.float32) * score_scale)
    attn_probs = low(jax.nn.softmax(scores, axis=-1))
    return jnp.dot(attn_probs, value_rows, precision=highest_precision, preferred_element_type=jnp.float32)

def forward(inputs, attn_gain, query_key_value_weight, attention_out_weight, mlp_gain, feedforward_in_weight, feedforward_out_weight):
    normed_input = low(layer_norm(inputs, attn_gain))
    projected_rows = reduced_precision_back(jnp.einsum('eai,iqz->eaqz', normed_input, query_key_value_weight, precision=highest_precision))
    positions = jnp.arange(LENGTH).astype(jnp.float32)
    split_heads = (SEQS, LENGTH, HEADS, HEAD_DIM)
    queries = low(rotary(projected_rows[:, :, 0].reshape(split_heads), positions))
    keys = low(rotary(projected_rows[:, :, 1].reshape(split_heads), positions))
    values = low(projected_rows[:, :, 2].reshape(split_heads))

    def arrange(tensor):
        return tensor.transpose(0, 2, 1, 3).reshape(SEQS * HEADS, LENGTH, HEAD_DIM)
    mixed = lax.map(jax.checkpoint(attend_one), (arrange(queries), arrange(keys), arrange(values)))
    mixed = mixed.reshape(SEQS, HEADS, LENGTH, HEAD_DIM).transpose(0, 2, 1, 3).reshape(SEQS, LENGTH, D)
    attention_context = low(reduced_precision_back(mixed))
    attention_branch = reduced_precision_back(jnp.einsum('cif,fj->cij', attention_context, attention_out_weight, precision=highest_precision))
    middle = inputs + attention_branch
    normed_middle = low(layer_norm(middle, mlp_gain))
    gate_and_lift = reduced_precision_back(jnp.einsum('xij,jkq->xikq', normed_middle, feedforward_in_weight, precision=highest_precision))
    gelu_activated_rows = low(jax.nn.gelu(gate_and_lift[:, :, 0], approximate=False) * gate_and_lift[:, :, 1])
    feedforward_branch = reduced_precision_back(jnp.einsum('wbj,jr->wbr', gelu_activated_rows, feedforward_out_weight, precision=highest_precision))
    return middle + feedforward_branch

def reference(inputs, attn_gain, query_key_value_weight, attention_out_weight, mlp_gain, feedforward_in_weight, feedforward_out_weight, grad_out):
    primals = (inputs.astype(jnp.float32), attn_gain.astype(jnp.float32), query_key_value_weight.astype(jnp.float32), attention_out_weight.astype(jnp.float32), mlp_gain.astype(jnp.float32), feedforward_in_weight.astype(jnp.float32), feedforward_out_weight.astype(jnp.float32))
    result, pullback = jax.vjp(forward, *primals)
    gradients = pullback(grad_out.astype(jnp.float32))
    return (result.astype(jnp.bfloat16), gradients[0], gradients[1], gradients[2], gradients[3], gradients[4], gradients[5], gradients[6])
```

```python
import functools

import jax
import jax.numpy as jnp
from jax import lax
from jax.sharding import PartitionSpec as P

HEAD_DIM = 64
eps_norm = 1e-05
rope_base = 160000.0
f32 = jnp.float32
bf16 = jnp.bfloat16


def rope_tables(positions):
    half_dim = HEAD_DIM // 2
    frequency = rope_base ** (-jnp.arange(half_dim).astype(f32) * 2.0 / HEAD_DIM)
    angles = positions[:, None] * frequency[None, :]
    angles = jnp.concatenate([angles, angles], axis=-1)[:, None, :]
    return jnp.cos(angles), jnp.sin(angles)


def rotary(tensor, cosine, sine):
    half_dim = HEAD_DIM // 2
    rotated = jnp.concatenate([-tensor[..., half_dim:], tensor[..., :half_dim]], axis=-1)
    return tensor * cosine + rotated * sine


def rotary_transposed(tensor, cosine, sine):
    half_dim = HEAD_DIM // 2
    turned = tensor * sine
    back = jnp.concatenate([turned[..., half_dim:], -turned[..., :half_dim]], axis=-1)
    return tensor * cosine + back


def norm_forward(rows, gain):
    width = rows.shape[-1]
    average = jnp.sum(rows, axis=-1, keepdims=True) / width
    variance = jnp.sum(rows * rows, axis=-1, keepdims=True) / width - average * average
    inverse = lax.rsqrt(variance + eps_norm)
    centred = (rows - average) * inverse
    return (centred * gain).astype(bf16), centred, inverse


def norm_backward(grad_normed, centred, inverse, gain):
    width = grad_normed.shape[-1]
    scaled = grad_normed * gain
    row_total = jnp.sum(scaled, axis=-1, keepdims=True)
    row_along = jnp.sum(scaled * centred, axis=-1, keepdims=True)
    return inverse * (scaled - row_total / width - centred * (row_along / width))


def gated_unit(gate, lift):
    return jax.nn.gelu(gate, approximate=False) * lift


def pick(array, index, axis=0):
    return lax.dynamic_index_in_dim(array, index, axis=axis, keepdims=False)


def place(pieces, own, axis):
    count = len(pieces)
    if count == 1:
        return pieces[0]
    if count == 2:
        return jnp.where(
            own == 0,
            jnp.concatenate(pieces, axis=axis),
            jnp.concatenate(pieces[::-1], axis=axis),
        )
    size = pieces[0].shape[axis]
    shape = list(pieces[0].shape)
    shape[axis] = size * count
    whole = jnp.zeros(shape, pieces[0].dtype)
    for relative, piece in enumerate(pieces):
        whole = lax.dynamic_update_slice_in_dim(whole, piece, (own ^ relative) * size, axis)
    return whole


def body(
    wide,
    narrow,
    inputs,
    attn_gain,
    query_key_value_weight,
    attention_out_weight,
    mlp_gain,
    feedforward_in_weight,
    feedforward_out_weight,
    grad_out,
):
    groups, columns = wide // 2, narrow // 2
    _, block, width = inputs.shape
    model = width * narrow
    depth = query_key_value_weight.shape[0]
    hidden = feedforward_out_weight.shape[0] // 2
    half = width // 2
    part = block // columns
    rows = 2 * block
    heads = width // HEAD_DIM
    score_scale = HEAD_DIM ** (-0.5)
    wide_at, narrow_at = lax.axis_index("wide"), lax.axis_index("narrow")
    group, side = wide_at // 2, wide_at % 2
    column, core = narrow_at // 2, narrow_at % 2
    dot = functools.partial(jnp.einsum, preferred_element_type=f32)

    def swap(array, mask):
        if mask == 0:
            return array
        return lax.ppermute(
            array, ("wide", "narrow"), [(i, i ^ mask) for i in range(wide * narrow)]
        )

    def over_chips(column_rel, side_rel):
        return 2 * column_rel + narrow * side_rel

    def over_groups(group_rel):
        return 2 * narrow * group_rel

    def fetch(bundle):
        received = swap(pick(bundle, 1 - side), narrow)
        pair = place([pick(bundle, side), received], side, 0)
        whole = place([swap(pair, over_groups(k)) for k in range(groups)], group, 0)
        return whole, swap(whole, 1)

    def halves(array):
        return array.reshape(depth, -1, 2, array.shape[-1] // 2).transpose(2, 0, 1, 3)

    attn_bundle = jnp.concatenate(
        [halves(query_key_value_weight), halves(attention_out_weight.T[:, None])], axis=2
    ).reshape(2, depth, 4 * half)
    mlp_bundle = jnp.concatenate(
        [halves(feedforward_in_weight), halves(feedforward_out_weight.T[:, None])], axis=2
    ).reshape(2, depth, 3 * hidden)

    both = jnp.stack([inputs, grad_out])
    received = swap(pick(both, 1 - core, 1), 1)
    features = place([pick(both, core, 1), received], core, 2)

    def gather_features(array):
        return jnp.concatenate(
            [
                place([swap(array, over_chips(k, s)) for k in range(columns)], column, 1)
                for s in range(2)
            ],
            axis=0,
        )

    def gather_rows(array):
        return jnp.concatenate(
            [
                place([swap(array, over_chips(k, s)) for k in range(columns)], column, 0)
                for s in range(2)
            ],
            axis=0,
        )

    def scatter_rows(array):
        blocks = array.reshape(2, columns, part, model)
        total = pick(blocks[0], column)
        for s in range(2):
            for k in range(columns):
                if k or s:
                    piece = pick(blocks[s], column ^ k).astype(bf16)
                    total = total + swap(piece, over_chips(k, s)).astype(f32)
        return total

    def own_rows(array):
        return pick(array.reshape(2, columns, part, -1)[0], column)

    gains = jnp.stack([attn_gain, mlp_gain])
    gains = place([gains, swap(gains, 1)], core, 1)
    gains = place([swap(gains, 2 * k) for k in range(columns)], column, 1)

    resid_in = gather_features(features[0]).astype(f32)
    attn_own, attn_other = fetch(attn_bundle)
    attn_weight = jnp.stack([attn_own, attn_other]).reshape(2, model, 4, half)
    qkv_weight, out_weight = attn_weight[:, :, :3], attn_weight[:, :, 3]
    grad_rows = gather_features(features[1])
    mlp_own, mlp_other = fetch(mlp_bundle)
    mlp_weight = jnp.stack([mlp_own, mlp_other]).reshape(2, model, 3, hidden)
    in_weight, down_weight = mlp_weight[:, :, :2], mlp_weight[:, :, 2]
    chips = [(k, s) for s in range(2) for k in range(columns)]
    out_pieces = jnp.stack([swap(out_weight[0], over_chips(k, s)) for k, s in chips])
    out_whole = jnp.stack([out_pieces, swap(out_pieces, 1)])

    token = (jnp.arange(rows) // block) ^ side
    positions = ((group * 2 + token) * block + jnp.arange(rows) % block).astype(f32)
    cosine, sine = rope_tables(positions)

    normed_input, centred_one, inverse_one = norm_forward(resid_in, gains[0])
    projected = dot("td,bdcm->tcbm", normed_input, qkv_weight).reshape(rows, 3, heads, HEAD_DIM)
    queries = rotary(projected[:, 0], cosine, sine).astype(bf16)
    keys_local = rotary(projected[:, 1], cosine, sine).astype(bf16).reshape(rows, width)
    values_local = projected[:, 2].astype(bf16).reshape(rows, width)

    def gather_groups(array):
        return jnp.concatenate([swap(array, over_groups(k)) for k in range(groups)], axis=0)

    keys = gather_groups(keys_local).reshape(-1, heads, HEAD_DIM)
    values = gather_groups(values_local).reshape(-1, heads, HEAD_DIM)
    scores = dot("qhe,khe->hqk", queries, keys) * score_scale
    row_peak = jnp.max(scores, axis=-1, keepdims=True)
    log_total = row_peak + jnp.log(jnp.sum(jnp.exp(scores - row_peak), axis=-1, keepdims=True))
    probs = jnp.exp(scores - log_total).astype(bf16)
    context = dot("hqk,khe->qhe", probs, values).astype(bf16).reshape(rows, width)

    def from_chip(array, k, s):
        array = swap(array, over_chips(k, s))
        return jnp.concatenate([array[block:], array[:block]], axis=0) if s else array

    contexts = jnp.stack([from_chip(context, k, s) for k, s in chips]).reshape(
        len(chips), rows, 2, half
    )
    middle = resid_in + dot("ptbm,bpdm->td", contexts, out_whole)
    normed_middle, centred_two, inverse_two = norm_forward(middle, gains[1])
    gate_up = dot("td,bdcf->ctbf", normed_middle, in_weight)
    activated_full, unit_back = jax.vjp(gated_unit, gate_up[0], gate_up[1])
    activated = activated_full.astype(bf16)
    grad_activated = dot("td,bdf->tbf", grad_rows, down_weight)
    grad_gate_up = jnp.stack(unit_back(grad_activated)).astype(bf16)
    grad_two_partial = dot("ctbf,bdcf->td", grad_gate_up, in_weight)
    grad_two = scatter_rows(grad_two_partial)
    grad_result_rows = own_rows(grad_rows).astype(f32)
    grad_middle = grad_result_rows + norm_backward(
        grad_two, own_rows(centred_two), own_rows(inverse_two), gains[1]
    )
    grad_attn = gather_rows(grad_middle.astype(bf16))

    branch = dot("tbf,bdf->td", activated, down_weight).reshape(2, block, columns, 2 * width)
    total = pick(branch[0] + middle.reshape(2, block, columns, 2 * width)[0], column, 1)
    for k, s in chips:
        if k or s:
            piece = pick(branch[s], column ^ k, 1).astype(bf16)
            total = total + swap(piece, over_chips(k, s)).astype(f32)
    total = total.astype(bf16).reshape(block, 2, width)
    result = place(
        [pick(total, core, 1)[None], swap(pick(total, 1 - core, 1), 1)[None]], core, 0
    )

    def reduce_weight(own, other):
        total = own + swap(other.astype(bf16), 1).astype(f32)
        blocks = total.reshape(groups, 2 * depth, -1)
        total = pick(blocks, group)
        for k in range(1, groups):
            total = total + swap(pick(blocks, group ^ k).astype(bf16), over_groups(k)).astype(f32)
        total = total.reshape(2, depth, -1)
        kept = pick(total, side)
        received = swap(pick(total, 1 - side).astype(bf16), narrow).astype(f32)
        return place([kept[None], received[None]], side, 0)

    def join(array):
        return array.transpose(1, 2, 0, 3).reshape(depth, array.shape[2], -1)

    grad_down = dot("td,tbf->bdf", grad_rows, activated)
    grad_in = dot("td,ctbf->bdcf", normed_middle, grad_gate_up)
    grad_mlp = jnp.concatenate([grad_in, grad_down[:, :, None]], axis=2).reshape(
        2, model, 3 * hidden
    )
    grad_mlp = join(reduce_weight(grad_mlp[0], grad_mlp[1]).reshape(2, depth, 3, hidden))

    grad_context = dot("td,bdm->tbm", grad_attn, out_weight).astype(bf16)
    grad_out_weight = dot("td,tbm->bdm", grad_attn, context.reshape(rows, 2, half))
    grad_context = grad_context.reshape(rows, heads, HEAD_DIM)
    probs_again = jnp.exp(dot("qhe,khe->hqk", queries, keys) * score_scale - log_total)
    probs_low = probs_again.astype(bf16)

    def scatter_groups(array):
        blocks = array.reshape(groups, rows, width)
        total = blocks[0]
        for k in range(1, groups):
            total = total + swap(blocks[k].astype(bf16), over_groups(k)).astype(f32)
        return total

    grad_values = scatter_groups(dot("hqk,qhe->khe", probs_low, grad_context))
    grad_probs = dot("qhe,khe->hqk", grad_context, values)
    row_delta = jnp.sum(probs_again * grad_probs, axis=-1, keepdims=True)
    grad_scores = (probs_again * (grad_probs - row_delta)).astype(bf16)
    grad_keys = scatter_groups(dot("hqk,qhe->khe", grad_scores, queries) * score_scale)
    grad_queries = dot("hqk,khe->qhe", grad_scores, keys) * score_scale
    grad_projected = jnp.stack(
        [
            rotary_transposed(grad_queries, cosine, sine),
            rotary_transposed(grad_keys.reshape(rows, heads, HEAD_DIM), cosine, sine),
            grad_values.reshape(rows, heads, HEAD_DIM),
        ],
        axis=1,
    ).astype(bf16).reshape(rows, 3, 2, half)
    grad_one_partial = dot("tcbm,bdcm->td", grad_projected, qkv_weight)
    grad_one = scatter_rows(grad_one_partial)
    grad_qkv = dot("td,tcbm->bdcm", normed_input, grad_projected)
    grad_attn_weight = jnp.concatenate([grad_qkv, grad_out_weight[:, :, None]], axis=2).reshape(
        2, model, 4 * half
    )
    grad_attn_weight = join(
        reduce_weight(grad_attn_weight[0], grad_attn_weight[1]).reshape(2, depth, 4, half)
    )
    grad_rows_in = grad_middle + norm_backward(
        grad_one, own_rows(centred_one), own_rows(inverse_one), gains[0]
    )
    by_owner = grad_rows_in.reshape(part, columns, 2, width)

    def send(k, c):
        piece = pick(pick(by_owner, column ^ k, 1), core ^ c, 1)
        return swap(piece, 2 * k + c)

    grad_inputs = place(
        [
            place([send(k, c) for k in range(columns)], column, 0)[None]
            for c in range(2)
        ],
        core,
        0,
    )

    gain_grads = jnp.stack(
        [
            jnp.sum(grad_one_partial * centred_one, axis=0),
            jnp.sum(grad_two_partial * centred_two, axis=0),
        ]
    ).reshape(2, narrow, width)
    gain_total = pick(gain_grads, narrow_at, 1)
    for m in range(1, narrow):
        gain_total = gain_total + swap(pick(gain_grads, narrow_at ^ m, 1), m)
    gain_total = lax.psum(gain_total, "wide")
    return (
        result,
        grad_inputs,
        gain_total[0],
        grad_attn_weight[:, :3],
        grad_attn_weight[:, 3].T,
        gain_total[1],
        grad_mlp[:, :2],
        grad_mlp[:, 2].T,
    )


def solution(mesh):
    in_specs = (
        P(None, "wide", "narrow"),
        P("narrow"),
        P("wide", None, "narrow"),
        P("narrow", "wide"),
        P("narrow"),
        P("wide", None, "narrow"),
        P("narrow", "wide"),
        P(None, "wide", "narrow"),
    )
    out_specs = (
        P(None, "wide", "narrow"),
        P(None, "wide", "narrow"),
        P("narrow"),
        P("wide", None, "narrow"),
        P("narrow", "wide"),
        P("narrow"),
        P("wide", None, "narrow"),
        P("narrow", "wide"),
    )
    step = functools.partial(body, mesh.shape["wide"], mesh.shape["narrow"])
    return jax.shard_map(step, mesh=mesh, in_specs=in_specs, out_specs=out_specs, check_vma=False)
```

```python
import functools

import jax
import jax.numpy as jnp
from jax import lax
from jax.sharding import PartitionSpec as P

HEAD_DIM = 64
eps_norm = 1e-05
rope_base = 160000.0
f32 = jnp.float32
bf16 = jnp.bfloat16


def rope_tables(positions):
    half_dim = HEAD_DIM // 2
    frequency = rope_base ** (-jnp.arange(half_dim).astype(f32) * 2.0 / HEAD_DIM)
    angles = positions[:, None] * frequency[None, :]
    angles = jnp.concatenate([angles, angles], axis=-1)[:, None, :]
    return jnp.cos(angles), jnp.sin(angles)


def rotary(tensor, cosine, sine):
    half_dim = HEAD_DIM // 2
    rotated = jnp.concatenate([-tensor[..., half_dim:], tensor[..., :half_dim]], axis=-1)
    return tensor * cosine + rotated * sine


def rotary_transposed(tensor, cosine, sine):
    half_dim = HEAD_DIM // 2
    turned = tensor * sine
    back = jnp.concatenate([turned[..., half_dim:], -turned[..., :half_dim]], axis=-1)
    return tensor * cosine + back


def norm_forward(rows, gain):
    width = rows.shape[-1]
    average = jnp.sum(rows, axis=-1, keepdims=True) / width
    variance = jnp.sum(rows * rows, axis=-1, keepdims=True) / width - average * average
    inverse = lax.rsqrt(variance + eps_norm)
    centred = (rows - average) * inverse
    return (centred * gain).astype(bf16), centred, inverse


def norm_backward(grad_normed, centred, inverse, gain):
    width = grad_normed.shape[-1]
    scaled = grad_normed * gain
    row_total = jnp.sum(scaled, axis=-1, keepdims=True)
    row_along = jnp.sum(scaled * centred, axis=-1, keepdims=True)
    return inverse * (scaled - row_total / width - centred * (row_along / width))


def gated_unit(gate, lift):
    return jax.nn.gelu(gate, approximate=False) * lift


def pick(array, index, axis=0):
    return lax.dynamic_index_in_dim(array, index, axis=axis, keepdims=False)


def ring_masks(count):
    masks, unit = [], 1
    while unit < count:
        masks += [unit] + ([3 * unit] if 4 * unit <= count else [])
        unit *= 4
    return masks


def place(pieces, own, axis):
    count = len(pieces)
    if count == 1:
        return pieces[0]
    if count == 2:
        return jnp.where(
            own == 0,
            jnp.concatenate(pieces, axis=axis),
            jnp.concatenate(pieces[::-1], axis=axis),
        )
    size = pieces[0].shape[axis]
    shape = list(pieces[0].shape)
    shape[axis] = size * count
    whole = jnp.zeros(shape, pieces[0].dtype)
    for relative, piece in enumerate(pieces):
        whole = lax.dynamic_update_slice_in_dim(whole, piece, (own ^ relative) * size, axis)
    return whole


def body(
    wide,
    narrow,
    inputs,
    attn_gain,
    query_key_value_weight,
    attention_out_weight,
    mlp_gain,
    feedforward_in_weight,
    feedforward_out_weight,
    grad_out,
):
    groups, columns = wide // 2, narrow // 2
    _, block, width = inputs.shape
    model = width * narrow
    depth = query_key_value_weight.shape[0]
    hidden = feedforward_out_weight.shape[0] // 2
    half = width // 2
    part = block // columns
    rows = 2 * block
    heads = width // HEAD_DIM
    score_scale = HEAD_DIM ** (-0.5)
    wide_at, narrow_at = lax.axis_index("wide"), lax.axis_index("narrow")
    group, side = wide_at // 2, wide_at % 2
    column, core = narrow_at // 2, narrow_at % 2
    dot = functools.partial(jnp.einsum, preferred_element_type=f32)

    def swap(array, mask):
        if mask == 0:
            return array
        return lax.ppermute(
            array, ("wide", "narrow"), [(i, i ^ mask) for i in range(wide * narrow)]
        )

    def over_chips(column_rel, side_rel):
        return 2 * column_rel + narrow * side_rel

    def over_groups(group_rel):
        return 2 * narrow * group_rel

    def after(array, *others):
        return lax.optimization_barrier((array, *others))[0]

    def gather_ring(array, unit, count):
        if count == 1:
            return [array]
        if count == 2:
            return [array, swap(array, unit)]
        cut = array.shape[0] // 2
        near, far = swap(array, unit), swap(array, 3 * unit)
        across = jnp.concatenate([swap(far[:cut], unit), swap(near[cut:], 3 * unit)], axis=0)
        quad = [array, near, across, far]
        if count == 4:
            return quad
        return [q for quads in gather_ring(jnp.stack(quad, 1), 4 * unit, count // 4) for q in jnp.moveaxis(quads, 1, 0)]

    def scatter_ring(pieces, unit):
        count = len(pieces)
        if count == 1:
            return pieces[0]
        if count == 2:
            return pieces[0] + swap(pieces[1].astype(bf16), unit).astype(f32)
        if count > 4:
            stacked = [jnp.stack(pieces[k : k + 4], 1) for k in range(0, count, 4)]
            pieces = list(jnp.moveaxis(scatter_ring(stacked, 4 * unit), 1, 0))
        own, near, across, far = pieces
        cut = own.shape[0] // 2
        across = across.astype(bf16)
        for_far = swap(across[:cut], unit).astype(f32)
        for_near = swap(across[cut:], 3 * unit).astype(f32)
        near = jnp.concatenate([near[:cut], near[cut:] + for_near], axis=0).astype(bf16)
        far = jnp.concatenate([far[:cut] + for_far, far[cut:]], axis=0).astype(bf16)
        return own + swap(near, unit).astype(f32) + swap(far, 3 * unit).astype(f32)

    def fetch_side(bundle):
        received = swap(pick(bundle, 1 - side), narrow)
        return place([pick(bundle, side), received], side, 0)

    def fetch_groups(pair):
        return place(gather_ring(pair, 2 * narrow, groups), group, 0)

    def halves(array):
        return array.reshape(depth, -1, 2, array.shape[-1] // 2).transpose(2, 0, 1, 3)

    qkv_bundle = halves(query_key_value_weight).reshape(2, depth, 3 * half)
    out_bundle = halves(attention_out_weight.T[:, None]).reshape(2, depth, half)
    mlp_bundle = jnp.concatenate(
        [halves(feedforward_in_weight), halves(feedforward_out_weight.T[:, None])], axis=2
    ).reshape(2, depth, 3 * hidden)

    both = jnp.stack([inputs, grad_out])
    received = swap(pick(both, 1 - core, 1), 1)
    features = place([pick(both, core, 1), received], core, 2)

    def gather_features(array):
        return jnp.concatenate(
            [
                place([swap(array, over_chips(k, s)) for k in range(columns)], column, 1)
                for s in range(2)
            ],
            axis=0,
        )

    def gather_rows(array):
        return jnp.concatenate(
            [
                place([swap(array, over_chips(k, s)) for k in range(columns)], column, 0)
                for s in range(2)
            ],
            axis=0,
        )

    def scatter_rows(array):
        blocks = array.reshape(2, columns, part, model)
        total = pick(blocks[0], column)
        for s in range(2):
            for k in range(columns):
                if k or s:
                    piece = pick(blocks[s], column ^ k).astype(bf16)
                    total = total + swap(piece, over_chips(k, s)).astype(f32)
        return total

    def own_rows(array):
        return pick(array.reshape(2, columns, part, -1)[0], column)

    qkv_pair = fetch_side(qkv_bundle)
    shards = after(features[0], qkv_pair)
    resid_in = gather_features(shards)
    qkv_own = fetch_groups(qkv_pair)
    gains = jnp.stack([attn_gain, mlp_gain])
    gains = place([gains, swap(gains, 1)], core, 1)
    gains = place([swap(gains, 2 * k) for k in range(columns)], column, 1)
    out_pair = fetch_side(after(out_bundle, resid_in))
    mlp_pair = fetch_side(after(mlp_bundle, resid_in))
    qkv_own, out_pair = lax.optimization_barrier((qkv_own, out_pair))
    qkv_weight = jnp.stack([qkv_own, swap(qkv_own, 1)]).reshape(2, model, 3, half)
    resid_in = resid_in.astype(f32)
    token = (jnp.arange(rows) // block) ^ side
    positions = ((group * 2 + token) * block + jnp.arange(rows) % block).astype(f32)
    cosine, sine = rope_tables(positions)

    normed_input, centred_one, inverse_one = norm_forward(resid_in, gains[0])
    projected = dot("td,bdcm->tcbm", normed_input, qkv_weight).reshape(rows, 3, heads, HEAD_DIM)
    queries = rotary(projected[:, 0], cosine, sine).astype(bf16)
    keys_local = rotary(projected[:, 1], cosine, sine).astype(bf16).reshape(rows, width)
    values_local = projected[:, 2].astype(bf16).reshape(rows, width)

    pairs = jnp.stack([keys_local, values_local], axis=1)
    pairs = jnp.concatenate(gather_ring(pairs, 2 * narrow, groups), axis=0)
    out_own = fetch_groups(after(out_pair, keys_local))
    out_weight = jnp.stack([out_own, swap(out_own, 1)])
    grad_rows = gather_features(after(features[1], keys_local))
    chips = [(k, s) for s in range(2) for k in range(columns)]
    out_pieces = jnp.stack([swap(after(out_own, grad_rows), over_chips(k, s)) for k, s in chips])
    out_whole = jnp.stack([out_pieces, swap(out_pieces, 1)])
    mlp_pair = after(mlp_pair, pairs)
    mlp_own = fetch_groups(mlp_pair)
    mlp_weight = jnp.stack([mlp_own, swap(mlp_own, 1)]).reshape(2, model, 3, hidden)
    in_weight, down_weight = mlp_weight[:, :, :2], mlp_weight[:, :, 2]
    keys = pairs[:, 0].reshape(-1, heads, HEAD_DIM)
    values = pairs[:, 1].reshape(-1, heads, HEAD_DIM)
    scores = dot("qhe,khe->hqk", queries, keys) * score_scale
    row_peak = jnp.max(scores, axis=-1, keepdims=True)
    log_total = row_peak + jnp.log(jnp.sum(jnp.exp(scores - row_peak), axis=-1, keepdims=True))
    probs = jnp.exp(scores - log_total).astype(bf16)
    context = dot("hqk,khe->qhe", probs, values).astype(bf16).reshape(rows, width)

    def from_chip(array, k, s):
        array = swap(array, over_chips(k, s))
        return jnp.concatenate([array[block:], array[:block]], axis=0) if s else array

    contexts = jnp.stack([from_chip(context, k, s) for k, s in chips]).reshape(
        len(chips), rows, 2, half
    )
    middle = resid_in + dot("ptbm,bpdm->td", contexts, out_whole)
    normed_middle, centred_two, inverse_two = norm_forward(middle, gains[1])
    gate_up = dot("td,bdcf->ctbf", normed_middle, in_weight)
    activated_full, unit_back = jax.vjp(gated_unit, gate_up[0], gate_up[1])
    activated = activated_full.astype(bf16)
    grad_activated = dot("td,bdf->tbf", grad_rows, down_weight)
    grad_gate_up = jnp.stack(unit_back(grad_activated)).astype(bf16)
    grad_two_partial = dot("ctbf,bdcf->td", grad_gate_up, in_weight)
    grad_two = scatter_rows(grad_two_partial)
    grad_result_rows = own_rows(grad_rows).astype(f32)
    grad_middle = grad_result_rows + norm_backward(
        grad_two, own_rows(centred_two), own_rows(inverse_two), gains[1]
    )
    def reduce_cores(own, other):
        return own + swap(other.astype(bf16), 1).astype(f32)

    def reduce_groups(total):
        blocks = total.reshape(groups, 2 * depth, -1)
        return scatter_ring([pick(blocks, group ^ k) for k in range(groups)], 2 * narrow)

    def reduce_side(total):
        total = total.reshape(2, depth, -1)
        kept = pick(total, side)
        received = swap(pick(total, 1 - side).astype(bf16), narrow).astype(f32)
        return place([kept[None], received[None]], side, 0)

    def join(array):
        return array.transpose(1, 2, 0, 3).reshape(depth, array.shape[2], -1)

    grad_down = dot("td,tbf->bdf", grad_rows, activated)
    grad_in = dot("td,ctbf->bdcf", normed_middle, grad_gate_up)
    grad_mlp = jnp.concatenate([grad_in, grad_down[:, :, None]], axis=2).reshape(
        2, model, 3 * hidden
    )
    grad_mlp = reduce_cores(grad_mlp[0], grad_mlp[1])
    grad_middle_low, grad_mlp = lax.optimization_barrier((grad_middle.astype(bf16), grad_mlp))
    grad_attn = gather_rows(grad_middle_low)
    grad_mlp = reduce_groups(grad_mlp)

    branch = dot("tbf,bdf->td", after(activated, grad_attn), down_weight).reshape(2, block, columns, 2 * width)
    total = pick(branch[0] + middle.reshape(2, block, columns, 2 * width)[0], column, 1)
    for k, s in chips:
        if k or s:
            piece = pick(branch[s], column ^ k, 1).astype(bf16)
            total = total + swap(piece, over_chips(k, s)).astype(f32)
    total = total.astype(bf16).reshape(block, 2, width)
    result = place(
        [pick(total, core, 1)[None], swap(pick(total, 1 - core, 1), 1)[None]], core, 0
    )

    grad_context = dot("td,bdm->tbm", grad_attn, out_weight).astype(bf16)
    grad_out_weight = dot("td,tbm->bdm", grad_attn, context.reshape(rows, 2, half))
    grad_context = grad_context.reshape(rows, heads, HEAD_DIM)
    probs_again = jnp.exp(dot("qhe,khe->hqk", queries, keys) * score_scale - log_total)
    probs_low = probs_again.astype(bf16)

    def scatter_groups(array):
        blocks = array.reshape(groups, rows, width)
        return scatter_ring([blocks[k] for k in range(groups)], 2 * narrow)

    grad_values = scatter_groups(dot("hqk,qhe->khe", probs_low, grad_context))
    grad_probs = dot("qhe,khe->hqk", grad_context, values)
    row_delta = jnp.sum(probs_again * grad_probs, axis=-1, keepdims=True)
    grad_scores = (probs_again * (grad_probs - row_delta)).astype(bf16)
    grad_keys = scatter_groups(dot("hqk,qhe->khe", grad_scores, queries) * score_scale)
    grad_queries = dot("hqk,khe->qhe", grad_scores, keys) * score_scale
    grad_projected = jnp.stack(
        [
            rotary_transposed(grad_queries, cosine, sine),
            rotary_transposed(grad_keys.reshape(rows, heads, HEAD_DIM), cosine, sine),
            grad_values.reshape(rows, heads, HEAD_DIM),
        ],
        axis=1,
    ).astype(bf16).reshape(rows, 3, 2, half)
    grad_one_partial = dot("tcbm,bdcm->td", grad_projected, qkv_weight)
    grad_one_partial, grad_mlp = lax.optimization_barrier((grad_one_partial, grad_mlp))
    grad_one = scatter_rows(grad_one_partial)
    grad_mlp = join(reduce_side(grad_mlp).reshape(2, depth, 3, hidden))
    grad_qkv = dot("td,tcbm->bdcm", normed_input, grad_projected)
    grad_attn_weight = jnp.concatenate([grad_qkv, grad_out_weight[:, :, None]], axis=2).reshape(
        2, model, 4 * half
    )
    grad_attn_weight = reduce_groups(reduce_cores(grad_attn_weight[0], grad_attn_weight[1]))
    grad_attn_weight = join(reduce_side(grad_attn_weight).reshape(2, depth, 4, half))
    grad_rows_in = grad_middle + norm_backward(
        grad_one, own_rows(centred_one), own_rows(inverse_one), gains[0]
    )
    by_owner = grad_rows_in.reshape(part, columns, 2, width)

    def send(k, c):
        piece = pick(pick(by_owner, column ^ k, 1), core ^ c, 1)
        return swap(piece, 2 * k + c)

    grad_inputs = place(
        [
            place([send(k, c) for k in range(columns)], column, 0)[None]
            for c in range(2)
        ],
        core,
        0,
    )

    gain_grads = jnp.stack(
        [
            jnp.sum(grad_one_partial * centred_one, axis=0),
            jnp.sum(grad_two_partial * centred_two, axis=0),
        ]
    ).reshape(2, narrow, width)
    gain_total = pick(gain_grads, narrow_at, 1)
    for m in range(1, narrow):
        gain_total = gain_total + swap(pick(gain_grads, narrow_at ^ m, 1), m)
    gain_total = gain_total + swap(gain_total, narrow)
    for mask in ring_masks(groups):
        gain_total = gain_total + swap(gain_total, 2 * narrow * mask)
    return (
        result,
        grad_inputs,
        gain_total[0],
        grad_attn_weight[:, :3],
        grad_attn_weight[:, 3].T,
        gain_total[1],
        grad_mlp[:, :2],
        grad_mlp[:, 2].T,
    )


def solution(mesh):
    in_specs = (
        P(None, "wide", "narrow"),
        P("narrow"),
        P("wide", None, "narrow"),
        P("narrow", "wide"),
        P("narrow"),
        P("wide", None, "narrow"),
        P("narrow", "wide"),
        P(None, "wide", "narrow"),
    )
    out_specs = (
        P(None, "wide", "narrow"),
        P(None, "wide", "narrow"),
        P("narrow"),
        P("wide", None, "narrow"),
        P("narrow", "wide"),
        P("narrow"),
        P("wide", None, "narrow"),
        P("narrow", "wide"),
    )
    step = functools.partial(body, mesh.shape["wide"], mesh.shape["narrow"])
    return jax.shard_map(step, mesh=mesh, in_specs=in_specs, out_specs=out_specs, check_vma=False)
```

```python
import functools
import math

import jax
import jax.numpy as jnp
from jax import lax
from jax.experimental import pallas as pl
from jax.experimental.pallas import tpu as pltpu
from jax.sharding import PartitionSpec as P

HEAD_DIM = 64
eps_norm = 1e-05
rope_base = 160000.0
f32 = jnp.float32
bf16 = jnp.bfloat16


def mm(a, b):
    return lax.dot_general(a, b, (((1,), (0,)), ((), ())), preferred_element_type=f32)


def mm_nt(a, b):
    return lax.dot_general(a, b, (((1,), (1,)), ((), ())), preferred_element_type=f32)


def aligned(index, size):
    return pl.ds(pl.multiple_of(index * size, size), size)


def norm_rows(rows):
    width = rows.shape[-1]
    average = jnp.sum(rows, axis=-1, keepdims=True) / width
    variance = jnp.sum(rows * rows, axis=-1, keepdims=True) / width - average * average
    inverse = lax.rsqrt(variance + eps_norm)
    return (rows - average) * inverse, inverse


def norm_backward(grad_normed, centred, inverse, gain):
    width = grad_normed.shape[-1]
    scaled = grad_normed * gain
    row_total = jnp.sum(scaled, axis=-1, keepdims=True)
    row_along = jnp.sum(scaled * centred, axis=-1, keepdims=True)
    return inverse * (scaled - row_total / width - centred * (row_along / width))


def rope_tables(positions, lanes):
    half_dim = HEAD_DIM // 2
    frequency = rope_base ** (-jnp.arange(half_dim).astype(f32) * 2.0 / HEAD_DIM)
    angles = positions[:, None] * frequency[None, :]
    angles = jnp.concatenate([angles, angles] * (lanes // HEAD_DIM), axis=-1)
    return jnp.cos(angles), jnp.sin(angles)


def rotated(tensor):
    lanes, half_dim = tensor.shape[-1], HEAD_DIM // 2
    lane = lax.broadcasted_iota(jnp.int32, tensor.shape, 1)
    up = pltpu.roll(tensor, half_dim, 1)
    down = pltpu.roll(tensor, lanes - half_dim, 1)
    return jnp.where(lane % HEAD_DIM < half_dim, -down, up)


def call(kernel, outs, at, *arrays, scratch=()):
    return pl.pallas_call(
        kernel,
        out_shape=[jax.ShapeDtypeStruct(shape, dtype) for shape, dtype in outs],
        in_specs=[pl.BlockSpec(memory_space=pltpu.SMEM)]
        + [pl.BlockSpec(memory_space=pltpu.VMEM)] * len(arrays),
        out_specs=[pl.BlockSpec(memory_space=pltpu.VMEM)] * len(outs),
        scratch_shapes=[pltpu.VMEM(shape, dtype) for shape, dtype in scratch],
        compiler_params=pltpu.CompilerParams(vmem_limit_bytes=60 * 1024 * 1024),
        name=kernel.func.__name__,
    )(at, *arrays)


def ring_masks(count):
    masks, unit = [], 1
    while unit < count:
        masks += [unit] + ([3 * unit] if 4 * unit <= count else [])
        unit *= 4
    return masks


def pick(array, index, axis=0):
    return lax.dynamic_index_in_dim(array, index, axis=axis, keepdims=False)


def place(pieces, own, axis):
    count = len(pieces)
    if count == 1:
        return pieces[0]
    if count == 2:
        return jnp.where(
            own == 0,
            jnp.concatenate(pieces, axis=axis),
            jnp.concatenate(pieces[::-1], axis=axis),
        )
    size = pieces[0].shape[axis]
    shape = list(pieces[0].shape)
    shape[axis] = size * count
    whole = jnp.zeros(shape, pieces[0].dtype)
    for relative, piece in enumerate(pieces):
        whole = lax.dynamic_update_slice_in_dim(whole, piece, (own ^ relative) * size, axis)
    return whole


def project(chips, at, *refs):
    shards, refs = refs[: len(chips)], refs[len(chips) :]
    own, other, gains, cosine, sine, rows_ref, grad_ref, normed_ref, query_ref, pair_ref = refs
    block, span = shards[0].shape[1:]
    half = own.shape[1] // 4
    for (k, s), shard in zip(chips, shards):
        lanes = aligned(at[0] ^ k, span)
        rows_ref[s * block : (s + 1) * block, lanes] = shard[0]
        grad_ref[s * block : (s + 1) * block, lanes] = shard[1]
    centred, _ = norm_rows(rows_ref[...].astype(f32))
    normed = (centred * gains[0:1, :]).astype(bf16)
    normed_ref[...] = normed
    queries, keys, values = [], [], []
    for weight in (own, other):
        projected = mm(normed, weight[:, : 3 * half])
        queries.append(projected[:, :half])
        keys.append(projected[:, half : 2 * half])
        values.append(projected[:, 2 * half :])
    query, key = jnp.concatenate(queries, axis=1), jnp.concatenate(keys, axis=1)
    cosine, sine = cosine[...], sine[...]
    query = (query * cosine + rotated(query) * sine).astype(bf16)
    key = (key * cosine + rotated(key) * sine).astype(bf16)
    query_ref[...] = query * jnp.asarray(HEAD_DIM**-0.5, bf16)
    pair_ref[:, : 2 * half] = key
    pair_ref[:, 2 * half :] = jnp.concatenate(values, axis=1).astype(bf16)


def attend(parts, at, query_ref, *refs):
    pieces, (context_ref, pairs_ref, total_ref) = refs[:parts], refs[parts:]
    start = 0
    for piece in pieces:
        pairs_ref[start : start + piece.shape[0], :] = piece[...]
        start += piece.shape[0]
    width = query_ref.shape[1]
    values = pairs_ref[:, width:].T
    contexts = []
    for h in range(width // HEAD_DIM):
        lanes = slice(h * HEAD_DIM, (h + 1) * HEAD_DIM)
        scores = mm_nt(pairs_ref[:, lanes], query_ref[:, lanes])
        peak = jnp.max(scores, axis=0, keepdims=True)
        log_total = peak + jnp.log(jnp.sum(jnp.exp(scores - peak), axis=0, keepdims=True))
        probs = jnp.exp(scores - log_total).astype(bf16)
        contexts.append(mm(values[lanes], probs))
        total_ref[h : h + 1, :] = log_total
    context_ref[...] = jnp.concatenate(contexts, axis=0).T.astype(bf16)


def feed(chips, at, *refs):
    count = len(chips)
    contexts, refs = refs[:count], refs[count:]
    (out_own, out_other, rows_ref, grad_ref, own, other, gains), refs = refs[:7], refs[7:]
    (middle_ref, middle_rows_ref, normed_ref, unit_ref, active_ref, gain_ref, total_ref), refs = refs[:7], refs[7:]
    pieces, scratch = refs[:-1], refs[-1]
    hidden = active_ref.shape[2]
    block, span = middle_ref.shape
    part = total_ref.shape[0]
    middle = rows_ref[...].astype(f32)
    for p, (k, s) in enumerate(chips):
        context = contexts[p][...]
        if s:
            context = jnp.concatenate([context[block:], context[:block]], axis=0)
        middle = middle + mm_nt(context, jnp.concatenate([out_own[p], out_other[p]], axis=1))
    scratch[...] = middle
    middle_ref[...] = scratch[:block, aligned(at[0], span)]
    middle_rows_ref[...] = scratch[aligned(at[0], part), :]
    centred, _ = norm_rows(middle)
    normed = (centred * gains[1:2, :]).astype(bf16)
    normed_ref[...] = normed
    partial = jnp.zeros_like(middle)
    for b, weight in enumerate((own, other)):
        gate_up = mm(normed, weight[:, : 2 * hidden])
        gate, lift = gate_up[:, :hidden], gate_up[:, hidden:]
        share = 0.5 + 0.5 * lax.erf(gate * math.sqrt(0.5))
        bent = gate * share
        active_ref[b] = (bent * lift).astype(bf16)
        slope = share + gate * jnp.exp(-0.5 * gate * gate) * (1.0 / math.sqrt(2.0 * math.pi))
        back = mm(grad_ref[...], weight[:, 2 * hidden :])
        unit = jnp.concatenate([back * lift * slope, back * bent], axis=1).astype(bf16)
        unit_ref[b] = unit
        partial = partial + mm_nt(unit, weight[:, : 2 * hidden])
    gain_ref[...] = jnp.sum(partial * centred, axis=0, keepdims=True)
    scratch[...] = partial
    cut_rows(chips, at, scratch, total_ref, pieces)


def cut_rows(chips, at, scratch, total_ref, pieces):
    part = total_ref.shape[0]
    columns = scratch.shape[0] // (2 * part)
    for p, (k, s) in enumerate(chips):
        rows = scratch[aligned(s * columns + (at[0] ^ k), part), :]
        if p:
            pieces[p - 1][...] = rows.astype(bf16)
        else:
            total_ref[...] = rows


def turn(at, total_ref, *refs):
    pieces, (middle_ref, grad_ref, gains, grad_middle_ref, low_ref) = refs[:-5], refs[-5:]
    part = total_ref.shape[0]
    total = total_ref[...]
    for piece in pieces:
        total = total + piece[...].astype(f32)
    centred, inverse = norm_rows(middle_ref[...])
    grad = grad_ref[aligned(at[0], part), :].astype(f32)
    grad = grad + norm_backward(total, centred, inverse, gains[1:2, :])
    grad_middle_ref[...] = grad
    low_ref[...] = grad.astype(bf16)


def settle(chips, at, *refs):
    (normed_ref, unit_ref, active_ref, grad_ref, own, other, middle_ref), refs = refs[:7], refs[7:]
    (own_ref, other_ref, total_ref), refs = refs[:3], refs[3:]
    pieces, scratch = refs[:-1], refs[-1]
    hidden = active_ref.shape[2]
    block, span = total_ref.shape
    normed, grad = normed_ref[...].T, grad_ref[...].T
    for b, out in enumerate((other_ref, own_ref)):
        out[:, : 2 * hidden] = mm(normed, unit_ref[1 - b]).astype(bf16)
        out[:, 2 * hidden :] = mm(grad, active_ref[1 - b]).astype(bf16)
    scratch[...] = mm_nt(active_ref[0], own[:, 2 * hidden :]) + mm_nt(active_ref[1], other[:, 2 * hidden :])
    for p, (k, s) in enumerate(chips):
        piece = scratch[s * block : (s + 1) * block, aligned(at[0] ^ k, span)]
        if p:
            pieces[p - 1][...] = piece.astype(bf16)
        else:
            total_ref[...] = piece + middle_ref[...]


def reflect(chips, at, *refs):
    pieces, refs = refs[: len(chips)], refs[len(chips) :]
    own, other, query_ref, pairs_ref, total_ref, grad_attn_ref, grad_query_ref, grad_pairs_ref = refs
    part = pieces[0].shape[0]
    rows, width = query_ref.shape
    columns = rows // (2 * part)
    half = width // 2
    for (k, s), piece in zip(chips, pieces):
        grad_attn_ref[aligned(s * columns + (at[0] ^ k), part), :] = piece[...]
    grad_attn = grad_attn_ref[...]
    grad_context = jnp.concatenate(
        [mm(grad_attn, own[:, 3 * half :]), mm(grad_attn, other[:, 3 * half :])], axis=1
    ).astype(bf16)
    keys = pairs_ref[:, :width].T
    grad_queries = []
    for h in range(width // HEAD_DIM):
        lanes = slice(h * HEAD_DIM, (h + 1) * HEAD_DIM)
        query = query_ref[:, lanes]
        grad = grad_context[:, lanes]
        probs = jnp.exp(mm_nt(pairs_ref[:, lanes], query) - total_ref[h : h + 1, :])
        value_lanes = slice(width + h * HEAD_DIM, width + (h + 1) * HEAD_DIM)
        grad_probs = mm_nt(pairs_ref[:, value_lanes], grad)
        delta = jnp.sum(probs * grad_probs, axis=0, keepdims=True)
        grad_scores = (probs * (grad_probs - delta)).astype(bf16)
        grad_pairs_ref[:, lanes] = mm(grad_scores, query)
        grad_pairs_ref[:, value_lanes] = mm(probs.astype(bf16), grad)
        grad_queries.append(mm(keys[lanes], grad_scores))
    grad_query_ref[...] = jnp.concatenate(grad_queries, axis=0).T * HEAD_DIM**-0.5


def unwind(chips, at, *refs):
    (grad_query_ref, grad_pairs_ref, cosine, sine, rows_ref, own, other), refs = refs[:7], refs[7:]
    (grad_projected_ref, gain_ref, total_ref), refs = refs[:3], refs[3:]
    pieces, scratch = refs[:-1], refs[-1]
    width = grad_query_ref.shape[1]
    half = width // 2
    cosine, sine = cosine[...], sine[...]
    grad_query, grad_key = grad_query_ref[...], grad_pairs_ref[:, :width]
    grad_query = (grad_query * cosine - rotated(grad_query * sine)).astype(bf16)
    grad_key = (grad_key * cosine - rotated(grad_key * sine)).astype(bf16)
    grad_value = grad_pairs_ref[:, width:].astype(bf16)
    partial = 0.0
    for b, weight in enumerate((own, other)):
        lanes = slice(b * half, (b + 1) * half)
        grad = jnp.concatenate([grad_query[:, lanes], grad_key[:, lanes], grad_value[:, lanes]], axis=1)
        grad_projected_ref[b] = grad
        partial = partial + mm_nt(grad, weight[:, : 3 * half])
    centred, _ = norm_rows(rows_ref[...].astype(f32))
    gain_ref[...] = jnp.sum(partial * centred, axis=0, keepdims=True)
    scratch[...] = partial
    cut_rows(chips, at, scratch, total_ref, pieces)


def repay(at, normed_ref, grad_projected_ref, grad_attn_ref, context_ref, own_ref, other_ref):
    half = context_ref.shape[1] // 2
    normed, grad_attn = normed_ref[...].T, grad_attn_ref[...].T
    for b, out in ((1, other_ref), (0, own_ref)):
        out[:, : 3 * half] = mm(normed, grad_projected_ref[b]).astype(bf16)
        out[:, 3 * half :] = mm(grad_attn, context_ref[:, b * half : (b + 1) * half]).astype(bf16)


def finish(narrow, at, total_ref, *refs):
    pieces, (rows_ref, grad_middle_ref, gains), outs, scratch = refs[: -narrow - 4], refs[-narrow - 4 : -narrow - 1], refs[-narrow - 1 : -1], refs[-1]
    part = total_ref.shape[0]
    width = outs[0].shape[1]
    total = total_ref[...]
    for piece in pieces:
        total = total + piece[...].astype(f32)
    centred, inverse = norm_rows(rows_ref[aligned(at[0], part), :].astype(f32))
    scratch[...] = grad_middle_ref[...] + norm_backward(total, centred, inverse, gains[0:1, :])
    for m, out in enumerate(outs):
        out[...] = scratch[:, aligned(at[1] ^ m, width)]


def body(
    wide,
    narrow,
    inputs,
    attn_gain,
    query_key_value_weight,
    attention_out_weight,
    mlp_gain,
    feedforward_in_weight,
    feedforward_out_weight,
    grad_out,
):
    groups, columns = wide // 2, narrow // 2
    _, block, width = inputs.shape
    model = width * narrow
    depth = query_key_value_weight.shape[0]
    hidden = feedforward_out_weight.shape[0] // 2
    half, span = width // 2, 2 * width
    part = block // columns
    rows = 2 * block
    length = groups * rows
    wide_at, narrow_at = lax.axis_index("wide"), lax.axis_index("narrow")
    group, side = wide_at // 2, wide_at % 2
    column, core = narrow_at // 2, narrow_at % 2
    at = jnp.stack([column, narrow_at]).astype(jnp.int32)
    chips = [(k, s) for s in range(2) for k in range(columns)]

    def swap(array, mask):
        if mask == 0:
            return array
        return lax.ppermute(
            array, ("wide", "narrow"), [(i, i ^ mask) for i in range(wide * narrow)]
        )

    def over_chips(column_rel, side_rel):
        return 2 * column_rel + narrow * side_rel

    def over_groups(group_rel):
        return 2 * narrow * group_rel

    def after(array, *others):
        return lax.optimization_barrier((array, *others))[0]

    def gather_ring(array, unit, count, split=False):
        if count == 1:
            return [array]
        if count == 2:
            return [array, swap(array, unit)]
        cut = array.shape[0] // 2
        near, far = swap(array, unit), swap(array, 3 * unit)
        across = [swap(far[:cut], unit), swap(near[cut:], 3 * unit)]
        if count == 4 and split:
            return [array, near, *across, far]
        across = jnp.concatenate(across, axis=0)
        quad = [array, near, across, far]
        if count == 4:
            return quad
        return [q for quads in gather_ring(jnp.stack(quad, 1), 4 * unit, count // 4) for q in jnp.moveaxis(quads, 1, 0)]

    def scatter_ring(pieces, unit):
        count = len(pieces)
        if count == 1:
            return pieces[0]
        if count == 2:
            return pieces[0] + swap(pieces[1].astype(bf16), unit).astype(f32)
        if count > 4:
            stacked = [jnp.stack(pieces[k : k + 4], 1) for k in range(0, count, 4)]
            pieces = list(jnp.moveaxis(scatter_ring(stacked, 4 * unit), 1, 0))
        own, near, across, far = pieces
        cut = own.shape[0] // 2
        across = across.astype(bf16)
        for_far = swap(across[:cut], unit).astype(f32)
        for_near = swap(across[cut:], 3 * unit).astype(f32)
        near = jnp.concatenate([near[:cut], near[cut:] + for_near], axis=0).astype(bf16)
        far = jnp.concatenate([far[:cut] + for_far, far[cut:]], axis=0).astype(bf16)
        return own + swap(near, unit).astype(f32) + swap(far, 3 * unit).astype(f32)

    def fetch_side(bundle):
        received = swap(pick(bundle, 1 - side), narrow)
        return place([pick(bundle, side), received], side, 0)

    def fetch_groups(pair):
        return place(gather_ring(pair, 2 * narrow, groups), group, 0)

    def halves(array):
        return array.reshape(depth, -1, 2, array.shape[-1] // 2).transpose(2, 0, 1, 3)

    def from_chips(array):
        return [swap(array, over_chips(k, s)) for k, s in chips]

    def to_chips(pieces):
        return [swap(piece, over_chips(k, s)) for (k, s), piece in zip(chips[1:], pieces)]

    def reduce_cores(own, other):
        return own.astype(f32) + swap(other, 1).astype(f32)

    def reduce_groups(total):
        blocks = total.reshape(groups, 2 * depth, -1)
        return scatter_ring([pick(blocks, group ^ k) for k in range(groups)], 2 * narrow)

    def reduce_side(total):
        total = total.reshape(2, depth, -1)
        kept = pick(total, side)
        received = swap(pick(total, 1 - side).astype(bf16), narrow).astype(f32)
        return place([kept[None], received[None]], side, 0)

    def join(array):
        return array.transpose(1, 2, 0, 3).reshape(depth, array.shape[2], -1)

    attn_bundle = jnp.concatenate(
        [halves(query_key_value_weight), halves(attention_out_weight.T[:, None])], axis=2
    ).reshape(2, depth, 4 * half)
    mlp_bundle = jnp.concatenate(
        [halves(feedforward_in_weight), halves(feedforward_out_weight.T[:, None])], axis=2
    ).reshape(2, depth, 3 * hidden)

    both = jnp.stack([inputs, grad_out])
    received = swap(pick(both, 1 - core, 1), 1)
    features = place([pick(both, core, 1), received], core, 2)
    attn_pair = fetch_side(attn_bundle)
    shards = from_chips(after(features, attn_pair))
    attn_own = fetch_groups(attn_pair)
    mlp_pair = fetch_side(after(mlp_bundle, attn_pair))
    attn_other = swap(attn_own, 1)
    gains = jnp.stack([attn_gain, mlp_gain])
    gains = place([gains, swap(gains, 1)], core, 1)
    gains = place([swap(gains, 2 * k) for k in range(columns)], column, 1)
    token = (jnp.arange(rows) // block) ^ side
    positions = ((group * 2 + token) * block + jnp.arange(rows) % block).astype(f32)
    cosine, sine = rope_tables(positions, width)

    rows_in, grad_rows, normed_one, query, pair = call(
        functools.partial(project, chips),
        [((rows, model), bf16)] * 3 + [((rows, width), bf16), ((rows, span), bf16)],
        at, *shards, attn_own, attn_other, gains, cosine, sine,
    )
    pairs = gather_ring(pair, 2 * narrow, groups, split=True)
    out_own = from_chips(after(attn_own[:, 3 * half :], pair))
    out_own = jnp.stack(out_own)
    out_other = swap(out_own, 1)
    context, pairs, total = call(
        functools.partial(attend, len(pairs)),
        [((rows, width), bf16), ((length, span), bf16), ((8, rows), f32)],
        at, query, *pairs,
    )
    contexts = from_chips(context)
    mlp_own = fetch_groups(mlp_pair)
    mlp_other = swap(mlp_own, 1)
    middle, middle_rows, normed_two, unit, active, mlp_gain_part, grad_two, *sends = call(
        functools.partial(feed, chips),
        [((block, span), f32), ((part, model), f32), ((rows, model), bf16), ((2, rows, 2 * hidden), bf16),
         ((2, rows, hidden), bf16), ((1, model), f32), ((part, model), f32)] + [((part, model), bf16)] * (len(chips) - 1),
        at, *contexts, out_own, out_other, rows_in, grad_rows, mlp_own, mlp_other, gains,
        scratch=[((rows, model), f32)],
    )
    received = to_chips(sends)
    grad_mlp_own, grad_mlp_other, branch, *branch_sends = call(
        functools.partial(settle, chips),
        [((model, 3 * hidden), bf16)] * 2 + [((block, span), f32)] + [((block, span), bf16)] * (len(chips) - 1),
        at, normed_two, unit, active, grad_rows, mlp_own, mlp_other, middle,
        scratch=[((rows, model), f32)],
    )
    grad_middle, grad_low = call(
        functools.partial(turn), [((part, model), f32), ((part, model), bf16)],
        at, grad_two, *received, middle_rows, grad_rows, gains,
    )
    grad_pieces = from_chips(grad_low)
    grad_mlp = reduce_cores(grad_mlp_own, grad_mlp_other)
    grad_attn, grad_query, grad_pairs = call(
        functools.partial(reflect, chips),
        [((rows, model), bf16), ((rows, width), f32), ((length, span), f32)],
        at, *grad_pieces, attn_own, attn_other, query, pairs, total,
    )
    grad_mlp = reduce_groups(grad_mlp)
    grad_pairs = scatter_ring(list(grad_pairs.reshape(groups, rows, span)), 2 * narrow)

    for piece in to_chips(branch_sends):
        branch = branch + piece.astype(f32)
    branch = branch.astype(bf16).reshape(block, 2, width)
    result = place([pick(branch, core, 1)[None], swap(pick(branch, 1 - core, 1), 1)[None]], core, 0)

    grad_pairs, grad_mlp = lax.optimization_barrier((grad_pairs, grad_mlp))
    grad_projected, attn_gain_part, grad_one, *sends = call(
        functools.partial(unwind, chips),
        [((2, rows, 3 * half), bf16), ((1, model), f32), ((part, model), f32)] + [((part, model), bf16)] * (len(chips) - 1),
        at, grad_query, grad_pairs, cosine, sine, rows_in, attn_own, attn_other,
        scratch=[((rows, model), f32)],
    )
    received = to_chips(sends)
    grad_attn_own, grad_attn_other = call(
        functools.partial(repay), [((model, 4 * half), bf16)] * 2,
        at, normed_one, grad_projected, grad_attn, context,
    )
    grad_mlp = join(reduce_side(grad_mlp).reshape(2, depth, 3, hidden))
    grad_attn_weight = reduce_groups(reduce_cores(grad_attn_own, grad_attn_other))
    grad_attn_weight = join(reduce_side(grad_attn_weight).reshape(2, depth, 4, half))
    sends = call(
        functools.partial(finish, narrow), [((part, width), f32)] * narrow,
        at, grad_one, *received, rows_in, grad_middle, gains,
        scratch=[((part, model), f32)],
    )
    grad_inputs = place(
        [place([swap(sends[2 * k + c], 2 * k + c) for k in range(columns)], column, 0)[None] for c in range(2)],
        core, 0,
    )
    gain_grads = jnp.concatenate([attn_gain_part, mlp_gain_part], axis=0).reshape(2, narrow, width)
    gain_total = pick(gain_grads, narrow_at, 1)
    for m in range(1, narrow):
        gain_total = gain_total + swap(pick(gain_grads, narrow_at ^ m, 1), m)
    gain_total = gain_total + swap(gain_total, narrow)
    for mask in ring_masks(groups):
        gain_total = gain_total + swap(gain_total, 2 * narrow * mask)
    return (
        result,
        grad_inputs,
        gain_total[0],
        grad_attn_weight[:, :3],
        grad_attn_weight[:, 3].T,
        gain_total[1],
        grad_mlp[:, :2],
        grad_mlp[:, 2].T,
    )


def solution(mesh):
    in_specs = (
        P(None, "wide", "narrow"),
        P("narrow"),
        P("wide", None, "narrow"),
        P("narrow", "wide"),
        P("narrow"),
        P("wide", None, "narrow"),
        P("narrow", "wide"),
        P(None, "wide", "narrow"),
    )
    out_specs = (
        P(None, "wide", "narrow"),
        P(None, "wide", "narrow"),
        P("narrow"),
        P("wide", None, "narrow"),
        P("narrow", "wide"),
        P("narrow"),
        P("wide", None, "narrow"),
        P("narrow", "wide"),
    )
    step = functools.partial(body, mesh.shape["wide"], mesh.shape["narrow"])
    return jax.shard_map(step, mesh=mesh, in_specs=in_specs, out_specs=out_specs, check_vma=False)
```

```python
import functools
import math

import jax
import jax.numpy as jnp
from jax import lax
from jax.experimental import pallas as pl
from jax.experimental.pallas import tpu as pltpu
from jax.sharding import PartitionSpec as P

HEAD_DIM = 64
eps_norm = 1e-05
rope_base = 160000.0
f32 = jnp.float32
bf16 = jnp.bfloat16


def mm(a, b):
    return lax.dot_general(a, b, (((1,), (0,)), ((), ())), preferred_element_type=f32)


def mm_nt(a, b):
    return lax.dot_general(a, b, (((1,), (1,)), ((), ())), preferred_element_type=f32)


def aligned(index, size):
    return pl.ds(pl.multiple_of(index * size, size), size)


def norm_rows(rows):
    width = rows.shape[-1]
    average = jnp.sum(rows, axis=-1, keepdims=True) / width
    variance = jnp.sum(rows * rows, axis=-1, keepdims=True) / width - average * average
    inverse = lax.rsqrt(variance + eps_norm)
    return (rows - average) * inverse, inverse


def norm_backward(grad_normed, centred, inverse, gain):
    width = grad_normed.shape[-1]
    scaled = grad_normed * gain
    row_total = jnp.sum(scaled, axis=-1, keepdims=True)
    row_along = jnp.sum(scaled * centred, axis=-1, keepdims=True)
    return inverse * (scaled - row_total / width - centred * (row_along / width))


def rope_tables(positions, lanes):
    half_dim = HEAD_DIM // 2
    frequency = rope_base ** (-jnp.arange(half_dim).astype(f32) * 2.0 / HEAD_DIM)
    angles = positions[:, None] * frequency[None, :]
    angles = jnp.concatenate([angles, angles] * (lanes // HEAD_DIM), axis=-1)
    return jnp.cos(angles), jnp.sin(angles)


def rotated(tensor):
    lanes, half_dim = tensor.shape[-1], HEAD_DIM // 2
    lane = lax.broadcasted_iota(jnp.int32, tensor.shape, 1)
    up = pltpu.roll(tensor, half_dim, 1)
    down = pltpu.roll(tensor, lanes - half_dim, 1)
    return jnp.where(lane % HEAD_DIM < half_dim, -down, up)


def call(kernel, outs, at, *arrays, scratch=()):
    return pl.pallas_call(
        kernel,
        out_shape=[jax.ShapeDtypeStruct(shape, dtype) for shape, dtype in outs],
        in_specs=[pl.BlockSpec(memory_space=pltpu.SMEM)]
        + [pl.BlockSpec(memory_space=pltpu.VMEM)] * len(arrays),
        out_specs=[pl.BlockSpec(memory_space=pltpu.VMEM)] * len(outs),
        scratch_shapes=[pltpu.VMEM(shape, dtype) for shape, dtype in scratch],
        compiler_params=pltpu.CompilerParams(vmem_limit_bytes=60 * 1024 * 1024),
        name=kernel.func.__name__,
    )(at, *arrays)


def ring_masks(count):
    masks, unit = [], 1
    while unit < count:
        masks += [unit] + ([3 * unit] if 4 * unit <= count else [])
        unit *= 4
    return masks


def pick(array, index, axis=0):
    return lax.dynamic_index_in_dim(array, index, axis=axis, keepdims=False)


def place(pieces, own, axis):
    count = len(pieces)
    if count == 1:
        return pieces[0]
    if count == 2:
        return jnp.where(
            own == 0,
            jnp.concatenate(pieces, axis=axis),
            jnp.concatenate(pieces[::-1], axis=axis),
        )
    size = pieces[0].shape[axis]
    shape = list(pieces[0].shape)
    shape[axis] = size * count
    whole = jnp.zeros(shape, pieces[0].dtype)
    for relative, piece in enumerate(pieces):
        whole = lax.dynamic_update_slice_in_dim(whole, piece, (own ^ relative) * size, axis)
    return whole


def project(chips, at, *refs):
    shards, refs = refs[: len(chips)], refs[len(chips) :]
    own, other, gains, cosine, sine, rows_ref, grad_ref, normed_ref, query_ref, pair_ref = refs
    block, span = shards[0].shape[1:]
    half = own.shape[1] // 4
    for (k, s), shard in zip(chips, shards):
        lanes = aligned(at[0] ^ k, span)
        rows_ref[s * block : (s + 1) * block, lanes] = shard[0]
        grad_ref[s * block : (s + 1) * block, lanes] = shard[1]
    centred, _ = norm_rows(rows_ref[...].astype(f32))
    normed = (centred * gains[0:1, :]).astype(bf16)
    normed_ref[...] = normed
    queries, keys, values = [], [], []
    for weight in (own, other):
        projected = mm(normed, weight[:, : 3 * half])
        queries.append(projected[:, :half])
        keys.append(projected[:, half : 2 * half])
        values.append(projected[:, 2 * half :])
    query, key = jnp.concatenate(queries, axis=1), jnp.concatenate(keys, axis=1)
    cosine, sine = cosine[...], sine[...]
    query = (query * cosine + rotated(query) * sine).astype(bf16)
    key = (key * cosine + rotated(key) * sine).astype(bf16)
    query_ref[...] = query * jnp.asarray(HEAD_DIM**-0.5, bf16)
    pair_ref[:, : 2 * half] = key
    pair_ref[:, 2 * half :] = jnp.concatenate(values, axis=1).astype(bf16)


def attend(parts, at, query_ref, *refs):
    pieces, (context_ref, pairs_ref, total_ref) = refs[:parts], refs[parts:]
    start = 0
    for piece in pieces:
        pairs_ref[start : start + piece.shape[0], :] = piece[...]
        start += piece.shape[0]
    width = query_ref.shape[1]
    values = pairs_ref[:, width:].T
    contexts = []
    for h in range(width // HEAD_DIM):
        lanes = slice(h * HEAD_DIM, (h + 1) * HEAD_DIM)
        scores = mm_nt(pairs_ref[:, lanes], query_ref[:, lanes])
        peak = jnp.max(scores, axis=0, keepdims=True)
        log_total = peak + jnp.log(jnp.sum(jnp.exp(scores - peak), axis=0, keepdims=True))
        probs = jnp.exp(scores - log_total).astype(bf16)
        contexts.append(mm(values[lanes], probs))
        total_ref[h : h + 1, :] = log_total
    context_ref[...] = jnp.concatenate(contexts, axis=0).T.astype(bf16)


def feed(chips, at, *refs):
    count = len(chips)
    contexts, refs = refs[:count], refs[count:]
    (out_own, out_other, rows_ref, grad_ref, own, other, gains), refs = refs[:7], refs[7:]
    (middle_ref, middle_rows_ref, normed_ref, unit_ref, active_ref, gain_ref, total_ref), refs = refs[:7], refs[7:]
    pieces, scratch = refs[:-1], refs[-1]
    hidden = active_ref.shape[2]
    block, span = middle_ref.shape
    part = total_ref.shape[0]
    middle = rows_ref[...].astype(f32)
    for p, (k, s) in enumerate(chips):
        context = contexts[p][...]
        if s:
            context = jnp.concatenate([context[block:], context[:block]], axis=0)
        middle = middle + mm_nt(context, jnp.concatenate([out_own[p], out_other[p]], axis=1))
    scratch[...] = middle
    middle_ref[...] = scratch[:block, aligned(at[0], span)]
    middle_rows_ref[...] = scratch[aligned(at[0], part), :]
    centred, _ = norm_rows(middle)
    normed = (centred * gains[1:2, :]).astype(bf16)
    normed_ref[...] = normed
    partial = jnp.zeros_like(middle)
    for b, weight in enumerate((own, other)):
        gate_up = mm(normed, weight[:, : 2 * hidden])
        gate, lift = gate_up[:, :hidden], gate_up[:, hidden:]
        share = 0.5 + 0.5 * lax.erf(gate * math.sqrt(0.5))
        bent = gate * share
        active_ref[b] = (bent * lift).astype(bf16)
        slope = share + gate * jnp.exp(-0.5 * gate * gate) * (1.0 / math.sqrt(2.0 * math.pi))
        back = mm(grad_ref[...], weight[:, 2 * hidden : 3 * hidden])
        unit = jnp.concatenate([back * lift * slope, back * bent], axis=1).astype(bf16)
        unit_ref[b] = unit
        partial = partial + mm_nt(unit, weight[:, : 2 * hidden])
    gain_ref[...] = jnp.sum(partial * centred, axis=0, keepdims=True)
    scratch[...] = partial
    cut_rows(chips, at, scratch, total_ref, pieces)


def cut_rows(chips, at, scratch, total_ref, pieces):
    part = total_ref.shape[0]
    columns = scratch.shape[0] // (2 * part)
    for p, (k, s) in enumerate(chips):
        rows = scratch[aligned(s * columns + (at[0] ^ k), part), :]
        if p:
            pieces[p - 1][...] = rows.astype(bf16)
        else:
            total_ref[...] = rows


def turn(at, total_ref, *refs):
    pieces, (middle_ref, grad_ref, gains, grad_middle_ref, low_ref) = refs[:-5], refs[-5:]
    part = total_ref.shape[0]
    total = total_ref[...]
    for piece in pieces:
        total = total + piece[...].astype(f32)
    centred, inverse = norm_rows(middle_ref[...])
    grad = grad_ref[aligned(at[0], part), :].astype(f32)
    grad = grad + norm_backward(total, centred, inverse, gains[1:2, :])
    grad_middle_ref[...] = grad
    low_ref[...] = grad.astype(bf16)


def settle(chips, at, *refs):
    (normed_ref, unit_ref, active_ref, grad_ref, own, other, middle_ref), refs = refs[:7], refs[7:]
    (own_ref, other_ref, total_ref), refs = refs[:3], refs[3:]
    pieces, scratch = refs[:-1], refs[-1]
    hidden = active_ref.shape[2]
    block, span = total_ref.shape
    normed, grad = normed_ref[...].T, grad_ref[...].T
    for b, out in enumerate((other_ref, own_ref)):
        out[:, : 2 * hidden] = mm(normed, unit_ref[1 - b]).astype(bf16)
        out[:, 2 * hidden : 3 * hidden] = mm(grad, active_ref[1 - b]).astype(bf16)
        if out.shape[1] > 3 * hidden:
            out[:, 3 * hidden :] = jnp.zeros((out.shape[0], out.shape[1] - 3 * hidden), bf16)
    scratch[...] = mm_nt(active_ref[0], own[:, 2 * hidden : 3 * hidden]) + mm_nt(active_ref[1], other[:, 2 * hidden : 3 * hidden])
    for p, (k, s) in enumerate(chips):
        piece = scratch[s * block : (s + 1) * block, aligned(at[0] ^ k, span)]
        if p:
            pieces[p - 1][...] = piece.astype(bf16)
        else:
            total_ref[...] = piece + middle_ref[...]


def reflect(chips, at, *refs):
    pieces, refs = refs[: len(chips)], refs[len(chips) :]
    own, other, query_ref, pairs_ref, total_ref, grad_attn_ref, grad_query_ref, grad_pairs_ref = refs
    part = pieces[0].shape[0]
    rows, width = query_ref.shape
    columns = rows // (2 * part)
    half = width // 2
    for (k, s), piece in zip(chips, pieces):
        grad_attn_ref[aligned(s * columns + (at[0] ^ k), part), :] = piece[...]
    grad_attn = grad_attn_ref[...]
    grad_context = jnp.concatenate(
        [mm(grad_attn, own[:, 3 * half :]), mm(grad_attn, other[:, 3 * half :])], axis=1
    ).astype(bf16)
    keys = pairs_ref[:, :width].T
    grad_queries = []
    for h in range(width // HEAD_DIM):
        lanes = slice(h * HEAD_DIM, (h + 1) * HEAD_DIM)
        query = query_ref[:, lanes]
        grad = grad_context[:, lanes]
        probs = jnp.exp(mm_nt(pairs_ref[:, lanes], query) - total_ref[h : h + 1, :])
        value_lanes = slice(width + h * HEAD_DIM, width + (h + 1) * HEAD_DIM)
        grad_probs = mm_nt(pairs_ref[:, value_lanes], grad)
        delta = jnp.sum(probs * grad_probs, axis=0, keepdims=True)
        grad_scores = (probs * (grad_probs - delta)).astype(bf16)
        grad_pairs_ref[:, lanes] = mm(grad_scores, query)
        grad_pairs_ref[:, value_lanes] = mm(probs.astype(bf16), grad)
        grad_queries.append(mm(keys[lanes], grad_scores))
    grad_query_ref[...] = jnp.concatenate(grad_queries, axis=0).T * HEAD_DIM**-0.5


def unwind(chips, at, *refs):
    (grad_query_ref, grad_pairs_ref, cosine, sine, rows_ref, own, other), refs = refs[:7], refs[7:]
    (grad_projected_ref, gain_ref, total_ref), refs = refs[:3], refs[3:]
    pieces, scratch = refs[:-1], refs[-1]
    width = grad_query_ref.shape[1]
    half = width // 2
    cosine, sine = cosine[...], sine[...]
    grad_query, grad_key = grad_query_ref[...], grad_pairs_ref[:, :width]
    grad_query = (grad_query * cosine - rotated(grad_query * sine)).astype(bf16)
    grad_key = (grad_key * cosine - rotated(grad_key * sine)).astype(bf16)
    grad_value = grad_pairs_ref[:, width:].astype(bf16)
    partial = 0.0
    for b, weight in enumerate((own, other)):
        lanes = slice(b * half, (b + 1) * half)
        grad = jnp.concatenate([grad_query[:, lanes], grad_key[:, lanes], grad_value[:, lanes]], axis=1)
        grad_projected_ref[b] = grad
        partial = partial + mm_nt(grad, weight[:, : 3 * half])
    centred, _ = norm_rows(rows_ref[...].astype(f32))
    gain_ref[...] = jnp.sum(partial * centred, axis=0, keepdims=True)
    scratch[...] = partial
    cut_rows(chips, at, scratch, total_ref, pieces)


def repay(at, normed_ref, grad_projected_ref, grad_attn_ref, context_ref, own_ref, other_ref):
    half = context_ref.shape[1] // 2
    normed, grad_attn = normed_ref[...].T, grad_attn_ref[...].T
    for b, out in ((1, other_ref), (0, own_ref)):
        out[:, : 3 * half] = mm(normed, grad_projected_ref[b]).astype(bf16)
        out[:, 3 * half :] = mm(grad_attn, context_ref[:, b * half : (b + 1) * half]).astype(bf16)


def finish(narrow, at, total_ref, *refs):
    pieces, (rows_ref, grad_middle_ref, gains), outs, scratch = refs[: -narrow - 4], refs[-narrow - 4 : -narrow - 1], refs[-narrow - 1 : -1], refs[-1]
    part = total_ref.shape[0]
    width = outs[0].shape[1]
    total = total_ref[...]
    for piece in pieces:
        total = total + piece[...].astype(f32)
    centred, inverse = norm_rows(rows_ref[aligned(at[0], part), :].astype(f32))
    scratch[...] = grad_middle_ref[...] + norm_backward(total, centred, inverse, gains[0:1, :])
    for m, out in enumerate(outs):
        out[...] = scratch[:, aligned(at[1] ^ m, width)]


def body(
    wide,
    narrow,
    inputs,
    attn_gain,
    query_key_value_weight,
    attention_out_weight,
    mlp_gain,
    feedforward_in_weight,
    feedforward_out_weight,
    grad_out,
):
    groups, columns = wide // 2, narrow // 2
    _, block, width = inputs.shape
    model = width * narrow
    depth = query_key_value_weight.shape[0]
    hidden = feedforward_out_weight.shape[0] // 2
    half, span = width // 2, 2 * width
    part = block // columns
    rows = 2 * block
    length = groups * rows
    wide_at, narrow_at = lax.axis_index("wide"), lax.axis_index("narrow")
    group, side = wide_at // 2, wide_at % 2
    column, core = narrow_at // 2, narrow_at % 2
    at = jnp.stack([column, narrow_at]).astype(jnp.int32)
    chips = [(k, s) for s in range(2) for k in range(columns)]

    def swap(array, mask):
        if mask == 0:
            return array
        return lax.ppermute(
            array, ("wide", "narrow"), [(i, i ^ mask) for i in range(wide * narrow)]
        )

    def over_chips(column_rel, side_rel):
        return 2 * column_rel + narrow * side_rel

    def over_groups(group_rel):
        return 2 * narrow * group_rel

    def after(array, *others):
        return lax.optimization_barrier((array, *others))[0]

    def swap_ways(array, even, odd):
        pairs = [(i, i ^ (odd if i % 2 else even)) for i in range(wide * narrow)]
        return lax.ppermute(array, ("wide", "narrow"), pairs)

    def ring_order(count):
        if count < 4:
            return list(range(count))
        quad = [0, 1 + 2 * core, 3 - 2 * core, 2]
        return [low + 4 * high for high in ring_order(count // 4) for low in quad]

    def ring_first(array, unit):
        return swap_ways(array, unit, 3 * unit), swap_ways(array, 3 * unit, unit)

    def ring_last(second, unit):
        return swap_ways(second, unit, 3 * unit)

    def gather_ring(array, unit, count):
        if count < 4:
            return [swap(array, unit * k) for k in range(count)]
        first, second = ring_first(array, unit)
        quad = [array, first, second, ring_last(second, unit)]
        if count == 4:
            return quad
        return [q for quads in gather_ring(jnp.stack(quad), 4 * unit, count // 4) for q in quads]

    def scatter_first(pieces, unit):
        count = len(pieces)
        if count < 4:
            return pieces, None
        if count > 4:
            stacked = [jnp.stack(pieces[k : k + 4]) for k in range(0, count, 4)]
            pieces = list(scatter_ring(stacked, 4 * unit))
        own, first, second, across = pieces
        passing = swap_ways(across.astype(bf16), unit, 3 * unit)
        arrived = swap_ways(first.astype(bf16), unit, 3 * unit)
        return own, (second, passing, arrived)

    def scatter_last(own, state, unit):
        if state is None:
            total = own[0].astype(f32)
            for k in range(1, len(own)):
                total = total + swap(own[k].astype(bf16), unit * k).astype(f32)
            return total
        second, passing, arrived = state
        second = (second.astype(f32) + passing.astype(f32)).astype(bf16)
        return own.astype(f32) + arrived.astype(f32) + swap_ways(second, 3 * unit, unit).astype(f32)

    def scatter_ring(pieces, unit):
        return scatter_last(*scatter_first(pieces, unit), unit)

    def place_groups(pieces):
        size = pieces[0].shape[0]
        whole = jnp.zeros((size * groups, pieces[0].shape[1]), pieces[0].dtype)
        for relative, piece in zip(ring_order(groups), pieces):
            whole = lax.dynamic_update_slice_in_dim(whole, piece, (group ^ relative) * size, 0)
        return whole

    def fetch_side(bundle):
        received = swap(pick(bundle, 1 - side), narrow)
        return place([pick(bundle, side), received], side, 0)

    def halves(array):
        return array.reshape(depth, -1, 2, array.shape[-1] // 2).transpose(2, 0, 1, 3)

    def from_chips(array):
        return [swap(array, over_chips(k, s)) for k, s in chips]

    def to_chips(pieces):
        return [swap(piece, over_chips(k, s)) for (k, s), piece in zip(chips[1:], pieces)]

    def reduce_cores(own, other):
        return own.astype(f32) + swap(other, 1).astype(f32)

    def group_blocks(total):
        blocks = total.reshape(groups, 2 * depth, -1)
        return [pick(blocks, group ^ k) for k in ring_order(groups)]

    def reduce_side(total):
        total = total.reshape(2, depth, -1)
        kept = pick(total, side)
        received = swap(pick(total, 1 - side).astype(bf16), narrow).astype(f32)
        return place([kept[None], received[None]], side, 0)

    def join(array):
        return array.transpose(1, 2, 0, 3).reshape(depth, array.shape[2], -1)

    attn_bundle = jnp.concatenate(
        [halves(query_key_value_weight), halves(attention_out_weight.T[:, None])], axis=2
    ).reshape(2, depth, 4 * half)
    mlp_bundle = jnp.concatenate(
        [halves(feedforward_in_weight), halves(feedforward_out_weight.T[:, None])], axis=2
    ).reshape(2, depth, 3 * hidden)
    lanes = -(-3 * hidden // 128) * 128
    mlp_bundle = jnp.pad(mlp_bundle, ((0, 0), (0, 0), (0, lanes - 3 * hidden)))

    both = jnp.stack([inputs, grad_out])
    received = swap(pick(both, 1 - core, 1), 1)
    features = place([pick(both, core, 1), received], core, 2)
    unit_mask = 2 * narrow
    attn_pair = fetch_side(attn_bundle)
    features = after(features, attn_pair)
    shards = from_chips(features)
    if groups >= 4:
        quad = [attn_pair, *ring_first(attn_pair, unit_mask)]
        quad, shards = lax.optimization_barrier((quad, shards))
        quad.append(ring_last(quad[2], unit_mask))
        if groups > 4:
            quad = [q for quads in gather_ring(jnp.stack(quad), 4 * unit_mask, groups // 4) for q in quads]
    else:
        quad = gather_ring(attn_pair, unit_mask, groups)
    mlp_pair = fetch_side(after(mlp_bundle, shards))
    gains = after(jnp.stack([attn_gain, mlp_gain]), shards)
    gains = place([gains, swap(gains, 1)], core, 1)
    gains = place([swap(gains, 2 * k) for k in range(columns)], column, 1)
    attn_own = place_groups(quad)
    attn_other = swap(attn_own, 1)
    mlp_pair = after(mlp_pair, attn_own)
    mlp_first = ring_first(mlp_pair, unit_mask) if groups >= 4 else None
    token = (jnp.arange(rows) // block) ^ side
    positions = ((group * 2 + token) * block + jnp.arange(rows) % block).astype(f32)
    cosine, sine = rope_tables(positions, width)

    rows_in, grad_rows, normed_one, query, pair = call(
        functools.partial(project, chips),
        [((rows, model), bf16)] * 3 + [((rows, width), bf16), ((rows, span), bf16)],
        at, *shards, attn_own, attn_other, gains, cosine, sine,
    )
    pairs = gather_ring(pair, unit_mask, groups)
    out_own = from_chips(after(attn_own[:, 3 * half :], pair))
    if groups >= 4:
        mlp_quad = [mlp_pair, *mlp_first]
        pairs, mlp_quad = lax.optimization_barrier((pairs, mlp_quad))
        mlp_quad.append(ring_last(mlp_quad[2], unit_mask))
        if groups > 4:
            mlp_quad = [q for quads in gather_ring(jnp.stack(mlp_quad), 4 * unit_mask, groups // 4) for q in quads]
    else:
        mlp_quad = gather_ring(mlp_pair, unit_mask, groups)
    context, pairs, total = call(
        functools.partial(attend, len(pairs)),
        [((rows, width), bf16), ((length, span), bf16), ((8, rows), f32)],
        at, query, *pairs,
    )
    context, out_own, mlp_quad = lax.optimization_barrier((context, out_own, mlp_quad))
    out_own = jnp.stack(out_own)
    out_other = swap(out_own, 1)
    contexts = from_chips(context)
    mlp_own = place_groups(mlp_quad)
    mlp_other = swap(mlp_own, 1)
    middle, middle_rows, normed_two, unit, active, mlp_gain_part, grad_two, *sends = call(
        functools.partial(feed, chips),
        [((block, span), f32), ((part, model), f32), ((rows, model), bf16), ((2, rows, 2 * hidden), bf16),
         ((2, rows, hidden), bf16), ((1, model), f32), ((part, model), f32)] + [((part, model), bf16)] * (len(chips) - 1),
        at, *contexts, out_own, out_other, rows_in, grad_rows, mlp_own, mlp_other, gains,
        scratch=[((rows, model), f32)],
    )
    received = to_chips(sends)
    grad_mlp_own, grad_mlp_other, branch, *branch_sends = call(
        functools.partial(settle, chips),
        [((model, lanes), bf16)] * 2 + [((block, span), f32)] + [((block, span), bf16)] * (len(chips) - 1),
        at, normed_two, unit, active, grad_rows, mlp_own, mlp_other, middle,
        scratch=[((rows, model), f32)],
    )
    grad_middle, grad_low = call(
        functools.partial(turn), [((part, model), f32), ((part, model), bf16)],
        at, grad_two, *received, middle_rows, grad_rows, gains,
    )
    grad_pieces = from_chips(grad_low)
    grad_mlp = reduce_cores(grad_mlp_own, grad_mlp_other)
    grad_pieces, grad_mlp = lax.optimization_barrier((grad_pieces, grad_mlp))
    mlp_state = scatter_first(group_blocks(grad_mlp), unit_mask)
    grad_attn, grad_query, grad_pairs = call(
        functools.partial(reflect, chips),
        [((rows, model), bf16), ((rows, width), f32), ((length, span), f32)],
        at, *grad_pieces, attn_own, attn_other, query, pairs, total,
    )
    if groups >= 4:
        mlp_state, grad_pairs, branch_sends = lax.optimization_barrier((mlp_state, grad_pairs, branch_sends))
    grad_pairs = scatter_ring(list(grad_pairs.reshape(groups, rows, span)), unit_mask)

    for piece in to_chips(branch_sends):
        branch = branch + piece.astype(f32)
    branch = branch.astype(bf16).reshape(block, 2, width)
    result = place([pick(branch, core, 1)[None], swap(pick(branch, 1 - core, 1), 1)[None]], core, 0)

    grad_pairs, mlp_state = lax.optimization_barrier((grad_pairs, mlp_state))
    grad_mlp = scatter_last(*mlp_state, unit_mask)
    grad_projected, attn_gain_part, grad_one, *sends = call(
        functools.partial(unwind, chips),
        [((2, rows, 3 * half), bf16), ((1, model), f32), ((part, model), f32)] + [((part, model), bf16)] * (len(chips) - 1),
        at, grad_query, grad_pairs, cosine, sine, rows_in, attn_own, attn_other,
        scratch=[((rows, model), f32)],
    )
    received = to_chips(sends)
    grad_attn_own, grad_attn_other = call(
        functools.partial(repay), [((model, 4 * half), bf16)] * 2,
        at, normed_one, grad_projected, grad_attn, context,
    )
    grad_attn_weight = reduce_cores(grad_attn_own, grad_attn_other)
    grad_attn_weight, grad_mlp, received = lax.optimization_barrier((grad_attn_weight, grad_mlp, received))
    grad_mlp = join(reduce_side(grad_mlp)[..., : 3 * hidden].reshape(2, depth, 3, hidden))
    grad_attn_weight = scatter_ring(group_blocks(grad_attn_weight), unit_mask)
    grad_attn_weight = join(reduce_side(grad_attn_weight).reshape(2, depth, 4, half))
    sends = call(
        functools.partial(finish, narrow), [((part, width), f32)] * narrow,
        at, grad_one, *received, rows_in, grad_middle, gains,
        scratch=[((part, model), f32)],
    )
    grad_inputs = place(
        [place([swap(sends[2 * k + c], 2 * k + c) for k in range(columns)], column, 0)[None] for c in range(2)],
        core, 0,
    )
    gain_grads = jnp.concatenate([after(attn_gain_part, *received), mlp_gain_part], axis=0).reshape(2, narrow, width)
    gain_total = pick(gain_grads, narrow_at, 1)
    for m in range(1, narrow):
        gain_total = gain_total + swap(pick(gain_grads, narrow_at ^ m, 1), m)
    gain_total = gain_total + swap(gain_total, narrow)
    for mask in ring_masks(groups):
        gain_total = gain_total + swap(gain_total, 2 * narrow * mask)
    return (
        result,
        grad_inputs,
        gain_total[0],
        grad_attn_weight[:, :3],
        grad_attn_weight[:, 3].T,
        gain_total[1],
        grad_mlp[:, :2],
        grad_mlp[:, 2].T,
    )


def solution(mesh):
    in_specs = (
        P(None, "wide", "narrow"),
        P("narrow"),
        P("wide", None, "narrow"),
        P("narrow", "wide"),
        P("narrow"),
        P("wide", None, "narrow"),
        P("narrow", "wide"),
        P(None, "wide", "narrow"),
    )
    out_specs = (
        P(None, "wide", "narrow"),
        P(None, "wide", "narrow"),
        P("narrow"),
        P("wide", None, "narrow"),
        P("narrow", "wide"),
        P("narrow"),
        P("wide", None, "narrow"),
        P("narrow", "wide"),
    )
    step = functools.partial(body, mesh.shape["wide"], mesh.shape["narrow"])
    return jax.shard_map(step, mesh=mesh, in_specs=in_specs, out_specs=out_specs, check_vma=False)
```

```python
import functools
import math

import jax
import jax.numpy as jnp
from jax import lax
from jax.experimental import pallas as pl
from jax.experimental.pallas import tpu as pltpu
from jax.sharding import PartitionSpec as P

HEAD_DIM = 64
eps_norm = 1e-05
rope_base = 160000.0
f32 = jnp.float32
bf16 = jnp.bfloat16


def mm(a, b):
    return lax.dot_general(a, b, (((1,), (0,)), ((), ())), preferred_element_type=f32)


def mm_nt(a, b):
    return lax.dot_general(a, b, (((1,), (1,)), ((), ())), preferred_element_type=f32)


def aligned(index, size):
    return pl.ds(pl.multiple_of(index * size, size), size)


def norm_rows(rows):
    width = rows.shape[-1]
    average = jnp.sum(rows, axis=-1, keepdims=True) / width
    variance = jnp.sum(rows * rows, axis=-1, keepdims=True) / width - average * average
    inverse = lax.rsqrt(variance + eps_norm)
    return (rows - average) * inverse, inverse


def norm_backward(grad_normed, centred, inverse, gain):
    width = grad_normed.shape[-1]
    scaled = grad_normed * gain
    row_total = jnp.sum(scaled, axis=-1, keepdims=True)
    row_along = jnp.sum(scaled * centred, axis=-1, keepdims=True)
    return inverse * (scaled - row_total / width - centred * (row_along / width))


def rope_tables(positions, lanes):
    half_dim = HEAD_DIM // 2
    frequency = rope_base ** (-jnp.arange(half_dim).astype(f32) * 2.0 / HEAD_DIM)
    angles = positions[:, None] * frequency[None, :]
    angles = jnp.concatenate([angles, angles] * (lanes // HEAD_DIM), axis=-1)
    return jnp.cos(angles), jnp.sin(angles)


def rotated(tensor):
    lanes, half_dim = tensor.shape[-1], HEAD_DIM // 2
    lane = lax.broadcasted_iota(jnp.int32, tensor.shape, 1)
    up = pltpu.roll(tensor, half_dim, 1)
    down = pltpu.roll(tensor, lanes - half_dim, 1)
    return jnp.where(lane % HEAD_DIM < half_dim, -down, up)


def call(kernel, outs, at, *arrays, scratch=()):
    return pl.pallas_call(
        kernel,
        out_shape=[jax.ShapeDtypeStruct(shape, dtype) for shape, dtype in outs],
        in_specs=[pl.BlockSpec(memory_space=pltpu.SMEM)]
        + [pl.BlockSpec(memory_space=pltpu.VMEM)] * len(arrays),
        out_specs=[pl.BlockSpec(memory_space=pltpu.VMEM)] * len(outs),
        scratch_shapes=[pltpu.VMEM(shape, dtype) for shape, dtype in scratch],
        compiler_params=pltpu.CompilerParams(vmem_limit_bytes=60 * 1024 * 1024),
        name=kernel.func.__name__,
    )(at, *arrays)


def ring_masks(count):
    masks, unit = [], 1
    while unit < count:
        masks += [unit] + ([3 * unit] if 4 * unit <= count else [])
        unit *= 4
    return masks


def pick(array, index, axis=0):
    return lax.dynamic_index_in_dim(array, index, axis=axis, keepdims=False)


def place(pieces, own, axis):
    count = len(pieces)
    if count == 1:
        return pieces[0]
    if count == 2:
        return jnp.where(
            own == 0,
            jnp.concatenate(pieces, axis=axis),
            jnp.concatenate(pieces[::-1], axis=axis),
        )
    size = pieces[0].shape[axis]
    shape = list(pieces[0].shape)
    shape[axis] = size * count
    whole = jnp.zeros(shape, pieces[0].dtype)
    for relative, piece in enumerate(pieces):
        whole = lax.dynamic_update_slice_in_dim(whole, piece, (own ^ relative) * size, axis)
    return whole


def project(chips, at, *refs):
    shards, refs = refs[: len(chips)], refs[len(chips) :]
    own, other, gains, cosine, sine, rows_ref, grad_ref, normed_ref, query_ref, pair_ref = refs
    block, span = shards[0].shape[1:]
    half = own.shape[1] // 4
    for (k, s), shard in zip(chips, shards):
        lanes = aligned(at[0] ^ k, span)
        rows_ref[s * block : (s + 1) * block, lanes] = shard[0]
        grad_ref[s * block : (s + 1) * block, lanes] = shard[1]
    centred, _ = norm_rows(rows_ref[...].astype(f32))
    normed = (centred * gains[0:1, :]).astype(bf16)
    normed_ref[...] = normed
    queries, keys, values = [], [], []
    for weight in (own, other):
        projected = mm(normed, weight[:, : 3 * half])
        queries.append(projected[:, :half])
        keys.append(projected[:, half : 2 * half])
        values.append(projected[:, 2 * half :])
    query, key = jnp.concatenate(queries, axis=1), jnp.concatenate(keys, axis=1)
    cosine, sine = cosine[...], sine[...]
    query = (query * cosine + rotated(query) * sine).astype(bf16)
    key = (key * cosine + rotated(key) * sine).astype(bf16)
    query_ref[...] = query * jnp.asarray(HEAD_DIM**-0.5, bf16)
    pair_ref[:, : 2 * half] = key
    pair_ref[:, 2 * half :] = jnp.concatenate(values, axis=1).astype(bf16)


def attend(parts, at, query_ref, *refs):
    pieces, (context_ref, pairs_ref, total_ref) = refs[:parts], refs[parts:]
    start = 0
    for piece in pieces:
        pairs_ref[start : start + piece.shape[0], :] = piece[...]
        start += piece.shape[0]
    width = query_ref.shape[1]
    values = pairs_ref[:, width:].T
    contexts = []
    for h in range(width // HEAD_DIM):
        lanes = slice(h * HEAD_DIM, (h + 1) * HEAD_DIM)
        scores = mm_nt(pairs_ref[:, lanes], query_ref[:, lanes])
        peak = jnp.max(scores, axis=0, keepdims=True)
        log_total = peak + jnp.log(jnp.sum(jnp.exp(scores - peak), axis=0, keepdims=True))
        probs = jnp.exp(scores - log_total).astype(bf16)
        contexts.append(mm(values[lanes], probs))
        total_ref[h : h + 1, :] = log_total
    context_ref[...] = jnp.concatenate(contexts, axis=0).T.astype(bf16)


def feed(chips, at, *refs):
    count = len(chips)
    contexts, refs = refs[:count], refs[count:]
    (out_own, out_other, rows_ref, grad_ref, own, other, gains), refs = refs[:7], refs[7:]
    (middle_ref, middle_rows_ref, normed_ref, unit_ref, active_ref, gain_ref, total_ref), refs = refs[:7], refs[7:]
    pieces, scratch = refs[:-1], refs[-1]
    hidden = active_ref.shape[2]
    block, span = middle_ref.shape
    part = total_ref.shape[0]
    middle = rows_ref[...].astype(f32)
    for p, (k, s) in enumerate(chips):
        context = contexts[p][...]
        if s:
            context = jnp.concatenate([context[block:], context[:block]], axis=0)
        middle = middle + mm_nt(context, jnp.concatenate([out_own[p], out_other[p]], axis=1))
    scratch[...] = middle
    middle_ref[...] = scratch[:block, aligned(at[0], span)]
    middle_rows_ref[...] = scratch[aligned(at[0], part), :]
    centred, _ = norm_rows(middle)
    normed = (centred * gains[1:2, :]).astype(bf16)
    normed_ref[...] = normed
    partial = jnp.zeros_like(middle)
    for b, weight in enumerate((own, other)):
        gate_up = mm(normed, weight[:, : 2 * hidden])
        gate, lift = gate_up[:, :hidden], gate_up[:, hidden:]
        share = 0.5 + 0.5 * lax.erf(gate * math.sqrt(0.5))
        bent = gate * share
        active_ref[b] = (bent * lift).astype(bf16)
        slope = share + gate * jnp.exp(-0.5 * gate * gate) * (1.0 / math.sqrt(2.0 * math.pi))
        back = mm(grad_ref[...], weight[:, 2 * hidden : 3 * hidden])
        unit = jnp.concatenate([back * lift * slope, back * bent], axis=1).astype(bf16)
        unit_ref[b] = unit
        partial = partial + mm_nt(unit, weight[:, : 2 * hidden])
    gain_ref[...] = jnp.sum(partial * centred, axis=0, keepdims=True)
    scratch[...] = partial
    cut_rows(chips, at, scratch, total_ref, pieces)


def cut_rows(chips, at, scratch, total_ref, pieces):
    part = total_ref.shape[0]
    columns = scratch.shape[0] // (2 * part)
    for p, (k, s) in enumerate(chips):
        rows = scratch[aligned(s * columns + (at[0] ^ k), part), :]
        if p:
            pieces[p - 1][...] = rows.astype(bf16)
        else:
            total_ref[...] = rows


def turn(at, total_ref, *refs):
    pieces, (middle_ref, grad_ref, gains, grad_middle_ref, low_ref) = refs[:-5], refs[-5:]
    part = total_ref.shape[0]
    total = total_ref[...]
    for piece in pieces:
        total = total + piece[...].astype(f32)
    centred, inverse = norm_rows(middle_ref[...])
    grad = grad_ref[aligned(at[0], part), :].astype(f32)
    grad = grad + norm_backward(total, centred, inverse, gains[1:2, :])
    grad_middle_ref[...] = grad
    low_ref[...] = grad.astype(bf16)


def settle(chips, at, *refs):
    (normed_ref, unit_ref, active_ref, grad_ref, own, other, middle_ref), refs = refs[:7], refs[7:]
    (own_ref, other_ref, total_ref), refs = refs[:3], refs[3:]
    pieces, scratch = refs[:-1], refs[-1]
    hidden = active_ref.shape[2]
    block, span = total_ref.shape
    normed, grad = normed_ref[...].T, grad_ref[...].T
    for b, out in enumerate((other_ref, own_ref)):
        out[:, : 2 * hidden] = mm(normed, unit_ref[1 - b]).astype(bf16)
        out[:, 2 * hidden : 3 * hidden] = mm(grad, active_ref[1 - b]).astype(bf16)
        if out.shape[1] > 3 * hidden:
            out[:, 3 * hidden :] = jnp.zeros((out.shape[0], out.shape[1] - 3 * hidden), bf16)
    scratch[...] = mm_nt(active_ref[0], own[:, 2 * hidden : 3 * hidden]) + mm_nt(active_ref[1], other[:, 2 * hidden : 3 * hidden])
    for p, (k, s) in enumerate(chips):
        piece = scratch[s * block : (s + 1) * block, aligned(at[0] ^ k, span)]
        if p:
            pieces[p - 1][...] = piece.astype(bf16)
        else:
            total_ref[...] = piece + middle_ref[...]


def reflect(chips, at, *refs):
    pieces, refs = refs[: len(chips)], refs[len(chips) :]
    own, other, query_ref, pairs_ref, total_ref, grad_attn_ref, grad_query_ref, grad_pairs_ref = refs
    part = pieces[0].shape[0]
    rows, width = query_ref.shape
    columns = rows // (2 * part)
    half = width // 2
    for (k, s), piece in zip(chips, pieces):
        grad_attn_ref[aligned(s * columns + (at[0] ^ k), part), :] = piece[...]
    grad_attn = grad_attn_ref[...]
    grad_context = jnp.concatenate(
        [mm(grad_attn, own[:, 3 * half :]), mm(grad_attn, other[:, 3 * half :])], axis=1
    ).astype(bf16)
    keys = pairs_ref[:, :width].T
    grad_queries = []
    for h in range(width // HEAD_DIM):
        lanes = slice(h * HEAD_DIM, (h + 1) * HEAD_DIM)
        query = query_ref[:, lanes]
        grad = grad_context[:, lanes]
        probs = jnp.exp(mm_nt(pairs_ref[:, lanes], query) - total_ref[h : h + 1, :])
        value_lanes = slice(width + h * HEAD_DIM, width + (h + 1) * HEAD_DIM)
        grad_probs = mm_nt(pairs_ref[:, value_lanes], grad)
        delta = jnp.sum(probs * grad_probs, axis=0, keepdims=True)
        grad_scores = (probs * (grad_probs - delta)).astype(bf16)
        grad_pairs_ref[:, lanes] = mm(grad_scores, query)
        grad_pairs_ref[:, value_lanes] = mm(probs.astype(bf16), grad)
        grad_queries.append(mm(keys[lanes], grad_scores))
    grad_query_ref[...] = jnp.concatenate(grad_queries, axis=0).T * HEAD_DIM**-0.5


def unwind(chips, at, *refs):
    (grad_query_ref, grad_pairs_ref, cosine, sine, rows_ref, own, other), refs = refs[:7], refs[7:]
    (grad_projected_ref, gain_ref, total_ref), refs = refs[:3], refs[3:]
    pieces, scratch = refs[:-1], refs[-1]
    width = grad_query_ref.shape[1]
    half = width // 2
    cosine, sine = cosine[...], sine[...]
    grad_query, grad_key = grad_query_ref[...], grad_pairs_ref[:, :width]
    grad_query = (grad_query * cosine - rotated(grad_query * sine)).astype(bf16)
    grad_key = (grad_key * cosine - rotated(grad_key * sine)).astype(bf16)
    grad_value = grad_pairs_ref[:, width:].astype(bf16)
    partial = 0.0
    for b, weight in enumerate((own, other)):
        lanes = slice(b * half, (b + 1) * half)
        grad = jnp.concatenate([grad_query[:, lanes], grad_key[:, lanes], grad_value[:, lanes]], axis=1)
        grad_projected_ref[b] = grad
        partial = partial + mm_nt(grad, weight[:, : 3 * half])
    centred, _ = norm_rows(rows_ref[...].astype(f32))
    gain_ref[...] = jnp.sum(partial * centred, axis=0, keepdims=True)
    scratch[...] = partial
    cut_rows(chips, at, scratch, total_ref, pieces)


def repay(at, normed_ref, grad_projected_ref, grad_attn_ref, context_ref, own_ref, other_ref):
    half = context_ref.shape[1] // 2
    normed, grad_attn = normed_ref[...].T, grad_attn_ref[...].T
    for b, out in ((1, other_ref), (0, own_ref)):
        out[:, : 3 * half] = mm(normed, grad_projected_ref[b]).astype(bf16)
        out[:, 3 * half :] = mm(grad_attn, context_ref[:, b * half : (b + 1) * half]).astype(bf16)


def finish(narrow, at, total_ref, *refs):
    pieces, (rows_ref, grad_middle_ref, gains), outs, scratch = refs[: -narrow - 4], refs[-narrow - 4 : -narrow - 1], refs[-narrow - 1 : -1], refs[-1]
    part = total_ref.shape[0]
    width = outs[0].shape[1]
    total = total_ref[...]
    for piece in pieces:
        total = total + piece[...].astype(f32)
    centred, inverse = norm_rows(rows_ref[aligned(at[0], part), :].astype(f32))
    scratch[...] = grad_middle_ref[...] + norm_backward(total, centred, inverse, gains[0:1, :])
    for m, out in enumerate(outs):
        out[...] = scratch[:, aligned(at[1] ^ m, width)]


def body(
    wide,
    narrow,
    inputs,
    attn_gain,
    query_key_value_weight,
    attention_out_weight,
    mlp_gain,
    feedforward_in_weight,
    feedforward_out_weight,
    grad_out,
):
    groups, columns = wide // 2, narrow // 2
    _, block, width = inputs.shape
    model = width * narrow
    depth = query_key_value_weight.shape[0]
    hidden = feedforward_out_weight.shape[0] // 2
    half, span = width // 2, 2 * width
    part = block // columns
    rows = 2 * block
    length = groups * rows
    wide_at, narrow_at = lax.axis_index("wide"), lax.axis_index("narrow")
    group, side = wide_at // 2, wide_at % 2
    column, core = narrow_at // 2, narrow_at % 2
    at = jnp.stack([column, narrow_at]).astype(jnp.int32)
    chips = [(k, s) for s in range(2) for k in range(columns)]

    def swap(array, mask):
        if mask == 0:
            return array
        return lax.ppermute(
            array, ("wide", "narrow"), [(i, i ^ mask) for i in range(wide * narrow)]
        )

    def over_chips(column_rel, side_rel):
        return 2 * column_rel + narrow * side_rel

    def over_groups(group_rel):
        return 2 * narrow * group_rel

    def after(array, *others):
        return lax.optimization_barrier((array, *others))[0]

    def swap_ways(array, even, odd):
        pairs = [(i, i ^ (odd if i % 2 else even)) for i in range(wide * narrow)]
        return lax.ppermute(array, ("wide", "narrow"), pairs)

    def ring_order(count):
        if count < 4:
            return list(range(count))
        quad = [0, 1 + 2 * core, 3 - 2 * core, 2]
        return [low + 4 * high for high in ring_order(count // 4) for low in quad]

    def ring_first(array, unit):
        return swap_ways(array, unit, 3 * unit), swap_ways(array, 3 * unit, unit)

    def ring_last(second, unit):
        return swap_ways(second, unit, 3 * unit)

    def gather_ring(array, unit, count):
        if count < 4:
            return [swap(array, unit * k) for k in range(count)]
        first, second = ring_first(array, unit)
        quad = [array, first, second, ring_last(second, unit)]
        if count == 4:
            return quad
        return [q for quads in gather_ring(jnp.stack(quad), 4 * unit, count // 4) for q in quads]

    def scatter_first(pieces, unit):
        count = len(pieces)
        if count < 4:
            return pieces, None
        if count > 4:
            stacked = [jnp.stack(pieces[k : k + 4]) for k in range(0, count, 4)]
            pieces = list(scatter_ring(stacked, 4 * unit))
        own, first, second, across = pieces
        passing = swap_ways(across.astype(bf16), unit, 3 * unit)
        arrived = swap_ways(first.astype(bf16), unit, 3 * unit)
        return own, (second, passing, arrived)

    def scatter_last(own, state, unit):
        if state is None:
            total = own[0].astype(f32)
            for k in range(1, len(own)):
                total = total + swap(own[k].astype(bf16), unit * k).astype(f32)
            return total
        second, passing, arrived = state
        second = (second.astype(f32) + passing.astype(f32)).astype(bf16)
        return own.astype(f32) + arrived.astype(f32) + swap_ways(second, 3 * unit, unit).astype(f32)

    def scatter_ring(pieces, unit):
        return scatter_last(*scatter_first(pieces, unit), unit)

    def place_groups(pieces, order=None):
        size = pieces[0].shape[0]
        whole = jnp.zeros((size * groups, pieces[0].shape[1]), pieces[0].dtype)
        for relative, piece in zip(order or ring_order(groups), pieces):
            whole = lax.dynamic_update_slice_in_dim(whole, piece, (group ^ relative) * size, 0)
        return whole

    def fetch_side(bundle):
        received = swap(pick(bundle, 1 - side), narrow)
        return place([pick(bundle, side), received], side, 0)

    def halves(array):
        return array.reshape(depth, -1, 2, array.shape[-1] // 2).transpose(2, 0, 1, 3)

    def from_chips(array):
        return [swap(array, over_chips(k, s)) for k, s in chips]

    def to_chips(pieces):
        return [swap(piece, over_chips(k, s)) for (k, s), piece in zip(chips[1:], pieces)]

    def reduce_cores(own, other, *others):
        return own.astype(f32) + after(swap(other, 1), *others).astype(f32)

    def group_blocks(total):
        blocks = total.reshape(groups, 2 * depth, -1)
        return [pick(blocks, group ^ k) for k in ring_order(groups)]

    def reduce_side(total):
        total = total.reshape(2, depth, -1)
        kept = pick(total, side)
        received = swap(pick(total, 1 - side).astype(bf16), narrow).astype(f32)
        return place([kept[None], received[None]], side, 0)

    def join(array):
        return array.transpose(1, 2, 0, 3).reshape(depth, array.shape[2], -1)

    attn_bundle = jnp.concatenate(
        [halves(query_key_value_weight), halves(attention_out_weight.T[:, None])], axis=2
    ).reshape(2, depth, 4 * half)
    mlp_bundle = jnp.concatenate(
        [halves(feedforward_in_weight), halves(feedforward_out_weight.T[:, None])], axis=2
    ).reshape(2, depth, 3 * hidden)
    lanes = -(-3 * hidden // 128) * 128
    mlp_bundle = jnp.pad(mlp_bundle, ((0, 0), (0, 0), (0, lanes - 3 * hidden)))

    both = jnp.stack([inputs, grad_out])
    received = swap(pick(both, 1 - core, 1), 1)
    features = place([pick(both, core, 1), received], core, 2)
    unit_mask = 2 * narrow
    attn_pair = fetch_side(attn_bundle)
    features = after(features, attn_pair)
    shards = from_chips(features)
    gains = after(jnp.stack([attn_gain, mlp_gain]), shards)
    gains = place([gains, swap(gains, 1)], core, 1)
    gains = place([swap(gains, 2 * k) for k in range(columns)], column, 1)
    mlp_pair = fetch_side(after(mlp_bundle, shards))
    if groups >= 4:
        quad = [attn_pair, *ring_first(attn_pair, unit_mask)]
        quad, shards = lax.optimization_barrier((quad, shards))
        quad.append(ring_last(quad[2], unit_mask))
        if groups > 4:
            quad = [q for quads in gather_ring(jnp.stack(quad), 4 * unit_mask, groups // 4) for q in quads]
    else:
        quad = gather_ring(attn_pair, unit_mask, groups)
    quad, mlp_pair, gains = lax.optimization_barrier((quad, mlp_pair, gains))
    attn_own = place_groups(quad)
    attn_other = swap(attn_own, 1)
    mlp_quad = [mlp_pair, *ring_first(mlp_pair, unit_mask)] if groups >= 4 else []
    out_own = from_chips(after(attn_own[:, 3 * half :], quad))
    token = (jnp.arange(rows) // block) ^ side
    positions = ((group * 2 + token) * block + jnp.arange(rows) % block).astype(f32)
    cosine, sine = rope_tables(positions, width)

    rows_in, grad_rows, normed_one, query, pair = call(
        functools.partial(project, chips),
        [((rows, model), bf16)] * 3 + [((rows, width), bf16), ((rows, span), bf16)],
        at, *shards, attn_own, attn_other, gains, cosine, sine,
    )
    pair, mlp_quad, out_own = lax.optimization_barrier((pair, mlp_quad, out_own))
    out_own = jnp.stack(out_own)
    out_other = swap(out_own, 1)
    pairs = gather_ring(pair, unit_mask, groups)
    early = [swap(piece, 1) for piece in mlp_quad]
    pairs, out_other, early = lax.optimization_barrier((pairs, out_other, early))
    if groups >= 4:
        mlp_quad.append(ring_last(after(mlp_quad[2], pairs), unit_mask))
    context, pairs, total = call(
        functools.partial(attend, len(pairs)),
        [((rows, width), bf16), ((length, span), bf16), ((8, rows), f32)],
        at, query, *pairs,
    )
    contexts = from_chips(context)
    if groups >= 4:
        late = after(mlp_quad.pop(), contexts)
        mlp_quad, early = [*mlp_quad, late], [*early, swap(late, 1)]
        order = ring_order(4)
        turned = [order[k] for k in (0, 2, 1, 3)]
        if groups > 4:
            mlp_quad = [q for quads in gather_ring(jnp.stack(mlp_quad), 4 * unit_mask, groups // 4) for q in quads]
            early = [q for quads in gather_ring(jnp.stack(early), 4 * unit_mask, groups // 4) for q in quads]
            order = [low + 4 * high for high in ring_order(groups // 4) for low in order]
            turned = [low + 4 * high for high in ring_order(groups // 4) for low in turned]
        mlp_own, mlp_other = place_groups(mlp_quad, order), place_groups(early, turned)
    else:
        mlp_own = place_groups(gather_ring(mlp_pair, unit_mask, groups))
        mlp_other = swap(mlp_own, 1)
    middle, middle_rows, normed_two, unit, active, mlp_gain_part, grad_two, *sends = call(
        functools.partial(feed, chips),
        [((block, span), f32), ((part, model), f32), ((rows, model), bf16), ((2, rows, 2 * hidden), bf16),
         ((2, rows, hidden), bf16), ((1, model), f32), ((part, model), f32)] + [((part, model), bf16)] * (len(chips) - 1),
        at, *contexts, out_own, out_other, rows_in, grad_rows, mlp_own, mlp_other, gains,
        scratch=[((rows, model), f32)],
    )
    received = to_chips(sends)
    grad_mlp_own, grad_mlp_other, branch, *branch_sends = call(
        functools.partial(settle, chips),
        [((model, lanes), bf16)] * 2 + [((block, span), f32)] + [((block, span), bf16)] * (len(chips) - 1),
        at, normed_two, unit, active, grad_rows, mlp_own, mlp_other, middle,
        scratch=[((rows, model), f32)],
    )
    grad_mlp_other = after(grad_mlp_other, received)
    grad_middle, grad_low = call(
        functools.partial(turn), [((part, model), f32), ((part, model), bf16)],
        at, grad_two, *received, middle_rows, grad_rows, gains,
    )
    grad_pieces = from_chips(grad_low)
    grad_mlp = reduce_cores(grad_mlp_own, grad_mlp_other, grad_low)
    mlp_state = scatter_first(group_blocks(grad_mlp), unit_mask)
    if groups >= 4:
        grad_pieces, passing = lax.optimization_barrier((grad_pieces, mlp_state[1][1]))
        mlp_state = (mlp_state[0], (mlp_state[1][0], passing, mlp_state[1][2]))
    grad_attn, grad_query, grad_pairs = call(
        functools.partial(reflect, chips),
        [((rows, model), bf16), ((rows, width), f32), ((length, span), f32)],
        at, *grad_pieces, attn_own, attn_other, query, pairs, total,
    )
    if groups >= 4:
        mlp_state, grad_pairs, branch_sends = lax.optimization_barrier((mlp_state, grad_pairs, branch_sends))
    grad_pairs = scatter_ring(list(grad_pairs.reshape(groups, rows, span)), unit_mask)

    branch_received = to_chips(branch_sends)
    grad_pairs, mlp_state, branch_received = lax.optimization_barrier((grad_pairs, mlp_state, branch_received))
    for piece in branch_received:
        branch = branch + piece.astype(f32)
    branch = branch.astype(bf16).reshape(block, 2, width)
    result = place([pick(branch, core, 1)[None], swap(pick(branch, 1 - core, 1), 1)[None]], core, 0)

    grad_mlp = scatter_last(*mlp_state, unit_mask)
    grad_projected, attn_gain_part, grad_one, *sends = call(
        functools.partial(unwind, chips),
        [((2, rows, 3 * half), bf16), ((1, model), f32), ((part, model), f32)] + [((part, model), bf16)] * (len(chips) - 1),
        at, grad_query, grad_pairs, cosine, sine, rows_in, attn_own, attn_other,
        scratch=[((rows, model), f32)],
    )
    received = to_chips(sends)
    grad_attn_own, grad_attn_other = call(
        functools.partial(repay), [((model, 4 * half), bf16)] * 2,
        at, normed_one, grad_projected, grad_attn, context,
    )
    grad_attn_other, grad_mlp, received = lax.optimization_barrier((grad_attn_other, grad_mlp, received))
    grad_attn_weight = reduce_cores(grad_attn_own, grad_attn_other)
    grad_mlp = join(reduce_side(grad_mlp)[..., : 3 * hidden].reshape(2, depth, 3, hidden))
    grad_attn_weight_sum = grad_attn_weight
    grad_attn_weight = scatter_ring(group_blocks(grad_attn_weight), unit_mask)
    grad_attn_weight = join(reduce_side(grad_attn_weight).reshape(2, depth, 4, half))
    grad_one = after(grad_one, grad_attn_own)
    sends = call(
        functools.partial(finish, narrow), [((part, width), f32)] * narrow,
        at, grad_one, *received, rows_in, grad_middle, gains,
        scratch=[((part, model), f32)],
    )
    sends = [swap(piece, m) for m, piece in enumerate(sends)]
    sends = after(sends, grad_attn_weight_sum)
    grad_inputs = place(
        [place([sends[2 * k + c] for k in range(columns)], column, 0)[None] for c in range(2)],
        core, 0,
    )
    gain_grads = jnp.concatenate([after(attn_gain_part, grad_attn_weight_sum), mlp_gain_part], axis=0).reshape(2, narrow, width)
    gain_total = pick(gain_grads, narrow_at, 1)
    for m in range(1, narrow):
        gain_total = gain_total + swap(pick(gain_grads, narrow_at ^ m, 1), m)
    gain_total = gain_total + swap(gain_total, narrow)
    for mask in ring_masks(groups):
        gain_total = gain_total + swap(gain_total, 2 * narrow * mask)
    return (
        result,
        grad_inputs,
        gain_total[0],
        grad_attn_weight[:, :3],
        grad_attn_weight[:, 3].T,
        gain_total[1],
        grad_mlp[:, :2],
        grad_mlp[:, 2].T,
    )


def solution(mesh):
    in_specs = (
        P(None, "wide", "narrow"),
        P("narrow"),
        P("wide", None, "narrow"),
        P("narrow", "wide"),
        P("narrow"),
        P("wide", None, "narrow"),
        P("narrow", "wide"),
        P(None, "wide", "narrow"),
    )
    out_specs = (
        P(None, "wide", "narrow"),
        P(None, "wide", "narrow"),
        P("narrow"),
        P("wide", None, "narrow"),
        P("narrow", "wide"),
        P("narrow"),
        P("wide", None, "narrow"),
        P("narrow", "wide"),
    )
    step = functools.partial(body, mesh.shape["wide"], mesh.shape["narrow"])
    return jax.shard_map(step, mesh=mesh, in_specs=in_specs, out_specs=out_specs, check_vma=False)
```

```python
import functools
import math

import jax
import jax.numpy as jnp
from jax import lax
from jax.experimental import pallas as pl
from jax.experimental.pallas import tpu as pltpu
from jax.sharding import PartitionSpec as P

HEAD_DIM = 64
eps_norm = 1e-05
rope_base = 160000.0
f32 = jnp.float32
bf16 = jnp.bfloat16


def mm(a, b):
    return lax.dot_general(a, b, (((1,), (0,)), ((), ())), preferred_element_type=f32)


def mm_nt(a, b):
    return lax.dot_general(a, b, (((1,), (1,)), ((), ())), preferred_element_type=f32)


def aligned(index, size):
    return pl.ds(pl.multiple_of(index * size, size), size)


def norm_rows(rows):
    width = rows.shape[-1]
    average = jnp.sum(rows, axis=-1, keepdims=True) / width
    variance = jnp.sum(rows * rows, axis=-1, keepdims=True) / width - average * average
    inverse = lax.rsqrt(variance + eps_norm)
    return (rows - average) * inverse, inverse


def norm_backward(grad_normed, centred, inverse, gain):
    width = grad_normed.shape[-1]
    scaled = grad_normed * gain
    row_total = jnp.sum(scaled, axis=-1, keepdims=True)
    row_along = jnp.sum(scaled * centred, axis=-1, keepdims=True)
    return inverse * (scaled - row_total / width - centred * (row_along / width))


def rope_tables(positions, lanes):
    half_dim = HEAD_DIM // 2
    frequency = rope_base ** (-jnp.arange(half_dim).astype(f32) * 2.0 / HEAD_DIM)
    angles = positions[:, None] * frequency[None, :]
    angles = jnp.concatenate([angles, angles] * (lanes // HEAD_DIM), axis=-1)
    return jnp.cos(angles), jnp.sin(angles)


def rotated(tensor):
    lanes, half_dim = tensor.shape[-1], HEAD_DIM // 2
    lane = lax.broadcasted_iota(jnp.int32, tensor.shape, 1)
    up = pltpu.roll(tensor, half_dim, 1)
    down = pltpu.roll(tensor, lanes - half_dim, 1)
    return jnp.where(lane % HEAD_DIM < half_dim, -down, up)


def call(kernel, outs, at, *arrays, scratch=()):
    return pl.pallas_call(
        kernel,
        out_shape=[jax.ShapeDtypeStruct(shape, dtype) for shape, dtype in outs],
        in_specs=[pl.BlockSpec(memory_space=pltpu.SMEM)]
        + [pl.BlockSpec(memory_space=pltpu.VMEM)] * len(arrays),
        out_specs=[pl.BlockSpec(memory_space=pltpu.VMEM)] * len(outs),
        scratch_shapes=[pltpu.VMEM(shape, dtype) for shape, dtype in scratch],
        compiler_params=pltpu.CompilerParams(vmem_limit_bytes=60 * 1024 * 1024),
        name=kernel.func.__name__,
    )(at, *arrays)


def ring_masks(count):
    masks, unit = [], 1
    while unit < count:
        masks += [unit] + ([3 * unit] if 4 * unit <= count else [])
        unit *= 4
    return masks


def pick(array, index, axis=0):
    return lax.dynamic_index_in_dim(array, index, axis=axis, keepdims=False)


def place(pieces, own, axis):
    count = len(pieces)
    if count == 1:
        return pieces[0]
    if count == 2:
        return jnp.where(
            own == 0,
            jnp.concatenate(pieces, axis=axis),
            jnp.concatenate(pieces[::-1], axis=axis),
        )
    size = pieces[0].shape[axis]
    shape = list(pieces[0].shape)
    shape[axis] = size * count
    whole = jnp.zeros(shape, pieces[0].dtype)
    for relative, piece in enumerate(pieces):
        whole = lax.dynamic_update_slice_in_dim(whole, piece, (own ^ relative) * size, axis)
    return whole


def contract(rows_ref, pieces, starts, lanes):
    total = 0.0
    for piece, start in zip(pieces, starts):
        total = total + mm(rows_ref[:, aligned(start, piece.shape[0])], piece[:, lanes])
    return total


def spread(out_ref, array, pieces, starts, lanes):
    for piece, start in zip(pieces, starts):
        out_ref[:, aligned(start, piece.shape[0])] += mm_nt(array, piece[:, lanes])


def both_cores(count, at, refs):
    first = [at[2 + p] for p in range(count)]
    second = [at[2 + count + p] for p in range(count)]
    return ((refs[:count], first), (refs[count : 2 * count], second)), refs[2 * count :]


def project(chips, count, at, *refs):
    shards, refs = refs[: len(chips)], refs[len(chips) :]
    weights, refs = both_cores(count, at, refs)
    gains, cosine, sine, rows_ref, grad_ref, normed_ref, query_ref, pair_ref = refs
    block, span = shards[0].shape[1:]
    half = query_ref.shape[1] // 2
    for (k, s), shard in zip(chips, shards):
        lanes = aligned(at[0] ^ k, span)
        rows_ref[s * block : (s + 1) * block, lanes] = shard[0]
        grad_ref[s * block : (s + 1) * block, lanes] = shard[1]
    centred, _ = norm_rows(rows_ref[...].astype(f32))
    normed_ref[...] = (centred * gains[0:1, :]).astype(bf16)
    queries, keys, values = [], [], []
    for pieces, starts in weights:
        projected = contract(normed_ref, pieces, starts, slice(0, 3 * half))
        queries.append(projected[:, :half])
        keys.append(projected[:, half : 2 * half])
        values.append(projected[:, 2 * half :])
    query, key = jnp.concatenate(queries, axis=1), jnp.concatenate(keys, axis=1)
    cosine, sine = cosine[...], sine[...]
    query = (query * cosine + rotated(query) * sine).astype(bf16)
    key = (key * cosine + rotated(key) * sine).astype(bf16)
    query_ref[...] = query * jnp.asarray(HEAD_DIM**-0.5, bf16)
    pair_ref[:, : 2 * half] = key
    pair_ref[:, 2 * half :] = jnp.concatenate(values, axis=1).astype(bf16)


def attend(parts, at, query_ref, *refs):
    pieces, (context_ref, pairs_ref, total_ref) = refs[:parts], refs[parts:]
    start = 0
    for piece in pieces:
        pairs_ref[start : start + piece.shape[0], :] = piece[...]
        start += piece.shape[0]
    width = query_ref.shape[1]
    values = pairs_ref[:, width:].T
    contexts = []
    for h in range(width // HEAD_DIM):
        lanes = slice(h * HEAD_DIM, (h + 1) * HEAD_DIM)
        scores = mm_nt(pairs_ref[:, lanes], query_ref[:, lanes])
        peak = jnp.max(scores, axis=0, keepdims=True)
        log_total = peak + jnp.log(jnp.sum(jnp.exp(scores - peak), axis=0, keepdims=True))
        probs = jnp.exp(scores - log_total).astype(bf16)
        contexts.append(mm(values[lanes], probs))
        total_ref[h : h + 1, :] = log_total
    context_ref[...] = jnp.concatenate(contexts, axis=0).T.astype(bf16)


def feed(chips, count, at, *refs):
    contexts, refs = refs[: len(chips)], refs[len(chips) :]
    weights, refs = both_cores(count, at, refs)
    (out_own, out_other, rows_ref, grad_ref, gains), refs = refs[:5], refs[5:]
    (middle_ref, middle_rows_ref, normed_ref, unit_ref, active_ref, gain_ref, total_ref), refs = refs[:7], refs[7:]
    pieces, scratch = refs[:-1], refs[-1]
    hidden = active_ref.shape[2]
    block, span = middle_ref.shape
    part = total_ref.shape[0]
    middle = rows_ref[...].astype(f32)
    for p, (k, s) in enumerate(chips):
        context = contexts[p][...]
        if s:
            context = jnp.concatenate([context[block:], context[:block]], axis=0)
        middle = middle + mm_nt(context, jnp.concatenate([out_own[p], out_other[p]], axis=1))
    scratch[...] = middle
    middle_ref[...] = scratch[:block, aligned(at[0], span)]
    middle_rows_ref[...] = scratch[aligned(at[0], part), :]
    centred, _ = norm_rows(middle)
    normed_ref[...] = (centred * gains[1:2, :]).astype(bf16)
    scratch[...] = jnp.zeros_like(scratch)
    for b, (weight, starts) in enumerate(weights):
        gate_up = contract(normed_ref, weight, starts, slice(0, 2 * hidden))
        gate, lift = gate_up[:, :hidden], gate_up[:, hidden:]
        share = 0.5 + 0.5 * lax.erf(gate * math.sqrt(0.5))
        bent = gate * share
        active_ref[b] = (bent * lift).astype(bf16)
        slope = share + gate * jnp.exp(-0.5 * gate * gate) * (1.0 / math.sqrt(2.0 * math.pi))
        back = contract(grad_ref, weight, starts, slice(2 * hidden, 3 * hidden))
        unit = jnp.concatenate([back * lift * slope, back * bent], axis=1).astype(bf16)
        unit_ref[b] = unit
        spread(scratch, unit, weight, starts, slice(0, 2 * hidden))
    gain_ref[...] = jnp.sum(scratch[...] * centred, axis=0, keepdims=True)
    cut_rows(chips, at, scratch, total_ref, pieces)


def cut_rows(chips, at, scratch, total_ref, pieces):
    part = total_ref.shape[0]
    columns = scratch.shape[0] // (2 * part)
    for p, (k, s) in enumerate(chips):
        rows = scratch[aligned(s * columns + (at[0] ^ k), part), :]
        if p:
            pieces[p - 1][...] = rows.astype(bf16)
        else:
            total_ref[...] = rows


def turn(at, total_ref, *refs):
    pieces, (middle_ref, grad_ref, gains, grad_middle_ref, low_ref) = refs[:-5], refs[-5:]
    part = total_ref.shape[0]
    total = total_ref[...]
    for piece in pieces:
        total = total + piece[...].astype(f32)
    centred, inverse = norm_rows(middle_ref[...])
    grad = grad_ref[aligned(at[0], part), :].astype(f32)
    grad = grad + norm_backward(total, centred, inverse, gains[1:2, :])
    grad_middle_ref[...] = grad
    low_ref[...] = grad.astype(bf16)


def settle(chips, count, at, *refs):
    weights, refs = both_cores(count, at, refs)
    (normed_ref, unit_ref, active_ref, grad_ref, middle_ref), refs = refs[:5], refs[5:]
    (own_ref, other_ref, total_ref), refs = refs[:3], refs[3:]
    pieces, scratch = refs[:-1], refs[-1]
    hidden = active_ref.shape[2]
    block, span = total_ref.shape
    normed, grad = normed_ref[...].T, grad_ref[...].T
    for b, out in enumerate((other_ref, own_ref)):
        out[:, : 2 * hidden] = mm(normed, unit_ref[1 - b]).astype(bf16)
        out[:, 2 * hidden : 3 * hidden] = mm(grad, active_ref[1 - b]).astype(bf16)
        if out.shape[1] > 3 * hidden:
            out[:, 3 * hidden :] = jnp.zeros((out.shape[0], out.shape[1] - 3 * hidden), bf16)
    scratch[...] = jnp.zeros_like(scratch)
    for b, (weight, starts) in enumerate(weights):
        spread(scratch, active_ref[b], weight, starts, slice(2 * hidden, 3 * hidden))
    for p, (k, s) in enumerate(chips):
        piece = scratch[s * block : (s + 1) * block, aligned(at[0] ^ k, span)]
        if p:
            pieces[p - 1][...] = piece.astype(bf16)
        else:
            total_ref[...] = piece + middle_ref[...]


def reflect(chips, count, at, *refs):
    pieces, refs = refs[: len(chips)], refs[len(chips) :]
    weights, refs = both_cores(count, at, refs)
    query_ref, pairs_ref, total_ref, grad_attn_ref, grad_query_ref, grad_pairs_ref = refs
    part = pieces[0].shape[0]
    rows, width = query_ref.shape
    columns = rows // (2 * part)
    half = width // 2
    for (k, s), piece in zip(chips, pieces):
        grad_attn_ref[aligned(s * columns + (at[0] ^ k), part), :] = piece[...]
    grad_context = jnp.concatenate(
        [contract(grad_attn_ref, weight, starts, slice(3 * half, 4 * half)) for weight, starts in weights],
        axis=1,
    ).astype(bf16)
    keys = pairs_ref[:, :width].T
    grad_queries = []
    for h in range(width // HEAD_DIM):
        lanes = slice(h * HEAD_DIM, (h + 1) * HEAD_DIM)
        query = query_ref[:, lanes]
        grad = grad_context[:, lanes]
        probs = jnp.exp(mm_nt(pairs_ref[:, lanes], query) - total_ref[h : h + 1, :])
        value_lanes = slice(width + h * HEAD_DIM, width + (h + 1) * HEAD_DIM)
        grad_probs = mm_nt(pairs_ref[:, value_lanes], grad)
        delta = jnp.sum(probs * grad_probs, axis=0, keepdims=True)
        grad_scores = (probs * (grad_probs - delta)).astype(bf16)
        grad_pairs_ref[:, lanes] = mm(grad_scores, query)
        grad_pairs_ref[:, value_lanes] = mm(probs.astype(bf16), grad)
        grad_queries.append(mm(keys[lanes], grad_scores))
    grad_query_ref[...] = jnp.concatenate(grad_queries, axis=0).T * HEAD_DIM**-0.5


def unwind(chips, count, at, *refs):
    weights, refs = both_cores(count, at, refs)
    (grad_query_ref, grad_pairs_ref, cosine, sine, rows_ref), refs = refs[:5], refs[5:]
    (grad_projected_ref, gain_ref, total_ref), refs = refs[:3], refs[3:]
    pieces, scratch = refs[:-1], refs[-1]
    width = grad_query_ref.shape[1]
    half = width // 2
    cosine, sine = cosine[...], sine[...]
    grad_query, grad_key = grad_query_ref[...], grad_pairs_ref[:, :width]
    grad_query = (grad_query * cosine - rotated(grad_query * sine)).astype(bf16)
    grad_key = (grad_key * cosine - rotated(grad_key * sine)).astype(bf16)
    grad_value = grad_pairs_ref[:, width:].astype(bf16)
    scratch[...] = jnp.zeros_like(scratch)
    for b, (weight, starts) in enumerate(weights):
        lanes = slice(b * half, (b + 1) * half)
        grad = jnp.concatenate([grad_query[:, lanes], grad_key[:, lanes], grad_value[:, lanes]], axis=1)
        grad_projected_ref[b] = grad
        spread(scratch, grad, weight, starts, slice(0, 3 * half))
    centred, _ = norm_rows(rows_ref[...].astype(f32))
    gain_ref[...] = jnp.sum(scratch[...] * centred, axis=0, keepdims=True)
    cut_rows(chips, at, scratch, total_ref, pieces)


def repay(at, normed_ref, grad_projected_ref, grad_attn_ref, context_ref, own_ref, other_ref):
    half = context_ref.shape[1] // 2
    normed, grad_attn = normed_ref[...].T, grad_attn_ref[...].T
    for b, out in ((1, other_ref), (0, own_ref)):
        out[:, : 3 * half] = mm(normed, grad_projected_ref[b]).astype(bf16)
        out[:, 3 * half :] = mm(grad_attn, context_ref[:, b * half : (b + 1) * half]).astype(bf16)


def finish(narrow, at, total_ref, *refs):
    pieces, (rows_ref, grad_middle_ref, gains), outs, scratch = refs[: -narrow - 4], refs[-narrow - 4 : -narrow - 1], refs[-narrow - 1 : -1], refs[-1]
    part = total_ref.shape[0]
    width = outs[0].shape[1]
    total = total_ref[...]
    for piece in pieces:
        total = total + piece[...].astype(f32)
    centred, inverse = norm_rows(rows_ref[aligned(at[0], part), :].astype(f32))
    scratch[...] = grad_middle_ref[...] + norm_backward(total, centred, inverse, gains[0:1, :])
    for m, out in enumerate(outs):
        out[...] = scratch[:, aligned(at[1] ^ m, width)]


def body(
    wide,
    narrow,
    inputs,
    attn_gain,
    query_key_value_weight,
    attention_out_weight,
    mlp_gain,
    feedforward_in_weight,
    feedforward_out_weight,
    grad_out,
):
    groups, columns = wide // 2, narrow // 2
    _, block, width = inputs.shape
    model = width * narrow
    depth = query_key_value_weight.shape[0]
    hidden = feedforward_out_weight.shape[0] // 2
    half, span = width // 2, 2 * width
    part = block // columns
    rows = 2 * block
    length = groups * rows
    wide_at, narrow_at = lax.axis_index("wide"), lax.axis_index("narrow")
    group, side = wide_at // 2, wide_at % 2
    column, core = narrow_at // 2, narrow_at % 2
    chips = [(k, s) for s in range(2) for k in range(columns)]

    def swap(array, mask):
        if mask == 0:
            return array
        return lax.ppermute(
            array, ("wide", "narrow"), [(i, i ^ mask) for i in range(wide * narrow)]
        )

    def over_chips(column_rel, side_rel):
        return 2 * column_rel + narrow * side_rel

    def over_groups(group_rel):
        return 2 * narrow * group_rel

    def after(array, *others):
        return lax.optimization_barrier((array, *others))[0]

    def swap_ways(array, even, odd):
        pairs = [(i, i ^ (odd if i % 2 else even)) for i in range(wide * narrow)]
        return lax.ppermute(array, ("wide", "narrow"), pairs)

    def ring_order(count):
        if count < 4:
            return list(range(count))
        quad = [0, 1 + 2 * core, 3 - 2 * core, 2]
        return [low + 4 * high for high in ring_order(count // 4) for low in quad]

    def other_way(relative):
        turned, unit = relative, 1
        while 4 * unit <= groups:
            turned, unit = turned ^ (2 * unit * ((relative // unit) % 2)), 4 * unit
        return turned

    def ring_first(array, unit):
        return swap_ways(array, unit, 3 * unit), swap_ways(array, 3 * unit, unit)

    def ring_last(second, unit):
        return swap_ways(second, unit, 3 * unit)

    def gather_ring(array, unit, count):
        if count < 4:
            return [swap(array, unit * k) for k in range(count)]
        first, second = ring_first(array, unit)
        quad = [array, first, second, ring_last(second, unit)]
        if count == 4:
            return quad
        return [q for quads in gather_ring(jnp.stack(quad), 4 * unit, count // 4) for q in quads]

    def scatter_first(pieces, unit):
        count = len(pieces)
        if count < 4:
            return pieces, None
        if count > 4:
            stacked = [jnp.stack(pieces[k : k + 4]) for k in range(0, count, 4)]
            pieces = list(scatter_ring(stacked, 4 * unit))
        own, first, second, across = pieces
        passing = swap_ways(across.astype(bf16), unit, 3 * unit)
        arrived = swap_ways(first.astype(bf16), unit, 3 * unit)
        return own, (second, passing, arrived)

    def scatter_last(own, state, unit):
        if state is None:
            total = own[0].astype(f32)
            for k in range(1, len(own)):
                total = total + swap(own[k].astype(bf16), unit * k).astype(f32)
            return total
        second, passing, arrived = state
        second = (second.astype(f32) + passing.astype(f32)).astype(bf16)
        return own.astype(f32) + arrived.astype(f32) + swap_ways(second, 3 * unit, unit).astype(f32)

    def scatter_ring(pieces, unit):
        return scatter_last(*scatter_first(pieces, unit), unit)

    def place_groups(pieces, order):
        size = pieces[0].shape[0]
        whole = jnp.zeros((size * groups, pieces[0].shape[1]), pieces[0].dtype)
        for relative, piece in zip(order, pieces):
            whole = lax.dynamic_update_slice_in_dim(whole, piece, (group ^ relative) * size, 0)
        return whole

    def fetch_side(bundle):
        received = swap(pick(bundle, 1 - side), narrow)
        return place([pick(bundle, side), received], side, 0)

    def halves(array):
        return array.reshape(depth, -1, 2, array.shape[-1] // 2).transpose(2, 0, 1, 3)

    def from_chips(array):
        return [swap(array, over_chips(k, s)) for k, s in chips]

    def to_chips(pieces):
        return [swap(piece, over_chips(k, s)) for (k, s), piece in zip(chips[1:], pieces)]

    def reduce_cores(own, other, *others):
        return own.astype(f32) + after(swap(other, 1), *others).astype(f32)

    def group_blocks(total):
        blocks = total.reshape(groups, 2 * depth, -1)
        return [pick(blocks, group ^ k) for k in ring_order(groups)]

    def reduce_side(total):
        total = total.reshape(2, depth, -1)
        kept = pick(total, side)
        received = swap(pick(total, 1 - side).astype(bf16), narrow).astype(f32)
        return place([kept[None], received[None]], side, 0)

    def join(array):
        return array.transpose(1, 2, 0, 3).reshape(depth, array.shape[2], -1)

    attn_bundle = jnp.concatenate(
        [halves(query_key_value_weight), halves(attention_out_weight.T[:, None])], axis=2
    ).reshape(2, depth, 4 * half)
    mlp_bundle = jnp.concatenate(
        [halves(feedforward_in_weight), halves(feedforward_out_weight.T[:, None])], axis=2
    ).reshape(2, depth, 3 * hidden)
    lanes = -(-3 * hidden // 128) * 128
    mlp_bundle = jnp.pad(mlp_bundle, ((0, 0), (0, 0), (0, lanes - 3 * hidden)))

    both = jnp.stack([inputs, grad_out])
    received = swap(pick(both, 1 - core, 1), 1)
    features = place([pick(both, core, 1), received], core, 2)
    unit_mask = 2 * narrow
    attn_pair = fetch_side(attn_bundle)
    features = after(features, attn_pair)
    shards = from_chips(features)
    gains = after(jnp.stack([attn_gain, mlp_gain]), shards)
    gains = place([gains, swap(gains, 1)], core, 1)
    gains = place([swap(gains, 2 * k) for k in range(columns)], column, 1)
    mlp_pair = fetch_side(after(mlp_bundle, shards))
    if groups >= 4:
        quad = [attn_pair, *ring_first(attn_pair, unit_mask)]
        quad, shards = lax.optimization_barrier((quad, shards))
        quad.append(ring_last(quad[2], unit_mask))
        if groups > 4:
            quad = [q for quads in gather_ring(jnp.stack(quad), 4 * unit_mask, groups // 4) for q in quads]
    else:
        quad = gather_ring(attn_pair, unit_mask, groups)
    mlp_pair, gains, quad = lax.optimization_barrier((mlp_pair, gains, quad))
    order = ring_order(groups)
    turned = [other_way(k) for k in order]
    count = groups if 2 * depth % 128 == 0 else 1
    starts = [group ^ k for k in order] + [group ^ k for k in turned] if count > 1 else [0, 0]

    def both_blocks(own, other):
        return [*own, *other] if count > 1 else [place_groups(own, order), place_groups(other, turned)]

    attn_weights = both_blocks(quad, [swap(piece, 1) for piece in quad])
    at = jnp.stack([column, narrow_at, *starts]).astype(jnp.int32)
    mlp_quad = [mlp_pair, *ring_first(mlp_pair, unit_mask)] if groups >= 4 else []
    token = (jnp.arange(rows) // block) ^ side
    positions = ((group * 2 + token) * block + jnp.arange(rows) % block).astype(f32)
    cosine, sine = rope_tables(positions, width)

    rows_in, grad_rows, normed_one, query, pair = call(
        functools.partial(project, chips, count),
        [((rows, model), bf16)] * 3 + [((rows, width), bf16), ((rows, span), bf16)],
        at, *shards, *attn_weights, gains, cosine, sine,
    )
    pairs = gather_ring(pair, unit_mask, groups)
    out_own = place_groups([after(piece[:, 3 * half :], pair) for piece in quad], order)
    out_own = jnp.stack(from_chips(out_own))
    early = [swap(piece, 1) for piece in mlp_quad]
    pairs, out_own, early = lax.optimization_barrier((pairs, out_own, early))
    out_other = swap(out_own, 1)
    if groups >= 4:
        mlp_quad.append(ring_last(after(mlp_quad[2], pairs), unit_mask))
    context, pairs, total = call(
        functools.partial(attend, len(pairs)),
        [((rows, width), bf16), ((length, span), bf16), ((8, rows), f32)],
        at, query, *pairs,
    )
    contexts = from_chips(context)
    if groups >= 4:
        late = after(mlp_quad.pop(), contexts)
        mlp_quad, early = [*mlp_quad, late], [*early, swap(late, 1)]
        if groups > 4:
            mlp_quad = [q for quads in gather_ring(jnp.stack(mlp_quad), 4 * unit_mask, groups // 4) for q in quads]
            early = [swap(piece, 1) for piece in mlp_quad]
    else:
        mlp_quad = gather_ring(mlp_pair, unit_mask, groups)
        early = [swap(piece, 1) for piece in mlp_quad]
    mlp_weights = both_blocks(mlp_quad, early)
    middle, middle_rows, normed_two, unit, active, mlp_gain_part, grad_two, *sends = call(
        functools.partial(feed, chips, count),
        [((block, span), f32), ((part, model), f32), ((rows, model), bf16), ((2, rows, 2 * hidden), bf16),
         ((2, rows, hidden), bf16), ((1, model), f32), ((part, model), f32)] + [((part, model), bf16)] * (len(chips) - 1),
        at, *contexts, *mlp_weights, out_own, out_other, rows_in, grad_rows, gains,
        scratch=[((rows, model), f32)],
    )
    received = to_chips(sends)
    grad_mlp_own, grad_mlp_other, branch, *branch_sends = call(
        functools.partial(settle, chips, count),
        [((model, lanes), bf16)] * 2 + [((block, span), f32)] + [((block, span), bf16)] * (len(chips) - 1),
        at, *mlp_weights, normed_two, unit, active, grad_rows, middle,
        scratch=[((rows, model), f32)],
    )
    grad_mlp_other = after(grad_mlp_other, received)
    grad_middle, grad_low = call(
        functools.partial(turn), [((part, model), f32), ((part, model), bf16)],
        at, grad_two, *received, middle_rows, grad_rows, gains,
    )
    grad_pieces = from_chips(grad_low)
    grad_mlp = reduce_cores(grad_mlp_own, grad_mlp_other, grad_low)
    mlp_state = scatter_first(group_blocks(grad_mlp), unit_mask)
    grad_attn, grad_query, grad_pairs = call(
        functools.partial(reflect, chips, count),
        [((rows, model), bf16), ((rows, width), f32), ((length, span), f32)],
        at, *grad_pieces, *attn_weights, query, pairs, total,
    )
    if groups >= 4:
        mlp_state, grad_pairs, branch_sends = lax.optimization_barrier((mlp_state, grad_pairs, branch_sends))
    grad_pairs = scatter_ring(list(grad_pairs.reshape(groups, rows, span)), unit_mask)

    branch_received = to_chips(branch_sends)
    grad_pairs, mlp_state, branch_received = lax.optimization_barrier((grad_pairs, mlp_state, branch_received))
    for piece in branch_received:
        branch = branch + piece.astype(f32)
    branch = branch.astype(bf16).reshape(block, 2, width)
    result = place([pick(branch, core, 1)[None], swap(pick(branch, 1 - core, 1), 1)[None]], core, 0)

    grad_mlp = scatter_last(*mlp_state, unit_mask)
    grad_projected, attn_gain_part, grad_one, *sends = call(
        functools.partial(unwind, chips, count),
        [((2, rows, 3 * half), bf16), ((1, model), f32), ((part, model), f32)] + [((part, model), bf16)] * (len(chips) - 1),
        at, *attn_weights, grad_query, grad_pairs, cosine, sine, rows_in,
        scratch=[((rows, model), f32)],
    )
    received = to_chips(sends)
    grad_attn_own, grad_attn_other = call(
        functools.partial(repay), [((model, 4 * half), bf16)] * 2,
        at, normed_one, grad_projected, grad_attn, context,
    )
    grad_attn_other, grad_mlp, received = lax.optimization_barrier((grad_attn_other, grad_mlp, received))
    grad_attn_weight = reduce_cores(grad_attn_own, grad_attn_other)
    grad_attn_weight_sum = grad_attn_weight
    state = scatter_first(group_blocks(grad_attn_weight), unit_mask)
    grad_one = after(grad_one, grad_attn_weight_sum)
    sends = call(
        functools.partial(finish, narrow), [((part, width), f32)] * narrow,
        at, grad_one, *received, rows_in, grad_middle, gains,
        scratch=[((part, model), f32)],
    )
    sends = [swap(piece, m) for m, piece in enumerate(sends)]
    sends, passed = lax.optimization_barrier((sends, state[1]))
    state = (state[0], passed)
    grad_mlp = after(grad_mlp, grad_attn_weight_sum)
    grad_mlp = join(reduce_side(grad_mlp)[..., : 3 * hidden].reshape(2, depth, 3, hidden))
    grad_attn_weight = scatter_last(*state, unit_mask)
    grad_attn_weight = join(reduce_side(grad_attn_weight).reshape(2, depth, 4, half))
    grad_inputs = place(
        [place([sends[2 * k + c] for k in range(columns)], column, 0)[None] for c in range(2)],
        core, 0,
    )
    gain_grads = jnp.concatenate([after(attn_gain_part, sends), mlp_gain_part], axis=0).reshape(2, narrow, width)
    gain_total = pick(gain_grads, narrow_at, 1)
    for m in range(1, narrow):
        gain_total = gain_total + swap(pick(gain_grads, narrow_at ^ m, 1), m)
    gain_total = gain_total + swap(gain_total, narrow)
    for mask in ring_masks(groups):
        gain_total = gain_total + swap(gain_total, 2 * narrow * mask)
    return (
        result,
        grad_inputs,
        gain_total[0],
        grad_attn_weight[:, :3],
        grad_attn_weight[:, 3].T,
        gain_total[1],
        grad_mlp[:, :2],
        grad_mlp[:, 2].T,
    )


def solution(mesh):
    in_specs = (
        P(None, "wide", "narrow"),
        P("narrow"),
        P("wide", None, "narrow"),
        P("narrow", "wide"),
        P("narrow"),
        P("wide", None, "narrow"),
        P("narrow", "wide"),
        P(None, "wide", "narrow"),
    )
    out_specs = (
        P(None, "wide", "narrow"),
        P(None, "wide", "narrow"),
        P("narrow"),
        P("wide", None, "narrow"),
        P("narrow", "wide"),
        P("narrow"),
        P("wide", None, "narrow"),
        P("narrow", "wide"),
    )
    step = functools.partial(body, mesh.shape["wide"], mesh.shape["narrow"])
    return jax.shard_map(step, mesh=mesh, in_specs=in_specs, out_specs=out_specs, check_vma=False)
```

```python
import functools
import math

import jax
import jax.numpy as jnp
from jax import lax
from jax.experimental import pallas as pl
from jax.experimental.pallas import tpu as pltpu
from jax.sharding import PartitionSpec as P

HEAD_DIM = 64
eps_norm = 1e-05
rope_base = 160000.0
f32 = jnp.float32
bf16 = jnp.bfloat16


def mm(a, b):
    return lax.dot_general(a, b, (((1,), (0,)), ((), ())), preferred_element_type=f32)


def mm_nt(a, b):
    return lax.dot_general(a, b, (((1,), (1,)), ((), ())), preferred_element_type=f32)


def aligned(index, size):
    return pl.ds(pl.multiple_of(index * size, size), size)


def norm_rows(rows):
    width = rows.shape[-1]
    average = jnp.sum(rows, axis=-1, keepdims=True) / width
    variance = jnp.sum(rows * rows, axis=-1, keepdims=True) / width - average * average
    inverse = lax.rsqrt(variance + eps_norm)
    return (rows - average) * inverse, inverse


def norm_backward(grad_normed, centred, inverse, gain):
    width = grad_normed.shape[-1]
    scaled = grad_normed * gain
    row_total = jnp.sum(scaled, axis=-1, keepdims=True)
    row_along = jnp.sum(scaled * centred, axis=-1, keepdims=True)
    return inverse * (scaled - row_total / width - centred * (row_along / width))


def rope_tables(positions, lanes):
    half_dim = HEAD_DIM // 2
    frequency = rope_base ** (-jnp.arange(half_dim).astype(f32) * 2.0 / HEAD_DIM)
    angles = positions[:, None] * frequency[None, :]
    angles = jnp.concatenate([angles, angles] * (lanes // HEAD_DIM), axis=-1)
    return jnp.cos(angles), jnp.sin(angles)


def rotated(tensor):
    lanes, half_dim = tensor.shape[-1], HEAD_DIM // 2
    lane = lax.broadcasted_iota(jnp.int32, tensor.shape, 1)
    up = pltpu.roll(tensor, half_dim, 1)
    down = pltpu.roll(tensor, lanes - half_dim, 1)
    return jnp.where(lane % HEAD_DIM < half_dim, -down, up)


def call(kernel, outs, at, *arrays, scratch=()):
    return pl.pallas_call(
        kernel,
        out_shape=[jax.ShapeDtypeStruct(shape, dtype) for shape, dtype in outs],
        in_specs=[pl.BlockSpec(memory_space=pltpu.SMEM)]
        + [pl.BlockSpec(memory_space=pltpu.VMEM)] * len(arrays),
        out_specs=[pl.BlockSpec(memory_space=pltpu.VMEM)] * len(outs),
        scratch_shapes=[pltpu.VMEM(shape, dtype) for shape, dtype in scratch],
        compiler_params=pltpu.CompilerParams(vmem_limit_bytes=60 * 1024 * 1024),
        name=kernel.func.__name__,
    )(at, *arrays)


def ring_masks(count):
    masks, unit = [], 1
    while unit < count:
        masks += [unit] + ([3 * unit] if 4 * unit <= count else [])
        unit *= 4
    return masks


def pick(array, index, axis=0):
    return lax.dynamic_index_in_dim(array, index, axis=axis, keepdims=False)


def place(pieces, own, axis):
    count = len(pieces)
    if count == 1:
        return pieces[0]
    if count == 2:
        return jnp.where(
            own == 0,
            jnp.concatenate(pieces, axis=axis),
            jnp.concatenate(pieces[::-1], axis=axis),
        )
    size = pieces[0].shape[axis]
    shape = list(pieces[0].shape)
    shape[axis] = size * count
    whole = jnp.zeros(shape, pieces[0].dtype)
    for relative, piece in enumerate(pieces):
        whole = lax.dynamic_update_slice_in_dim(whole, piece, (own ^ relative) * size, axis)
    return whole


def contract(rows_ref, pieces, starts, lanes):
    total = 0.0
    for piece, start in zip(pieces, starts):
        total = total + mm(rows_ref[:, aligned(start, piece.shape[0])], piece[:, lanes])
    return total


def spread(out_ref, array, pieces, starts, lanes):
    for piece, start in zip(pieces, starts):
        out_ref[:, aligned(start, piece.shape[0])] += mm_nt(array, piece[:, lanes])


def both_cores(count, at, refs):
    first = [at[2 + p] for p in range(count)]
    second = [at[2 + count + p] for p in range(count)]
    return ((refs[:count], first), (refs[count : 2 * count], second)), refs[2 * count :]


def project(chips, count, at, *refs):
    shards, refs = refs[: len(chips)], refs[len(chips) :]
    weights, refs = both_cores(count, at, refs)
    gains, cosine, sine, rows_ref, grad_ref, normed_ref, query_ref, pair_ref = refs
    block, span = shards[0].shape[1:]
    half = query_ref.shape[1] // 2
    for (k, s), shard in zip(chips, shards):
        lanes = aligned(at[0] ^ k, span)
        rows_ref[s * block : (s + 1) * block, lanes] = shard[0]
        grad_ref[s * block : (s + 1) * block, lanes] = shard[1]
    centred, _ = norm_rows(rows_ref[...].astype(f32))
    normed_ref[...] = (centred * gains[0:1, :]).astype(bf16)
    queries, keys, values = [], [], []
    for pieces, starts in weights:
        projected = contract(normed_ref, pieces, starts, slice(0, 3 * half))
        queries.append(projected[:, :half])
        keys.append(projected[:, half : 2 * half])
        values.append(projected[:, 2 * half :])
    query, key = jnp.concatenate(queries, axis=1), jnp.concatenate(keys, axis=1)
    cosine, sine = cosine[...], sine[...]
    query = (query * cosine + rotated(query) * sine).astype(bf16)
    key = (key * cosine + rotated(key) * sine).astype(bf16)
    query_ref[...] = query * jnp.asarray(HEAD_DIM**-0.5, bf16)
    pair_ref[:, : 2 * half] = key
    pair_ref[:, 2 * half :] = jnp.concatenate(values, axis=1).astype(bf16)


def attend(parts, at, query_ref, *refs):
    pieces, (context_ref, pairs_ref, total_ref) = refs[:parts], refs[parts:]
    start = 0
    for piece in pieces:
        pairs_ref[start : start + piece.shape[0], :] = piece[...]
        start += piece.shape[0]
    width = query_ref.shape[1]
    values = pairs_ref[:, width:].T
    contexts = []
    for h in range(width // HEAD_DIM):
        lanes = slice(h * HEAD_DIM, (h + 1) * HEAD_DIM)
        scores = mm_nt(pairs_ref[:, lanes], query_ref[:, lanes])
        peak = jnp.max(scores, axis=0, keepdims=True)
        log_total = peak + jnp.log(jnp.sum(jnp.exp(scores - peak), axis=0, keepdims=True))
        probs = jnp.exp(scores - log_total).astype(bf16)
        contexts.append(mm(values[lanes], probs))
        total_ref[h : h + 1, :] = log_total
    context_ref[...] = jnp.concatenate(contexts, axis=0).T.astype(bf16)


def feed(chips, count, at, *refs):
    contexts, refs = refs[: len(chips)], refs[len(chips) :]
    weights, refs = both_cores(count, at, refs)
    (out_own, out_other, rows_ref, grad_ref, gains), refs = refs[:5], refs[5:]
    (middle_ref, middle_rows_ref, normed_ref, unit_ref, active_ref, gain_ref, total_ref), refs = refs[:7], refs[7:]
    pieces, scratch = refs[:-1], refs[-1]
    hidden = active_ref.shape[2]
    block, span = middle_ref.shape
    part = total_ref.shape[0]
    middle = rows_ref[...].astype(f32)
    for p, (k, s) in enumerate(chips):
        context = contexts[p][...]
        if s:
            context = jnp.concatenate([context[block:], context[:block]], axis=0)
        middle = middle + mm_nt(context, jnp.concatenate([out_own[p], out_other[p]], axis=1))
    scratch[...] = middle
    middle_ref[...] = scratch[:block, aligned(at[0], span)]
    middle_rows_ref[...] = scratch[aligned(at[0], part), :]
    centred, _ = norm_rows(middle)
    normed_ref[...] = (centred * gains[1:2, :]).astype(bf16)
    scratch[...] = jnp.zeros_like(scratch)
    for b, (weight, starts) in enumerate(weights):
        gate_up = contract(normed_ref, weight, starts, slice(0, 2 * hidden))
        gate, lift = gate_up[:, :hidden], gate_up[:, hidden:]
        share = 0.5 + 0.5 * lax.erf(gate * math.sqrt(0.5))
        bent = gate * share
        active_ref[b] = (bent * lift).astype(bf16)
        slope = share + gate * jnp.exp(-0.5 * gate * gate) * (1.0 / math.sqrt(2.0 * math.pi))
        back = contract(grad_ref, weight, starts, slice(2 * hidden, 3 * hidden))
        unit = jnp.concatenate([back * lift * slope, back * bent], axis=1).astype(bf16)
        unit_ref[b] = unit
        spread(scratch, unit, weight, starts, slice(0, 2 * hidden))
    gain_ref[...] = jnp.sum(scratch[...] * centred, axis=0, keepdims=True)
    cut_rows(chips, at, scratch, total_ref, pieces)


def cut_rows(chips, at, scratch, total_ref, pieces):
    part = total_ref.shape[0]
    columns = scratch.shape[0] // (2 * part)
    for p, (k, s) in enumerate(chips):
        rows = scratch[aligned(s * columns + (at[0] ^ k), part), :]
        if p:
            pieces[p - 1][...] = rows.astype(bf16)
        else:
            total_ref[...] = rows


def turn(at, total_ref, *refs):
    pieces, (middle_ref, grad_ref, gains, grad_middle_ref, low_ref) = refs[:-5], refs[-5:]
    part = total_ref.shape[0]
    total = total_ref[...]
    for piece in pieces:
        total = total + piece[...].astype(f32)
    centred, inverse = norm_rows(middle_ref[...])
    grad = grad_ref[aligned(at[0], part), :].astype(f32)
    grad = grad + norm_backward(total, centred, inverse, gains[1:2, :])
    grad_middle_ref[...] = grad
    low_ref[...] = grad.astype(bf16)


def settle(chips, count, at, *refs):
    weights, refs = both_cores(count, at, refs)
    (normed_ref, unit_ref, active_ref, grad_ref, middle_ref), refs = refs[:5], refs[5:]
    (own_ref, other_ref, total_ref), refs = refs[:3], refs[3:]
    pieces, scratch = refs[:-1], refs[-1]
    hidden = active_ref.shape[2]
    block, span = total_ref.shape
    normed, grad = normed_ref[...].T, grad_ref[...].T
    for b, out in enumerate((other_ref, own_ref)):
        out[:, : 2 * hidden] = mm(normed, unit_ref[1 - b]).astype(bf16)
        out[:, 2 * hidden : 3 * hidden] = mm(grad, active_ref[1 - b]).astype(bf16)
        if out.shape[1] > 3 * hidden:
            out[:, 3 * hidden :] = jnp.zeros((out.shape[0], out.shape[1] - 3 * hidden), bf16)
    scratch[...] = jnp.zeros_like(scratch)
    for b, (weight, starts) in enumerate(weights):
        spread(scratch, active_ref[b], weight, starts, slice(2 * hidden, 3 * hidden))
    for p, (k, s) in enumerate(chips):
        piece = scratch[s * block : (s + 1) * block, aligned(at[0] ^ k, span)]
        if p:
            pieces[p - 1][...] = piece.astype(bf16)
        else:
            total_ref[...] = piece + middle_ref[...]


def reflect(chips, count, at, *refs):
    pieces, refs = refs[: len(chips)], refs[len(chips) :]
    weights, refs = both_cores(count, at, refs)
    query_ref, pairs_ref, total_ref, grad_attn_ref, grad_query_ref, grad_pairs_ref = refs
    part = pieces[0].shape[0]
    rows, width = query_ref.shape
    columns = rows // (2 * part)
    half = width // 2
    for (k, s), piece in zip(chips, pieces):
        grad_attn_ref[aligned(s * columns + (at[0] ^ k), part), :] = piece[...]
    grad_context = jnp.concatenate(
        [contract(grad_attn_ref, weight, starts, slice(3 * half, 4 * half)) for weight, starts in weights],
        axis=1,
    ).astype(bf16)
    keys = pairs_ref[:, :width].T
    grad_queries = []
    for h in range(width // HEAD_DIM):
        lanes = slice(h * HEAD_DIM, (h + 1) * HEAD_DIM)
        query = query_ref[:, lanes]
        grad = grad_context[:, lanes]
        probs = jnp.exp(mm_nt(pairs_ref[:, lanes], query) - total_ref[h : h + 1, :])
        value_lanes = slice(width + h * HEAD_DIM, width + (h + 1) * HEAD_DIM)
        grad_probs = mm_nt(pairs_ref[:, value_lanes], grad)
        delta = jnp.sum(probs * grad_probs, axis=0, keepdims=True)
        grad_scores = (probs * (grad_probs - delta)).astype(bf16)
        grad_pairs_ref[:, lanes] = mm(grad_scores, query)
        grad_pairs_ref[:, value_lanes] = mm(probs.astype(bf16), grad)
        grad_queries.append(mm(keys[lanes], grad_scores))
    grad_query_ref[...] = jnp.concatenate(grad_queries, axis=0).T * HEAD_DIM**-0.5


def unwind(chips, count, at, *refs):
    weights, refs = both_cores(count, at, refs)
    (grad_query_ref, grad_pairs_ref, cosine, sine, rows_ref), refs = refs[:5], refs[5:]
    (grad_projected_ref, gain_ref, total_ref), refs = refs[:3], refs[3:]
    pieces, scratch = refs[:-1], refs[-1]
    width = grad_query_ref.shape[1]
    half = width // 2
    cosine, sine = cosine[...], sine[...]
    grad_query, grad_key = grad_query_ref[...], grad_pairs_ref[:, :width]
    grad_query = (grad_query * cosine - rotated(grad_query * sine)).astype(bf16)
    grad_key = (grad_key * cosine - rotated(grad_key * sine)).astype(bf16)
    grad_value = grad_pairs_ref[:, width:].astype(bf16)
    scratch[...] = jnp.zeros_like(scratch)
    for b, (weight, starts) in enumerate(weights):
        lanes = slice(b * half, (b + 1) * half)
        grad = jnp.concatenate([grad_query[:, lanes], grad_key[:, lanes], grad_value[:, lanes]], axis=1)
        grad_projected_ref[b] = grad
        spread(scratch, grad, weight, starts, slice(0, 3 * half))
    centred, _ = norm_rows(rows_ref[...].astype(f32))
    gain_ref[...] = jnp.sum(scratch[...] * centred, axis=0, keepdims=True)
    cut_rows(chips, at, scratch, total_ref, pieces)


def repay(at, normed_ref, grad_projected_ref, grad_attn_ref, context_ref, own_ref, other_ref):
    half = context_ref.shape[1] // 2
    normed, grad_attn = normed_ref[...].T, grad_attn_ref[...].T
    for b, out in ((1, other_ref), (0, own_ref)):
        out[:, : 3 * half] = mm(normed, grad_projected_ref[b]).astype(bf16)
        out[:, 3 * half :] = mm(grad_attn, context_ref[:, b * half : (b + 1) * half]).astype(bf16)


def finish(narrow, at, total_ref, *refs):
    pieces, (rows_ref, grad_middle_ref, gains), outs, scratch = refs[: -narrow - 4], refs[-narrow - 4 : -narrow - 1], refs[-narrow - 1 : -1], refs[-1]
    part = total_ref.shape[0]
    width = outs[0].shape[1]
    total = total_ref[...]
    for piece in pieces:
        total = total + piece[...].astype(f32)
    centred, inverse = norm_rows(rows_ref[aligned(at[0], part), :].astype(f32))
    scratch[...] = grad_middle_ref[...] + norm_backward(total, centred, inverse, gains[0:1, :])
    for m, out in enumerate(outs):
        out[...] = scratch[:, aligned(at[1] ^ m, width)]


def body(
    wide,
    narrow,
    inputs,
    attn_gain,
    query_key_value_weight,
    attention_out_weight,
    mlp_gain,
    feedforward_in_weight,
    feedforward_out_weight,
    grad_out,
):
    groups, columns = wide // 2, narrow // 2
    _, block, width = inputs.shape
    model = width * narrow
    depth = query_key_value_weight.shape[0]
    hidden = feedforward_out_weight.shape[0] // 2
    half, span = width // 2, 2 * width
    part = block // columns
    rows = 2 * block
    length = groups * rows
    wide_at, narrow_at = lax.axis_index("wide"), lax.axis_index("narrow")
    group, side = wide_at // 2, wide_at % 2
    column, core = narrow_at // 2, narrow_at % 2
    chips = [(k, s) for s in range(2) for k in range(columns)]

    def swap(array, mask):
        if mask == 0:
            return array
        return lax.ppermute(
            array, ("wide", "narrow"), [(i, i ^ mask) for i in range(wide * narrow)]
        )

    def over_chips(column_rel, side_rel):
        return 2 * column_rel + narrow * side_rel

    def over_groups(group_rel):
        return 2 * narrow * group_rel

    def after(array, *others):
        return lax.optimization_barrier((array, *others))[0]

    def swap_ways(array, even, odd):
        pairs = [(i, i ^ (odd if i % 2 else even)) for i in range(wide * narrow)]
        return lax.ppermute(array, ("wide", "narrow"), pairs)

    def ring_order(count):
        if count < 4:
            return list(range(count))
        quad = [0, 1 + 2 * core, 3 - 2 * core, 2]
        return [low + 4 * high for high in ring_order(count // 4) for low in quad]

    def other_way(relative):
        turned, unit = relative, 1
        while 4 * unit <= groups:
            turned, unit = turned ^ (2 * unit * ((relative // unit) % 2)), 4 * unit
        return turned

    def ring_first(array, unit):
        return swap_ways(array, unit, 3 * unit), swap_ways(array, 3 * unit, unit)

    def ring_last(second, unit):
        return swap_ways(second, unit, 3 * unit)

    def gather_ring(array, unit, count):
        if count < 4:
            return [swap(array, unit * k) for k in range(count)]
        first, second = ring_first(array, unit)
        quad = [array, first, second, ring_last(second, unit)]
        if count == 4:
            return quad
        return [q for quads in gather_ring(jnp.stack(quad), 4 * unit, count // 4) for q in quads]

    def scatter_first(pieces, unit):
        count = len(pieces)
        if count < 4:
            return pieces, None
        if count > 4:
            stacked = [jnp.stack(pieces[k : k + 4]) for k in range(0, count, 4)]
            pieces = list(scatter_ring(stacked, 4 * unit))
        own, first, second, across = pieces
        passing = swap_ways(across.astype(bf16), unit, 3 * unit)
        arrived = swap_ways(first.astype(bf16), unit, 3 * unit)
        return own, (second, passing, arrived)

    def scatter_last(own, state, unit):
        if state is None:
            total = own[0].astype(f32)
            for k in range(1, len(own)):
                total = total + swap(own[k].astype(bf16), unit * k).astype(f32)
            return total
        second, passing, arrived = state
        second = (second.astype(f32) + passing.astype(f32)).astype(bf16)
        return own.astype(f32) + arrived.astype(f32) + swap_ways(second, 3 * unit, unit).astype(f32)

    def scatter_ring(pieces, unit):
        return scatter_last(*scatter_first(pieces, unit), unit)

    def place_groups(pieces, order):
        size = pieces[0].shape[0]
        whole = jnp.zeros((size * groups, pieces[0].shape[1]), pieces[0].dtype)
        for relative, piece in zip(order, pieces):
            whole = lax.dynamic_update_slice_in_dim(whole, piece, (group ^ relative) * size, 0)
        return whole

    def fetch_side(bundle):
        received = swap(pick(bundle, 1 - side), narrow)
        return place([pick(bundle, side), received], side, 0)

    def halves(array):
        return array.reshape(depth, -1, 2, array.shape[-1] // 2).transpose(2, 0, 1, 3)

    def from_chips(array):
        return [swap(array, over_chips(k, s)) for k, s in chips]

    def to_chips(pieces):
        return [swap(piece, over_chips(k, s)) for (k, s), piece in zip(chips[1:], pieces)]

    def reduce_cores(own, other, *others):
        blocks = own.reshape(groups, 2 * depth, -1)
        received = after(swap(other, 1), *others).reshape(groups, 2 * depth, -1)
        return [
            pick(blocks, group ^ k).astype(f32) + pick(received, group ^ k).astype(f32)
            for k in ring_order(groups)
        ]

    def reduce_side(total):
        total = total.reshape(2, depth, -1)
        kept = pick(total, side)
        received = swap(pick(total, 1 - side).astype(bf16), narrow).astype(f32)
        return place([kept[None], received[None]], side, 0)

    def join(array):
        return array.transpose(1, 2, 0, 3).reshape(depth, array.shape[2], -1)

    attn_bundle = jnp.concatenate(
        [halves(query_key_value_weight), halves(attention_out_weight.T[:, None])], axis=2
    ).reshape(2, depth, 4 * half)
    mlp_bundle = jnp.concatenate(
        [halves(feedforward_in_weight), halves(feedforward_out_weight.T[:, None])], axis=2
    ).reshape(2, depth, 3 * hidden)
    lanes = -(-3 * hidden // 128) * 128
    mlp_bundle = jnp.pad(mlp_bundle, ((0, 0), (0, 0), (0, lanes - 3 * hidden)))

    both = jnp.stack([inputs, grad_out])
    received = swap(pick(both, 1 - core, 1), 1)
    features = place([pick(both, core, 1), received], core, 2)
    unit_mask = 2 * narrow
    attn_pair = fetch_side(attn_bundle)
    shards = from_chips(features)
    gains = after(jnp.stack([attn_gain, mlp_gain]), shards)
    gains = place([gains, swap(gains, 1)], core, 1)
    gains = place([swap(gains, 2 * k) for k in range(columns)], column, 1)
    mlp_pair = fetch_side(after(mlp_bundle, shards))
    if groups >= 4:
        quad = [attn_pair, *ring_first(attn_pair, unit_mask)]
        quad, shards = lax.optimization_barrier((quad, shards))
        quad.append(ring_last(quad[2], unit_mask))
        if groups > 4:
            quad = [q for quads in gather_ring(jnp.stack(quad), 4 * unit_mask, groups // 4) for q in quads]
    else:
        quad = gather_ring(attn_pair, unit_mask, groups)
    order = ring_order(groups)
    turned = [other_way(k) for k in order]
    count = groups if 2 * depth % 128 == 0 else 1
    starts = [group ^ k for k in order] + [group ^ k for k in turned] if count > 1 else [0, 0]

    def both_blocks(own, other):
        return [*own, *other] if count > 1 else [place_groups(own, order), place_groups(other, turned)]

    token = (jnp.arange(rows) // block) ^ side
    positions = ((group * 2 + token) * block + jnp.arange(rows) % block).astype(f32)
    cosine, sine = rope_tables(positions, width)
    at = jnp.stack([column, narrow_at, *starts]).astype(jnp.int32)
    early = [swap(piece, 1) for piece in quad[:3]]
    mlp_pair, gains, quad, early, cosine, sine, at = lax.optimization_barrier(
        (mlp_pair, gains, quad, early, cosine, sine, at)
    )
    attn_weights = both_blocks(quad, [*early, *[swap(piece, 1) for piece in quad[len(early) :]]])
    mlp_quad = [mlp_pair, *ring_first(mlp_pair, unit_mask)] if groups >= 4 else []

    rows_in, grad_rows, normed_one, query, pair = call(
        functools.partial(project, chips, count),
        [((rows, model), bf16)] * 3 + [((rows, width), bf16), ((rows, span), bf16)],
        at, *shards, *attn_weights, gains, cosine, sine,
    )
    pairs = gather_ring(pair, unit_mask, groups)
    out_own = place_groups([after(piece[:, 3 * half :], pair) for piece in quad], order)
    out_own = jnp.stack(from_chips(out_own))
    early = [swap(piece, 1) for piece in mlp_quad]
    pairs, out_own, early = lax.optimization_barrier((pairs, out_own, early))
    out_other = swap(out_own, 1)
    if groups >= 4:
        mlp_quad.append(ring_last(after(mlp_quad[2], pairs), unit_mask))
    context, pairs, total = call(
        functools.partial(attend, len(pairs)),
        [((rows, width), bf16), ((length, span), bf16), ((8, rows), f32)],
        at, query, *pairs,
    )
    contexts = from_chips(context)
    if groups >= 4:
        late = after(mlp_quad.pop(), contexts)
        mlp_quad, early = [*mlp_quad, late], [*early, swap(late, 1)]
        if groups > 4:
            mlp_quad = [q for quads in gather_ring(jnp.stack(mlp_quad), 4 * unit_mask, groups // 4) for q in quads]
            early = [swap(piece, 1) for piece in mlp_quad]
    else:
        mlp_quad = gather_ring(mlp_pair, unit_mask, groups)
        early = [swap(piece, 1) for piece in mlp_quad]
    mlp_weights = both_blocks(mlp_quad, early)
    middle, middle_rows, normed_two, unit, active, mlp_gain_part, grad_two, *sends = call(
        functools.partial(feed, chips, count),
        [((block, span), f32), ((part, model), f32), ((rows, model), bf16), ((2, rows, 2 * hidden), bf16),
         ((2, rows, hidden), bf16), ((1, model), f32), ((part, model), f32)] + [((part, model), bf16)] * (len(chips) - 1),
        at, *contexts, *mlp_weights, out_own, out_other, rows_in, grad_rows, gains,
        scratch=[((rows, model), f32)],
    )
    received = to_chips(sends)
    grad_mlp_own, grad_mlp_other, branch, *branch_sends = call(
        functools.partial(settle, chips, count),
        [((model, lanes), bf16)] * 2 + [((block, span), f32)] + [((block, span), bf16)] * (len(chips) - 1),
        at, *mlp_weights, normed_two, unit, active, grad_rows, middle,
        scratch=[((rows, model), f32)],
    )
    grad_mlp_other = after(grad_mlp_other, received)
    grad_middle, grad_low = call(
        functools.partial(turn), [((part, model), f32), ((part, model), bf16)],
        at, grad_two, *received, middle_rows, grad_rows, gains,
    )
    grad_pieces = from_chips(grad_low)
    grad_mlp = reduce_cores(grad_mlp_own, grad_mlp_other, grad_low)
    mlp_state = scatter_first(grad_mlp, unit_mask)
    grad_attn, grad_query, grad_pairs = call(
        functools.partial(reflect, chips, count),
        [((rows, model), bf16), ((rows, width), f32), ((length, span), f32)],
        at, *grad_pieces, *attn_weights, query, pairs, total,
    )
    if groups >= 4:
        mlp_state, grad_pairs, branch_sends = lax.optimization_barrier((mlp_state, grad_pairs, branch_sends))
    grad_pairs = scatter_ring(list(grad_pairs.reshape(groups, rows, span)), unit_mask)

    branch_received = to_chips(branch_sends)
    grad_pairs, mlp_state, branch_received = lax.optimization_barrier((grad_pairs, mlp_state, branch_received))
    for piece in branch_received:
        branch = branch + piece.astype(f32)
    branch = branch.astype(bf16).reshape(block, 2, width)
    result = place([pick(branch, core, 1)[None], swap(pick(branch, 1 - core, 1), 1)[None]], core, 0)

    grad_mlp = scatter_last(*mlp_state, unit_mask)
    grad_projected, attn_gain_part, grad_one, *sends = call(
        functools.partial(unwind, chips, count),
        [((2, rows, 3 * half), bf16), ((1, model), f32), ((part, model), f32)] + [((part, model), bf16)] * (len(chips) - 1),
        at, *attn_weights, grad_query, grad_pairs, cosine, sine, rows_in,
        scratch=[((rows, model), f32)],
    )
    received = to_chips(sends)
    grad_attn_own, grad_attn_other = call(
        functools.partial(repay), [((model, 4 * half), bf16)] * 2,
        at, normed_one, grad_projected, grad_attn, context,
    )
    gain_grads = jnp.concatenate([after(attn_gain_part, grad_attn_own), mlp_gain_part], axis=0).reshape(2, narrow, width)
    gain_total = pick(gain_grads, narrow_at, 1)
    for m in range(1, narrow):
        gain_total = gain_total + swap(pick(gain_grads, narrow_at ^ m, 1), m)
    grad_attn_other, grad_mlp, received, gain_total = lax.optimization_barrier(
        (grad_attn_other, grad_mlp, received, gain_total)
    )
    grad_attn_weight = reduce_cores(grad_attn_own, grad_attn_other)
    grad_attn_weight_sum = [piece.astype(bf16) for piece in grad_attn_weight[1::2]]
    state = scatter_first(grad_attn_weight, unit_mask)
    grad_one = after(grad_one, *grad_attn_weight_sum)
    sends = call(
        functools.partial(finish, narrow), [((part, width), f32)] * narrow,
        at, grad_one, *received, rows_in, grad_middle, gains,
        scratch=[((part, model), f32)],
    )
    sends = [swap(piece, m) for m, piece in enumerate(sends)]
    gain_total = after(gain_total, *grad_attn_weight_sum)
    gain_total = gain_total + swap(gain_total, narrow)
    for mask in ring_masks(groups):
        gain_total = gain_total + swap(gain_total, 2 * narrow * mask)
    sends, passed, gain_total = lax.optimization_barrier((sends, state[1], gain_total))
    state = (state[0], passed)
    grad_mlp = after(grad_mlp, *grad_attn_weight_sum)
    grad_mlp = join(reduce_side(grad_mlp)[..., : 3 * hidden].reshape(2, depth, 3, hidden))
    grad_attn_weight = scatter_last(*state, unit_mask)
    grad_attn_weight = join(reduce_side(grad_attn_weight).reshape(2, depth, 4, half))
    grad_inputs = place(
        [place([sends[2 * k + c] for k in range(columns)], column, 0)[None] for c in range(2)],
        core, 0,
    )
    return (
        result,
        grad_inputs,
        gain_total[0],
        grad_attn_weight[:, :3],
        grad_attn_weight[:, 3].T,
        gain_total[1],
        grad_mlp[:, :2],
        grad_mlp[:, 2].T,
    )


def solution(mesh):
    in_specs = (
        P(None, "wide", "narrow"),
        P("narrow"),
        P("wide", None, "narrow"),
        P("narrow", "wide"),
        P("narrow"),
        P("wide", None, "narrow"),
        P("narrow", "wide"),
        P(None, "wide", "narrow"),
    )
    out_specs = (
        P(None, "wide", "narrow"),
        P(None, "wide", "narrow"),
        P("narrow"),
        P("wide", None, "narrow"),
        P("narrow", "wide"),
        P("narrow"),
        P("wide", None, "narrow"),
        P("narrow", "wide"),
    )
    step = functools.partial(body, mesh.shape["wide"], mesh.shape["narrow"])
    return jax.shard_map(step, mesh=mesh, in_specs=in_specs, out_specs=out_specs, check_vma=False)
```

```python
import functools
import math

import jax
import jax.numpy as jnp
from jax import lax
from jax.experimental import pallas as pl
from jax.experimental.pallas import tpu as pltpu
from jax.sharding import PartitionSpec as P

HEAD_DIM = 64
eps_norm = 1e-05
rope_base = 160000.0
f32 = jnp.float32
bf16 = jnp.bfloat16


def mm(a, b):
    return lax.dot_general(a, b, (((1,), (0,)), ((), ())), preferred_element_type=f32)


def mm_nt(a, b):
    return lax.dot_general(a, b, (((1,), (1,)), ((), ())), preferred_element_type=f32)


def aligned(index, size):
    return pl.ds(pl.multiple_of(index * size, size), size)


def norm_rows(rows):
    width = rows.shape[-1]
    average = jnp.sum(rows, axis=-1, keepdims=True) / width
    variance = jnp.sum(rows * rows, axis=-1, keepdims=True) / width - average * average
    inverse = lax.rsqrt(variance + eps_norm)
    return (rows - average) * inverse, inverse


def norm_backward(grad_normed, centred, inverse, gain):
    width = grad_normed.shape[-1]
    scaled = grad_normed * gain
    row_total = jnp.sum(scaled, axis=-1, keepdims=True)
    row_along = jnp.sum(scaled * centred, axis=-1, keepdims=True)
    return inverse * (scaled - row_total / width - centred * (row_along / width))


def rope_tables(positions, lanes):
    half_dim = HEAD_DIM // 2
    frequency = rope_base ** (-jnp.arange(half_dim).astype(f32) * 2.0 / HEAD_DIM)
    angles = positions[:, None] * frequency[None, :]
    angles = jnp.concatenate([angles, angles] * (lanes // HEAD_DIM), axis=-1)
    return jnp.cos(angles), jnp.sin(angles)


def rotated(tensor):
    lanes, half_dim = tensor.shape[-1], HEAD_DIM // 2
    lane = lax.broadcasted_iota(jnp.int32, tensor.shape, 1)
    up = pltpu.roll(tensor, half_dim, 1)
    down = pltpu.roll(tensor, lanes - half_dim, 1)
    return jnp.where(lane % HEAD_DIM < half_dim, -down, up)


def call(kernel, outs, at, *arrays, scratch=()):
    return pl.pallas_call(
        kernel,
        out_shape=[jax.ShapeDtypeStruct(shape, dtype) for shape, dtype in outs],
        in_specs=[pl.BlockSpec(memory_space=pltpu.SMEM)]
        + [pl.BlockSpec(memory_space=pltpu.VMEM)] * len(arrays),
        out_specs=[pl.BlockSpec(memory_space=pltpu.VMEM)] * len(outs),
        scratch_shapes=[pltpu.VMEM(shape, dtype) for shape, dtype in scratch],
        compiler_params=pltpu.CompilerParams(vmem_limit_bytes=60 * 1024 * 1024),
        name=kernel.func.__name__,
    )(at, *arrays)


def ring_masks(count):
    masks, unit = [], 1
    while unit < count:
        masks += [unit] + ([3 * unit] if 4 * unit <= count else [])
        unit *= 4
    return masks


def pick(array, index, axis=0):
    return lax.dynamic_index_in_dim(array, index, axis=axis, keepdims=False)


def place(pieces, own, axis):
    count = len(pieces)
    if count == 1:
        return pieces[0]
    if count == 2:
        return jnp.where(
            own == 0,
            jnp.concatenate(pieces, axis=axis),
            jnp.concatenate(pieces[::-1], axis=axis),
        )
    size = pieces[0].shape[axis]
    shape = list(pieces[0].shape)
    shape[axis] = size * count
    whole = jnp.zeros(shape, pieces[0].dtype)
    for relative, piece in enumerate(pieces):
        whole = lax.dynamic_update_slice_in_dim(whole, piece, (own ^ relative) * size, axis)
    return whole


def contract(rows_ref, pieces, starts, lanes):
    total = 0.0
    for piece, start in zip(pieces, starts):
        total = total + mm(rows_ref[:, aligned(start, piece.shape[0])], piece[:, lanes])
    return total


def spread(out_ref, array, pieces, starts, lanes):
    for piece, start in zip(pieces, starts):
        out_ref[:, aligned(start, piece.shape[0])] += mm_nt(array, piece[:, lanes])


def both_cores(count, at, refs):
    first = [at[2 + p] for p in range(count)]
    second = [at[2 + count + p] for p in range(count)]
    return ((refs[:count], first), (refs[count : 2 * count], second)), refs[2 * count :]


def project(chips, count, at, *refs):
    shards, refs = refs[: len(chips)], refs[len(chips) :]
    weights, refs = both_cores(count, at, refs)
    gains, cosine, sine, rows_ref, grad_ref, normed_ref, query_ref, pair_ref = refs
    block, span = shards[0].shape[1:]
    half = query_ref.shape[1] // 2
    for (k, s), shard in zip(chips, shards):
        lanes = aligned(at[0] ^ k, span)
        rows_ref[s * block : (s + 1) * block, lanes] = shard[0]
        grad_ref[s * block : (s + 1) * block, lanes] = shard[1]
    centred, _ = norm_rows(rows_ref[...].astype(f32))
    normed_ref[...] = (centred * gains[0:1, :]).astype(bf16)
    queries, keys, values = [], [], []
    for pieces, starts in weights:
        projected = contract(normed_ref, pieces, starts, slice(0, 3 * half))
        queries.append(projected[:, :half])
        keys.append(projected[:, half : 2 * half])
        values.append(projected[:, 2 * half :])
    query, key = jnp.concatenate(queries, axis=1), jnp.concatenate(keys, axis=1)
    cosine, sine = cosine[...], sine[...]
    query = (query * cosine + rotated(query) * sine).astype(bf16)
    key = (key * cosine + rotated(key) * sine).astype(bf16)
    query_ref[...] = query * jnp.asarray(HEAD_DIM**-0.5, bf16)
    pair_ref[:, : 2 * half] = key
    pair_ref[:, 2 * half :] = jnp.concatenate(values, axis=1).astype(bf16)


def attend(parts, at, query_ref, *refs):
    pieces, (context_ref, pairs_ref, total_ref) = refs[:parts], refs[parts:]
    start = 0
    for piece in pieces:
        pairs_ref[start : start + piece.shape[0], :] = piece[...]
        start += piece.shape[0]
    width = query_ref.shape[1]
    values = pairs_ref[:, width:].T
    contexts = []
    for h in range(width // HEAD_DIM):
        lanes = slice(h * HEAD_DIM, (h + 1) * HEAD_DIM)
        scores = mm_nt(pairs_ref[:, lanes], query_ref[:, lanes])
        peak = jnp.max(scores, axis=0, keepdims=True)
        log_total = peak + jnp.log(jnp.sum(jnp.exp(scores - peak), axis=0, keepdims=True))
        probs = jnp.exp(scores - log_total).astype(bf16)
        contexts.append(mm(values[lanes], probs))
        total_ref[h : h + 1, :] = log_total
    context_ref[...] = jnp.concatenate(contexts, axis=0).T.astype(bf16)


def feed(chips, count, at, *refs):
    contexts, refs = refs[: len(chips)], refs[len(chips) :]
    weights, refs = both_cores(count, at, refs)
    (out_own, out_other, rows_ref, grad_ref, gains), refs = refs[:5], refs[5:]
    (middle_ref, middle_rows_ref, normed_ref, unit_ref, active_ref, gain_ref, total_ref), refs = refs[:7], refs[7:]
    pieces, scratch = refs[:-1], refs[-1]
    hidden = active_ref.shape[2]
    block, span = middle_ref.shape
    part = total_ref.shape[0]
    middle = rows_ref[...].astype(f32)
    for p, (k, s) in enumerate(chips):
        context = contexts[p][...]
        if s:
            context = jnp.concatenate([context[block:], context[:block]], axis=0)
        middle = middle + mm_nt(context, jnp.concatenate([out_own[p], out_other[p]], axis=1))
    scratch[...] = middle
    middle_ref[...] = scratch[:block, aligned(at[0], span)]
    middle_rows_ref[...] = scratch[aligned(at[0], part), :]
    centred, _ = norm_rows(middle)
    normed_ref[...] = (centred * gains[1:2, :]).astype(bf16)
    scratch[...] = jnp.zeros_like(scratch)
    for b, (weight, starts) in enumerate(weights):
        gate_up = contract(normed_ref, weight, starts, slice(0, 2 * hidden))
        gate, lift = gate_up[:, :hidden], gate_up[:, hidden:]
        share = 0.5 + 0.5 * lax.erf(gate * math.sqrt(0.5))
        bent = gate * share
        active_ref[b] = (bent * lift).astype(bf16)
        slope = share + gate * jnp.exp(-0.5 * gate * gate) * (1.0 / math.sqrt(2.0 * math.pi))
        back = contract(grad_ref, weight, starts, slice(2 * hidden, 3 * hidden))
        unit = jnp.concatenate([back * lift * slope, back * bent], axis=1).astype(bf16)
        unit_ref[b] = unit
        spread(scratch, unit, weight, starts, slice(0, 2 * hidden))
    gain_ref[...] = jnp.sum(scratch[...] * centred, axis=0, keepdims=True)
    cut_rows(chips, at, scratch, total_ref, pieces)


def cut_rows(chips, at, scratch, total_ref, pieces):
    part = total_ref.shape[0]
    columns = scratch.shape[0] // (2 * part)
    for p, (k, s) in enumerate(chips):
        rows = scratch[aligned(s * columns + (at[0] ^ k), part), :]
        if p:
            pieces[p - 1][...] = rows.astype(bf16)
        else:
            total_ref[...] = rows


def turn(at, total_ref, *refs):
    pieces, (middle_ref, grad_ref, gains, grad_middle_ref, low_ref) = refs[:-5], refs[-5:]
    part = total_ref.shape[0]
    total = total_ref[...]
    for piece in pieces:
        total = total + piece[...].astype(f32)
    centred, inverse = norm_rows(middle_ref[...])
    grad = grad_ref[aligned(at[0], part), :].astype(f32)
    grad = grad + norm_backward(total, centred, inverse, gains[1:2, :])
    grad_middle_ref[...] = grad
    low_ref[...] = grad.astype(bf16)


def settle(chips, count, at, *refs):
    weights, refs = both_cores(count, at, refs)
    (normed_ref, unit_ref, active_ref, grad_ref, middle_ref), refs = refs[:5], refs[5:]
    (own_ref, other_ref, total_ref), refs = refs[:3], refs[3:]
    pieces, scratch = refs[:-1], refs[-1]
    hidden = active_ref.shape[2]
    block, span = total_ref.shape
    normed, grad = normed_ref[...].T, grad_ref[...].T
    for b, out in enumerate((other_ref, own_ref)):
        out[:, : 2 * hidden] = mm(normed, unit_ref[1 - b]).astype(bf16)
        out[:, 2 * hidden : 3 * hidden] = mm(grad, active_ref[1 - b]).astype(bf16)
        if out.shape[1] > 3 * hidden:
            out[:, 3 * hidden :] = jnp.zeros((out.shape[0], out.shape[1] - 3 * hidden), bf16)
    scratch[...] = jnp.zeros_like(scratch)
    for b, (weight, starts) in enumerate(weights):
        spread(scratch, active_ref[b], weight, starts, slice(2 * hidden, 3 * hidden))
    for p, (k, s) in enumerate(chips):
        piece = scratch[s * block : (s + 1) * block, aligned(at[0] ^ k, span)]
        if p:
            pieces[p - 1][...] = piece.astype(bf16)
        else:
            total_ref[...] = piece + middle_ref[...]


def reflect(chips, count, at, *refs):
    pieces, refs = refs[: len(chips)], refs[len(chips) :]
    weights, refs = both_cores(count, at, refs)
    query_ref, pairs_ref, total_ref, grad_attn_ref, grad_query_ref, grad_pairs_ref = refs
    part = pieces[0].shape[0]
    rows, width = query_ref.shape
    columns = rows // (2 * part)
    half = width // 2
    for (k, s), piece in zip(chips, pieces):
        grad_attn_ref[aligned(s * columns + (at[0] ^ k), part), :] = piece[...]
    grad_context = jnp.concatenate(
        [contract(grad_attn_ref, weight, starts, slice(3 * half, 4 * half)) for weight, starts in weights],
        axis=1,
    ).astype(bf16)
    keys = pairs_ref[:, :width].T
    grad_queries = []
    for h in range(width // HEAD_DIM):
        lanes = slice(h * HEAD_DIM, (h + 1) * HEAD_DIM)
        query = query_ref[:, lanes]
        grad = grad_context[:, lanes]
        probs = jnp.exp(mm_nt(pairs_ref[:, lanes], query) - total_ref[h : h + 1, :])
        value_lanes = slice(width + h * HEAD_DIM, width + (h + 1) * HEAD_DIM)
        grad_probs = mm_nt(pairs_ref[:, value_lanes], grad)
        delta = jnp.sum(probs * grad_probs, axis=0, keepdims=True)
        grad_scores = (probs * (grad_probs - delta)).astype(bf16)
        grad_pairs_ref[:, lanes] = mm(grad_scores, query)
        grad_pairs_ref[:, value_lanes] = mm(probs.astype(bf16), grad)
        grad_queries.append(mm(keys[lanes], grad_scores))
    grad_query_ref[...] = jnp.concatenate(grad_queries, axis=0).T * HEAD_DIM**-0.5


def unwind(chips, count, at, *refs):
    weights, refs = both_cores(count, at, refs)
    (grad_query_ref, grad_pairs_ref, cosine, sine, rows_ref), refs = refs[:5], refs[5:]
    (grad_projected_ref, gain_ref, total_ref), refs = refs[:3], refs[3:]
    pieces, scratch = refs[:-1], refs[-1]
    width = grad_query_ref.shape[1]
    half = width // 2
    cosine, sine = cosine[...], sine[...]
    grad_query, grad_key = grad_query_ref[...], grad_pairs_ref[:, :width]
    grad_query = (grad_query * cosine - rotated(grad_query * sine)).astype(bf16)
    grad_key = (grad_key * cosine - rotated(grad_key * sine)).astype(bf16)
    grad_value = grad_pairs_ref[:, width:].astype(bf16)
    scratch[...] = jnp.zeros_like(scratch)
    for b, (weight, starts) in enumerate(weights):
        lanes = slice(b * half, (b + 1) * half)
        grad = jnp.concatenate([grad_query[:, lanes], grad_key[:, lanes], grad_value[:, lanes]], axis=1)
        grad_projected_ref[b] = grad
        spread(scratch, grad, weight, starts, slice(0, 3 * half))
    centred, _ = norm_rows(rows_ref[...].astype(f32))
    gain_ref[...] = jnp.sum(scratch[...] * centred, axis=0, keepdims=True)
    cut_rows(chips, at, scratch, total_ref, pieces)


def repay(at, normed_ref, grad_projected_ref, grad_attn_ref, context_ref, own_ref, other_ref):
    half = context_ref.shape[1] // 2
    normed, grad_attn = normed_ref[...].T, grad_attn_ref[...].T
    for b, out in ((1, other_ref), (0, own_ref)):
        out[:, : 3 * half] = mm(normed, grad_projected_ref[b]).astype(bf16)
        out[:, 3 * half :] = mm(grad_attn, context_ref[:, b * half : (b + 1) * half]).astype(bf16)


def finish(narrow, at, total_ref, *refs):
    pieces, (rows_ref, grad_middle_ref, gains), outs, scratch = refs[: -narrow - 4], refs[-narrow - 4 : -narrow - 1], refs[-narrow - 1 : -1], refs[-1]
    part = total_ref.shape[0]
    width = outs[0].shape[1]
    total = total_ref[...]
    for piece in pieces:
        total = total + piece[...].astype(f32)
    centred, inverse = norm_rows(rows_ref[aligned(at[0], part), :].astype(f32))
    scratch[...] = grad_middle_ref[...] + norm_backward(total, centred, inverse, gains[0:1, :])
    for m, out in enumerate(outs):
        out[...] = scratch[:, aligned(at[1] ^ m, width)]


def body(
    wide,
    narrow,
    inputs,
    attn_gain,
    query_key_value_weight,
    attention_out_weight,
    mlp_gain,
    feedforward_in_weight,
    feedforward_out_weight,
    grad_out,
):
    groups, columns = wide // 2, narrow // 2
    _, block, width = inputs.shape
    model = width * narrow
    depth = query_key_value_weight.shape[0]
    hidden = feedforward_out_weight.shape[0] // 2
    half, span = width // 2, 2 * width
    part = block // columns
    rows = 2 * block
    length = groups * rows
    wide_at, narrow_at = lax.axis_index("wide"), lax.axis_index("narrow")
    group, side = wide_at // 2, wide_at % 2
    column, core = narrow_at // 2, narrow_at % 2
    chips = [(k, s) for s in range(2) for k in range(columns)]

    unit_mask = 2 * narrow

    def swap(array, mask):
        if mask == 0:
            return array
        return lax.ppermute(
            array, ("wide", "narrow"), [(i, i ^ mask) for i in range(wide * narrow)]
        )

    def over_chips(column_rel, side_rel):
        return 2 * column_rel + narrow * side_rel

    def over_groups(group_rel):
        return 2 * narrow * group_rel

    def after(array, *others):
        return lax.optimization_barrier((array, *others))[0]

    def swap_ways(array, even, odd):
        pairs = [(i, i ^ (odd if i % 2 else even)) for i in range(wide * narrow)]
        return lax.ppermute(array, ("wide", "narrow"), pairs)

    def ring_order(count):
        if count < 4:
            return list(range(count))
        quad = [0, 1 + 2 * core, 3 - 2 * core, 2]
        return [low + 4 * high for high in ring_order(count // 4) for low in quad]

    def other_way(relative):
        turned, unit = relative, 1
        while 4 * unit <= groups:
            turned, unit = turned ^ (2 * unit * ((relative // unit) % 2)), 4 * unit
        return turned

    def ring_first(array, unit):
        return swap_ways(array, unit, 3 * unit), swap_ways(array, 3 * unit, unit)

    def ring_last(second, unit):
        return swap_ways(second, unit, 3 * unit)

    def gather_ring(array, unit, count):
        if count < 4:
            return [swap(array, unit * k) for k in range(count)]
        first, second = ring_first(array, unit)
        quad = [array, first, second, ring_last(second, unit)]
        if count == 4:
            return quad
        return [q for quads in gather_ring(jnp.stack(quad), 4 * unit, count // 4) for q in quads]

    def scatter_first(pieces, unit):
        count = len(pieces)
        if count < 4:
            return pieces, None
        if count > 4:
            stacked = [jnp.stack(pieces[k : k + 4]) for k in range(0, count, 4)]
            pieces = list(scatter_ring(stacked, 4 * unit))
        own, first, second, across = pieces
        passing = swap_ways(across.astype(bf16), unit, 3 * unit)
        arrived = swap_ways(first.astype(bf16), unit, 3 * unit)
        return own, (second, passing, arrived)

    def scatter_last(own, state, unit):
        if state is None:
            total = own[0].astype(f32)
            for k in range(1, len(own)):
                total = total + swap(own[k].astype(bf16), unit * k).astype(f32)
            return total
        second, passing, arrived = state
        second = (second.astype(f32) + passing.astype(f32)).astype(bf16)
        return own.astype(f32) + arrived.astype(f32) + swap_ways(second, 3 * unit, unit).astype(f32)

    def scatter_ring(pieces, unit):
        return scatter_last(*scatter_first(pieces, unit), unit)

    def place_groups(pieces, order):
        size = pieces[0].shape[0]
        whole = jnp.zeros((size * groups, pieces[0].shape[1]), pieces[0].dtype)
        for relative, piece in zip(order, pieces):
            whole = lax.dynamic_update_slice_in_dim(whole, piece, (group ^ relative) * size, 0)
        return whole

    def fetch_side(bundle):
        received = swap(pick(bundle, 1 - side), narrow)
        return place([pick(bundle, side), received], side, 0)

    def halves(array):
        return array.reshape(depth, -1, 2, array.shape[-1] // 2).transpose(2, 0, 1, 3)

    def from_chips(array):
        return [swap(array, over_chips(k, s)) for k, s in chips]

    def to_chips(pieces):
        return [swap(piece, over_chips(k, s)) for (k, s), piece in zip(chips[1:], pieces)]

    def reduce_cores(own, other, *others):
        received = after(swap(other, 1), *others)

        def places(*later):
            blocks = []
            for place_at, k in enumerate(ring_order(groups)):
                pair = (own, received)
                if later and place_at % 2 == 0:
                    pair = lax.optimization_barrier((own, received, *later))[:2]
                pair = [pick(array.reshape(groups, 2 * depth, -1), group ^ k).astype(f32) for array in pair]
                blocks.append(pair[0] + pair[1])
            return blocks

        return places

    def scatter_early(places):
        if groups != 4:
            return scatter_first(places(), unit_mask)
        _, first, _, across = places()
        return swap_ways(across.astype(bf16), unit_mask, 3 * unit_mask), swap_ways(first.astype(bf16), unit_mask, 3 * unit_mask)

    def scatter_late(places, state, *later):
        if groups != 4:
            return scatter_last(*state, unit_mask)
        own, _, second, _ = places(*later)
        return scatter_last(own, (second, *state), unit_mask)

    def reduce_side(total):
        total = total.reshape(2, depth, -1)
        kept = pick(total, side)
        received = swap(pick(total, 1 - side).astype(bf16), narrow).astype(f32)
        return place([kept[None], received[None]], side, 0)

    def join(array):
        return array.transpose(1, 2, 0, 3).reshape(depth, array.shape[2], -1)

    attn_bundle = jnp.concatenate(
        [halves(query_key_value_weight), halves(attention_out_weight.T[:, None])], axis=2
    ).reshape(2, depth, 4 * half)
    mlp_bundle = jnp.concatenate(
        [halves(feedforward_in_weight), halves(feedforward_out_weight.T[:, None])], axis=2
    ).reshape(2, depth, 3 * hidden)
    lanes = -(-3 * hidden // 128) * 128
    mlp_bundle = jnp.pad(mlp_bundle, ((0, 0), (0, 0), (0, lanes - 3 * hidden)))

    both = jnp.stack([inputs, grad_out])
    received = swap(pick(both, 1 - core, 1), 1)
    features = place([pick(both, core, 1), received], core, 2)
    attn_pair = fetch_side(attn_bundle)
    shards = from_chips(features)
    gains = after(jnp.stack([attn_gain, mlp_gain]), shards)
    gains = place([gains, swap(gains, 1)], core, 1)
    gains = place([swap(gains, 2 * k) for k in range(columns)], column, 1)
    mlp_pair = fetch_side(after(mlp_bundle, shards))
    if groups >= 4:
        quad = [attn_pair, *ring_first(attn_pair, unit_mask)]
        quad, shards = lax.optimization_barrier((quad, shards))
        quad.append(ring_last(quad[2], unit_mask))
        if groups > 4:
            quad = [q for quads in gather_ring(jnp.stack(quad), 4 * unit_mask, groups // 4) for q in quads]
    else:
        quad = gather_ring(attn_pair, unit_mask, groups)
    order = ring_order(groups)
    turned = [other_way(k) for k in order]
    count = groups if 2 * depth % 128 == 0 else 1
    starts = [group ^ k for k in order] + [group ^ k for k in turned] if count > 1 else [0, 0]

    def both_blocks(own, other):
        return [*own, *other] if count > 1 else [place_groups(own, order), place_groups(other, turned)]

    token = (jnp.arange(rows) // block) ^ side
    positions = ((group * 2 + token) * block + jnp.arange(rows) % block).astype(f32)
    cosine, sine = rope_tables(positions, width)
    at = jnp.stack([column, narrow_at, *starts]).astype(jnp.int32)
    early = [swap(piece, 1) for piece in quad[:3]]
    mlp_pair, gains, quad, early, cosine, sine, at = lax.optimization_barrier(
        (mlp_pair, gains, quad, early, cosine, sine, at)
    )
    attn_weights = both_blocks(quad, [*early, *[swap(piece, 1) for piece in quad[len(early) :]]])
    mlp_quad = [mlp_pair, *ring_first(mlp_pair, unit_mask)] if groups >= 4 else []

    rows_in, grad_rows, normed_one, query, pair = call(
        functools.partial(project, chips, count),
        [((rows, model), bf16)] * 3 + [((rows, width), bf16), ((rows, span), bf16)],
        at, *shards, *attn_weights, gains, cosine, sine,
    )
    if groups == 4:
        first, second = lax.optimization_barrier(ring_first(pair, unit_mask))
        mlp_quad = [mlp_quad[0], *[after(piece, first, second) for piece in mlp_quad[1:]]]
        pairs = [pair, first, second, ring_last(second, unit_mask)]
    else:
        pairs = gather_ring(pair, unit_mask, groups)
    out_own = place_groups([after(piece[:, 3 * half :], *pairs[1:-1]) for piece in quad], order)
    out_own = jnp.stack(from_chips(out_own))
    early = [swap(piece, 1) for piece in mlp_quad]
    pairs, out_own, early = lax.optimization_barrier((pairs, out_own, early))
    out_other = swap(out_own, 1)
    if groups >= 4:
        mlp_quad.append(ring_last(after(mlp_quad[2], pairs), unit_mask))
    context, pairs, total = call(
        functools.partial(attend, len(pairs)),
        [((rows, width), bf16), ((length, span), bf16), ((8, rows), f32)],
        at, query, *pairs,
    )
    contexts = from_chips(context)
    if groups >= 4:
        late = after(mlp_quad.pop(), contexts)
        mlp_quad, early = [*mlp_quad, late], [*early, swap(late, 1)]
        if groups > 4:
            mlp_quad = [q for quads in gather_ring(jnp.stack(mlp_quad), 4 * unit_mask, groups // 4) for q in quads]
            early = [swap(piece, 1) for piece in mlp_quad]
    else:
        mlp_quad = gather_ring(mlp_pair, unit_mask, groups)
        early = [swap(piece, 1) for piece in mlp_quad]
    mlp_weights = both_blocks(mlp_quad, early)
    middle, middle_rows, normed_two, unit, active, mlp_gain_part, grad_two, *sends = call(
        functools.partial(feed, chips, count),
        [((block, span), f32), ((part, model), f32), ((rows, model), bf16), ((2, rows, 2 * hidden), bf16),
         ((2, rows, hidden), bf16), ((1, model), f32), ((part, model), f32)] + [((part, model), bf16)] * (len(chips) - 1),
        at, *contexts, *mlp_weights, out_own, out_other, rows_in, grad_rows, gains,
        scratch=[((rows, model), f32)],
    )
    received = to_chips(sends)
    grad_mlp_own, grad_mlp_other, branch, *branch_sends = call(
        functools.partial(settle, chips, count),
        [((model, lanes), bf16)] * 2 + [((block, span), f32)] + [((block, span), bf16)] * (len(chips) - 1),
        at, *mlp_weights, normed_two, unit, active, grad_rows, middle,
        scratch=[((rows, model), f32)],
    )
    grad_mlp_other = after(grad_mlp_other, received)
    grad_middle, grad_low = call(
        functools.partial(turn), [((part, model), f32), ((part, model), bf16)],
        at, grad_two, *received, middle_rows, grad_rows, gains,
    )
    grad_pieces = from_chips(grad_low)
    grad_mlp = reduce_cores(grad_mlp_own, grad_mlp_other, grad_low)
    mlp_state = scatter_early(grad_mlp)
    grad_attn, grad_query, grad_pairs = call(
        functools.partial(reflect, chips, count),
        [((rows, model), bf16), ((rows, width), f32), ((length, span), f32)],
        at, *grad_pieces, *attn_weights, query, pairs, total,
    )
    if groups >= 4:
        mlp_state, grad_pairs, branch_sends = lax.optimization_barrier((mlp_state, grad_pairs, branch_sends))
    grad_pairs = scatter_ring(list(grad_pairs.reshape(groups, rows, span)), unit_mask)

    branch_received = to_chips(branch_sends)
    grad_pairs, mlp_state, branch_received = lax.optimization_barrier((grad_pairs, mlp_state, branch_received))
    for piece in branch_received:
        branch = branch + piece.astype(f32)
    branch = branch.astype(bf16).reshape(block, 2, width)
    result = place([pick(branch, core, 1)[None], swap(pick(branch, 1 - core, 1), 1)[None]], core, 0)

    grad_mlp = scatter_late(grad_mlp, mlp_state, grad_query)
    grad_projected, attn_gain_part, grad_one, *sends = call(
        functools.partial(unwind, chips, count),
        [((2, rows, 3 * half), bf16), ((1, model), f32), ((part, model), f32)] + [((part, model), bf16)] * (len(chips) - 1),
        at, *attn_weights, grad_query, grad_pairs, cosine, sine, rows_in,
        scratch=[((rows, model), f32)],
    )
    received = to_chips(sends)
    grad_attn_own, grad_attn_other = call(
        functools.partial(repay), [((model, 4 * half), bf16)] * 2,
        at, normed_one, grad_projected, grad_attn, context,
    )
    grad_attn_other, grad_mlp, received = lax.optimization_barrier((grad_attn_other, grad_mlp, received))
    gain_grads = jnp.concatenate([after(attn_gain_part, *received), mlp_gain_part], axis=0).reshape(2, narrow, width)
    gain_total = pick(gain_grads, narrow_at, 1)
    for m in range(1, narrow):
        gain_total = gain_total + swap(pick(gain_grads, narrow_at ^ m, 1), m)
    attn_places = reduce_cores(grad_attn_own, grad_attn_other, gain_total)
    summed = [piece.astype(bf16) for piece in attn_places()[1::2]]
    state = scatter_early(attn_places)
    finished = call(
        functools.partial(finish, narrow), [((part, width), f32)] * narrow,
        at, after(grad_one, *summed), *received, rows_in, grad_middle, gains,
        scratch=[((part, model), f32)],
    )
    sends = [swap(piece, m) for m, piece in enumerate(finished)]
    gain_total = after(gain_total, *summed)
    gain_total = gain_total + swap(gain_total, narrow)
    sends, state, gain_total = lax.optimization_barrier((sends, state, gain_total))
    grad_mlp = after(grad_mlp, *summed)
    grad_mlp = join(reduce_side(grad_mlp)[..., : 3 * hidden].reshape(2, depth, 3, hidden))
    grad_attn_weight = scatter_late(attn_places, state, finished[0])
    gain_total = after(gain_total, grad_attn_weight)
    for mask in ring_masks(groups):
        gain_total = gain_total + swap(gain_total, 2 * narrow * mask)
    grad_attn_weight = join(reduce_side(grad_attn_weight).reshape(2, depth, 4, half))
    grad_inputs = place(
        [place([sends[2 * k + c] for k in range(columns)], column, 0)[None] for c in range(2)],
        core, 0,
    )
    return (
        result,
        grad_inputs,
        gain_total[0],
        grad_attn_weight[:, :3],
        grad_attn_weight[:, 3].T,
        gain_total[1],
        grad_mlp[:, :2],
        grad_mlp[:, 2].T,
    )


def solution(mesh):
    in_specs = (
        P(None, "wide", "narrow"),
        P("narrow"),
        P("wide", None, "narrow"),
        P("narrow", "wide"),
        P("narrow"),
        P("wide", None, "narrow"),
        P("narrow", "wide"),
        P(None, "wide", "narrow"),
    )
    out_specs = (
        P(None, "wide", "narrow"),
        P(None, "wide", "narrow"),
        P("narrow"),
        P("wide", None, "narrow"),
        P("narrow", "wide"),
        P("narrow"),
        P("wide", None, "narrow"),
        P("narrow", "wide"),
    )
    step = functools.partial(body, mesh.shape["wide"], mesh.shape["narrow"])
    return jax.shard_map(step, mesh=mesh, in_specs=in_specs, out_specs=out_specs, check_vma=False)
```

```python
import functools
import math

import jax
import jax.numpy as jnp
from jax import lax
from jax.experimental import pallas as pl
from jax.experimental.pallas import tpu as pltpu
from jax.sharding import PartitionSpec as P

HEAD_DIM = 64
eps_norm = 1e-05
rope_base = 160000.0
f32 = jnp.float32
bf16 = jnp.bfloat16


def mm(a, b):
    return lax.dot_general(a, b, (((1,), (0,)), ((), ())), preferred_element_type=f32)


def mm_nt(a, b):
    return lax.dot_general(a, b, (((1,), (1,)), ((), ())), preferred_element_type=f32)


def aligned(index, size):
    return pl.ds(pl.multiple_of(index * size, size), size)


def norm_rows(rows):
    width = rows.shape[-1]
    average = jnp.sum(rows, axis=-1, keepdims=True) / width
    variance = jnp.sum(rows * rows, axis=-1, keepdims=True) / width - average * average
    inverse = lax.rsqrt(variance + eps_norm)
    return (rows - average) * inverse, inverse


def norm_backward(grad_normed, centred, inverse, gain):
    width = grad_normed.shape[-1]
    scaled = grad_normed * gain
    row_total = jnp.sum(scaled, axis=-1, keepdims=True)
    row_along = jnp.sum(scaled * centred, axis=-1, keepdims=True)
    return inverse * (scaled - row_total / width - centred * (row_along / width))


def rope_tables(positions, lanes):
    half_dim = HEAD_DIM // 2
    frequency = rope_base ** (-jnp.arange(half_dim).astype(f32) * 2.0 / HEAD_DIM)
    angles = positions[:, None] * frequency[None, :]
    angles = jnp.concatenate([angles, angles] * (lanes // HEAD_DIM), axis=-1)
    return jnp.cos(angles), jnp.sin(angles)


def rotated(tensor):
    lanes, half_dim = tensor.shape[-1], HEAD_DIM // 2
    lane = lax.broadcasted_iota(jnp.int32, tensor.shape, 1)
    up = pltpu.roll(tensor, half_dim, 1)
    down = pltpu.roll(tensor, lanes - half_dim, 1)
    return jnp.where(lane % HEAD_DIM < half_dim, -down, up)


def call(kernel, outs, at, *arrays, scratch=()):
    return pl.pallas_call(
        kernel,
        out_shape=[jax.ShapeDtypeStruct(shape, dtype) for shape, dtype in outs],
        in_specs=[pl.BlockSpec(memory_space=pltpu.SMEM)]
        + [pl.BlockSpec(memory_space=pltpu.VMEM)] * len(arrays),
        out_specs=[pl.BlockSpec(memory_space=pltpu.VMEM)] * len(outs),
        scratch_shapes=[pltpu.VMEM(shape, dtype) for shape, dtype in scratch],
        compiler_params=pltpu.CompilerParams(vmem_limit_bytes=60 * 1024 * 1024),
        name=kernel.func.__name__,
    )(at, *arrays)


def ring_masks(count):
    masks, unit = [], 1
    while unit < count:
        masks += [unit] + ([3 * unit] if 4 * unit <= count else [])
        unit *= 4
    return masks


def pick(array, index, axis=0):
    return lax.dynamic_index_in_dim(array, index, axis=axis, keepdims=False)


def place(pieces, own, axis):
    count = len(pieces)
    if count == 1:
        return pieces[0]
    if count == 2:
        return jnp.where(
            own == 0,
            jnp.concatenate(pieces, axis=axis),
            jnp.concatenate(pieces[::-1], axis=axis),
        )
    size = pieces[0].shape[axis]
    shape = list(pieces[0].shape)
    shape[axis] = size * count
    whole = jnp.zeros(shape, pieces[0].dtype)
    for relative, piece in enumerate(pieces):
        whole = lax.dynamic_update_slice_in_dim(whole, piece, (own ^ relative) * size, axis)
    return whole


def contract(rows_ref, pieces, starts, lanes):
    total = 0.0
    for piece, start in zip(pieces, starts):
        total = total + mm(rows_ref[:, aligned(start, piece.shape[0])], piece[:, lanes])
    return total


def spread(out_ref, array, pieces, starts, lanes):
    for piece, start in zip(pieces, starts):
        out_ref[:, aligned(start, piece.shape[0])] += mm_nt(array, piece[:, lanes])


def both_cores(count, at, refs):
    first = [at[2 + p] for p in range(count)]
    second = [at[2 + count + p] for p in range(count)]
    return ((refs[:count], first), (refs[count : 2 * count], second)), refs[2 * count :]


def project(chips, count, at, *refs):
    shards, refs = refs[: len(chips)], refs[len(chips) :]
    weights, refs = both_cores(count, at, refs)
    gains, cosine, sine, rows_ref, grad_ref, normed_ref, query_ref, pair_ref = refs
    block, span = shards[0].shape[1:]
    half = query_ref.shape[1] // 2
    for (k, s), shard in zip(chips, shards):
        lanes = aligned(at[0] ^ k, span)
        rows_ref[s * block : (s + 1) * block, lanes] = shard[0]
        grad_ref[s * block : (s + 1) * block, lanes] = shard[1]
    centred, _ = norm_rows(rows_ref[...].astype(f32))
    normed_ref[...] = (centred * gains[0:1, :]).astype(bf16)
    queries, keys, values = [], [], []
    for pieces, starts in weights:
        projected = contract(normed_ref, pieces, starts, slice(0, 3 * half))
        queries.append(projected[:, :half])
        keys.append(projected[:, half : 2 * half])
        values.append(projected[:, 2 * half :])
    query, key = jnp.concatenate(queries, axis=1), jnp.concatenate(keys, axis=1)
    cosine, sine = cosine[...], sine[...]
    query = (query * cosine + rotated(query) * sine).astype(bf16)
    key = (key * cosine + rotated(key) * sine).astype(bf16)
    query_ref[...] = query * jnp.asarray(HEAD_DIM**-0.5, bf16)
    pair_ref[:, : 2 * half] = key
    pair_ref[:, 2 * half :] = jnp.concatenate(values, axis=1).astype(bf16)


def attend(parts, at, query_ref, *refs):
    pieces, (context_ref, pairs_ref, total_ref) = refs[:parts], refs[parts:]
    start = 0
    for piece in pieces:
        pairs_ref[start : start + piece.shape[0], :] = piece[...]
        start += piece.shape[0]
    width = query_ref.shape[1]
    values = pairs_ref[:, width:].T
    contexts = []
    for h in range(width // HEAD_DIM):
        lanes = slice(h * HEAD_DIM, (h + 1) * HEAD_DIM)
        scores = mm_nt(pairs_ref[:, lanes], query_ref[:, lanes])
        peak = jnp.max(scores, axis=0, keepdims=True)
        log_total = peak + jnp.log(jnp.sum(jnp.exp(scores - peak), axis=0, keepdims=True))
        probs = jnp.exp(scores - log_total).astype(bf16)
        contexts.append(mm(values[lanes], probs))
        total_ref[h : h + 1, :] = log_total
    context_ref[...] = jnp.concatenate(contexts, axis=0).T.astype(bf16)


def feed(chips, count, at, *refs):
    contexts, refs = refs[: len(chips)], refs[len(chips) :]
    weights, refs = both_cores(count, at, refs)
    (out_own, out_other, rows_ref, grad_ref, gains), refs = refs[:5], refs[5:]
    (middle_ref, middle_rows_ref, normed_ref, unit_ref, active_ref, gain_ref, total_ref), refs = refs[:7], refs[7:]
    pieces, scratch = refs[:-1], refs[-1]
    hidden = active_ref.shape[2]
    block, span = middle_ref.shape
    part = total_ref.shape[0]
    middle = rows_ref[...].astype(f32)
    for p, (k, s) in enumerate(chips):
        context = contexts[p][...]
        if s:
            context = jnp.concatenate([context[block:], context[:block]], axis=0)
        middle = middle + mm_nt(context, jnp.concatenate([out_own[p], out_other[p]], axis=1))
    scratch[...] = middle
    middle_ref[...] = scratch[:block, aligned(at[0], span)]
    middle_rows_ref[...] = scratch[aligned(at[0], part), :]
    centred, _ = norm_rows(middle)
    normed_ref[...] = (centred * gains[1:2, :]).astype(bf16)
    scratch[...] = jnp.zeros_like(scratch)
    for b, (weight, starts) in enumerate(weights):
        gate_up = contract(normed_ref, weight, starts, slice(0, 2 * hidden))
        gate, lift = gate_up[:, :hidden], gate_up[:, hidden:]
        share = 0.5 + 0.5 * lax.erf(gate * math.sqrt(0.5))
        bent = gate * share
        active_ref[b] = (bent * lift).astype(bf16)
        slope = share + gate * jnp.exp(-0.5 * gate * gate) * (1.0 / math.sqrt(2.0 * math.pi))
        back = contract(grad_ref, weight, starts, slice(2 * hidden, 3 * hidden))
        unit = jnp.concatenate([back * lift * slope, back * bent], axis=1).astype(bf16)
        unit_ref[b] = unit
        spread(scratch, unit, weight, starts, slice(0, 2 * hidden))
    gain_ref[...] = jnp.sum(scratch[...] * centred, axis=0, keepdims=True)
    cut_rows(chips, at, scratch, total_ref, pieces)


def cut_rows(chips, at, scratch, total_ref, pieces):
    part = total_ref.shape[0]
    columns = scratch.shape[0] // (2 * part)
    for p, (k, s) in enumerate(chips):
        rows = scratch[aligned(s * columns + (at[0] ^ k), part), :]
        if p:
            pieces[p - 1][...] = rows.astype(bf16)
        else:
            total_ref[...] = rows


def turn(at, total_ref, *refs):
    pieces, (middle_ref, grad_ref, gains, grad_middle_ref, low_ref) = refs[:-5], refs[-5:]
    part = total_ref.shape[0]
    total = total_ref[...]
    for piece in pieces:
        total = total + piece[...].astype(f32)
    centred, inverse = norm_rows(middle_ref[...])
    grad = grad_ref[aligned(at[0], part), :].astype(f32)
    grad = grad + norm_backward(total, centred, inverse, gains[1:2, :])
    grad_middle_ref[...] = grad
    low_ref[...] = grad.astype(bf16)


def settle(chips, count, at, *refs):
    weights, refs = both_cores(count, at, refs)
    (normed_ref, unit_ref, active_ref, grad_ref, middle_ref), refs = refs[:5], refs[5:]
    (own_ref, other_ref, total_ref), refs = refs[:3], refs[3:]
    pieces, scratch = refs[:-1], refs[-1]
    hidden = active_ref.shape[2]
    block, span = total_ref.shape
    normed, grad = normed_ref[...].T, grad_ref[...].T
    for b, out in enumerate((other_ref, own_ref)):
        out[:, : 2 * hidden] = mm(normed, unit_ref[1 - b]).astype(bf16)
        out[:, 2 * hidden : 3 * hidden] = mm(grad, active_ref[1 - b]).astype(bf16)
        if out.shape[1] > 3 * hidden:
            out[:, 3 * hidden :] = jnp.zeros((out.shape[0], out.shape[1] - 3 * hidden), bf16)
    scratch[...] = jnp.zeros_like(scratch)
    for b, (weight, starts) in enumerate(weights):
        spread(scratch, active_ref[b], weight, starts, slice(2 * hidden, 3 * hidden))
    for p, (k, s) in enumerate(chips):
        piece = scratch[s * block : (s + 1) * block, aligned(at[0] ^ k, span)]
        if p:
            pieces[p - 1][...] = piece.astype(bf16)
        else:
            total_ref[...] = piece + middle_ref[...]


def reflect(chips, count, at, *refs):
    pieces, refs = refs[: len(chips)], refs[len(chips) :]
    weights, refs = both_cores(count, at, refs)
    query_ref, pairs_ref, total_ref, grad_attn_ref, grad_query_ref, grad_pairs_ref = refs
    part = pieces[0].shape[0]
    rows, width = query_ref.shape
    columns = rows // (2 * part)
    half = width // 2
    for (k, s), piece in zip(chips, pieces):
        grad_attn_ref[aligned(s * columns + (at[0] ^ k), part), :] = piece[...]
    grad_context = jnp.concatenate(
        [contract(grad_attn_ref, weight, starts, slice(3 * half, 4 * half)) for weight, starts in weights],
        axis=1,
    ).astype(bf16)
    keys = pairs_ref[:, :width].T
    grad_queries = []
    for h in range(width // HEAD_DIM):
        lanes = slice(h * HEAD_DIM, (h + 1) * HEAD_DIM)
        query = query_ref[:, lanes]
        grad = grad_context[:, lanes]
        probs = jnp.exp(mm_nt(pairs_ref[:, lanes], query) - total_ref[h : h + 1, :])
        value_lanes = slice(width + h * HEAD_DIM, width + (h + 1) * HEAD_DIM)
        grad_probs = mm_nt(pairs_ref[:, value_lanes], grad)
        delta = jnp.sum(probs * grad_probs, axis=0, keepdims=True)
        grad_scores = (probs * (grad_probs - delta)).astype(bf16)
        grad_pairs_ref[:, lanes] = mm(grad_scores, query)
        grad_pairs_ref[:, value_lanes] = mm(probs.astype(bf16), grad)
        grad_queries.append(mm(keys[lanes], grad_scores))
    grad_query_ref[...] = jnp.concatenate(grad_queries, axis=0).T * HEAD_DIM**-0.5


def unwind(chips, count, at, *refs):
    weights, refs = both_cores(count, at, refs)
    (grad_query_ref, grad_pairs_ref, cosine, sine, rows_ref), refs = refs[:5], refs[5:]
    (grad_projected_ref, gain_ref, total_ref), refs = refs[:3], refs[3:]
    pieces, scratch = refs[:-1], refs[-1]
    width = grad_query_ref.shape[1]
    half = width // 2
    cosine, sine = cosine[...], sine[...]
    grad_query, grad_key = grad_query_ref[...], grad_pairs_ref[:, :width]
    grad_query = (grad_query * cosine - rotated(grad_query * sine)).astype(bf16)
    grad_key = (grad_key * cosine - rotated(grad_key * sine)).astype(bf16)
    grad_value = grad_pairs_ref[:, width:].astype(bf16)
    scratch[...] = jnp.zeros_like(scratch)
    for b, (weight, starts) in enumerate(weights):
        lanes = slice(b * half, (b + 1) * half)
        grad = jnp.concatenate([grad_query[:, lanes], grad_key[:, lanes], grad_value[:, lanes]], axis=1)
        grad_projected_ref[b] = grad
        spread(scratch, grad, weight, starts, slice(0, 3 * half))
    centred, _ = norm_rows(rows_ref[...].astype(f32))
    gain_ref[...] = jnp.sum(scratch[...] * centred, axis=0, keepdims=True)
    cut_rows(chips, at, scratch, total_ref, pieces)


def repay(at, normed_ref, grad_projected_ref, grad_attn_ref, context_ref, own_ref, other_ref):
    half = context_ref.shape[1] // 2
    normed, grad_attn = normed_ref[...].T, grad_attn_ref[...].T
    for b, out in ((1, other_ref), (0, own_ref)):
        out[:, : 3 * half] = mm(normed, grad_projected_ref[b]).astype(bf16)
        out[:, 3 * half :] = mm(grad_attn, context_ref[:, b * half : (b + 1) * half]).astype(bf16)


def finish(narrow, at, total_ref, *refs):
    pieces, (rows_ref, grad_middle_ref, gains), outs, scratch = refs[: -narrow - 4], refs[-narrow - 4 : -narrow - 1], refs[-narrow - 1 : -1], refs[-1]
    part = total_ref.shape[0]
    width = outs[0].shape[1]
    total = total_ref[...]
    for piece in pieces:
        total = total + piece[...].astype(f32)
    centred, inverse = norm_rows(rows_ref[aligned(at[0], part), :].astype(f32))
    scratch[...] = grad_middle_ref[...] + norm_backward(total, centred, inverse, gains[0:1, :])
    for m, out in enumerate(outs):
        out[...] = scratch[:, aligned(at[1] ^ m, width)]


def body(
    wide,
    narrow,
    inputs,
    attn_gain,
    query_key_value_weight,
    attention_out_weight,
    mlp_gain,
    feedforward_in_weight,
    feedforward_out_weight,
    grad_out,
):
    groups, columns = wide // 2, narrow // 2
    _, block, width = inputs.shape
    model = width * narrow
    depth = query_key_value_weight.shape[0]
    hidden = feedforward_out_weight.shape[0] // 2
    half, span = width // 2, 2 * width
    part = block // columns
    rows = 2 * block
    length = groups * rows
    wide_at, narrow_at = lax.axis_index("wide"), lax.axis_index("narrow")
    group, side = wide_at // 2, wide_at % 2
    column, core = narrow_at // 2, narrow_at % 2
    chips = [(k, s) for s in range(2) for k in range(columns)]

    unit_mask = 2 * narrow

    def swap(array, mask):
        if mask == 0:
            return array
        return lax.ppermute(
            array, ("wide", "narrow"), [(i, i ^ mask) for i in range(wide * narrow)]
        )

    def over_chips(column_rel, side_rel):
        return 2 * column_rel + narrow * side_rel

    def over_groups(group_rel):
        return 2 * narrow * group_rel

    def after(array, *others):
        return lax.optimization_barrier((array, *others))[0]

    def swap_ways(array, even, odd):
        pairs = [(i, i ^ (odd if i % 2 else even)) for i in range(wide * narrow)]
        return lax.ppermute(array, ("wide", "narrow"), pairs)

    def ring_order(count):
        if count < 4:
            return list(range(count))
        quad = [0, 1 + 2 * core, 3 - 2 * core, 2]
        return [low + 4 * high for high in ring_order(count // 4) for low in quad]

    def other_way(relative):
        turned, unit = relative, 1
        while 4 * unit <= groups:
            turned, unit = turned ^ (2 * unit * ((relative // unit) % 2)), 4 * unit
        return turned

    def ring_first(array, unit):
        return swap_ways(array, unit, 3 * unit), swap_ways(array, 3 * unit, unit)

    def ring_last(second, unit):
        return swap_ways(second, unit, 3 * unit)

    def gather_ring(array, unit, count):
        if count < 4:
            return [swap(array, unit * k) for k in range(count)]
        first, second = ring_first(array, unit)
        quad = [array, first, second, ring_last(second, unit)]
        if count == 4:
            return quad
        return [q for quads in gather_ring(jnp.stack(quad), 4 * unit, count // 4) for q in quads]

    def scatter_first(pieces, unit):
        count = len(pieces)
        if count < 4:
            return pieces, None
        if count > 4:
            stacked = [jnp.stack(pieces[k : k + 4]) for k in range(0, count, 4)]
            pieces = list(scatter_ring(stacked, 4 * unit))
        own, first, second, across = pieces
        passing = swap_ways(across.astype(bf16), unit, 3 * unit)
        arrived = swap_ways(first.astype(bf16), unit, 3 * unit)
        return own, (second, passing, arrived)

    def scatter_last(own, state, unit):
        if state is None:
            total = own[0].astype(f32)
            for k in range(1, len(own)):
                total = total + swap(own[k].astype(bf16), unit * k).astype(f32)
            return total
        second, passing, arrived = state
        second = (second.astype(f32) + passing.astype(f32)).astype(bf16)
        return own.astype(f32) + arrived.astype(f32) + swap_ways(second, 3 * unit, unit).astype(f32)

    def scatter_ring(pieces, unit):
        return scatter_last(*scatter_first(pieces, unit), unit)

    def place_groups(pieces, order):
        size = pieces[0].shape[0]
        whole = jnp.zeros((size * groups, pieces[0].shape[1]), pieces[0].dtype)
        for relative, piece in zip(order, pieces):
            whole = lax.dynamic_update_slice_in_dim(whole, piece, (group ^ relative) * size, 0)
        return whole

    def fetch_side(bundle):
        received = swap(pick(bundle, 1 - side), narrow)
        return place([pick(bundle, side), received], side, 0)

    def halves(array):
        return array.reshape(depth, -1, 2, array.shape[-1] // 2).transpose(2, 0, 1, 3)

    def from_chips(array):
        return [swap(array, over_chips(k, s)) for k, s in chips]

    def to_chips(pieces):
        return [swap(piece, over_chips(k, s)) for (k, s), piece in zip(chips[1:], pieces)]

    def reduce_cores(own, other, *others):
        received = after(swap(other, 1), *others)

        def places(*later):
            blocks = []
            for place_at, k in enumerate(ring_order(groups)):
                pair = (own, received)
                if later and place_at % 2 == 0:
                    pair = lax.optimization_barrier((own, received, *later))[:2]
                pair = [pick(array.reshape(groups, 2 * depth, -1), group ^ k).astype(f32) for array in pair]
                blocks.append(pair[0] + pair[1])
            return blocks

        return places

    def scatter_early(places):
        if groups != 4:
            return scatter_first(places(), unit_mask)
        _, first, _, across = places()
        return swap_ways(across.astype(bf16), unit_mask, 3 * unit_mask), swap_ways(first.astype(bf16), unit_mask, 3 * unit_mask)

    def scatter_late(places, state, *later):
        if groups != 4:
            return scatter_last(*state, unit_mask)
        own, _, second, _ = places(*later)
        return scatter_last(own, (second, *state), unit_mask)

    def reduce_side(total):
        total = total.reshape(2, depth, -1)
        kept = pick(total, side)
        received = swap(pick(total, 1 - side).astype(bf16), narrow).astype(f32)
        return place([kept[None], received[None]], side, 0)

    def join(array):
        return array.transpose(1, 2, 0, 3).reshape(depth, array.shape[2], -1)

    attn_bundle = jnp.concatenate(
        [halves(query_key_value_weight), halves(attention_out_weight.T[:, None])], axis=2
    ).reshape(2, depth, 4 * half)
    mlp_bundle = jnp.concatenate(
        [halves(feedforward_in_weight), halves(feedforward_out_weight.T[:, None])], axis=2
    ).reshape(2, depth, 3 * hidden)
    lanes = -(-3 * hidden // 128) * 128
    mlp_bundle = jnp.pad(mlp_bundle, ((0, 0), (0, 0), (0, lanes - 3 * hidden)))

    both = jnp.stack([inputs, grad_out])
    received = swap(pick(both, 1 - core, 1), 1)
    features = place([pick(both, core, 1), received], core, 2)
    attn_pair = fetch_side(attn_bundle)
    shards = from_chips(features)
    gains = after(jnp.stack([attn_gain, mlp_gain]), shards)
    gains = place([gains, swap(gains, 1)], core, 1)
    gains = place([swap(gains, 2 * k) for k in range(columns)], column, 1)
    mlp_pair = fetch_side(after(mlp_bundle, shards))
    if groups >= 4:
        quad = [attn_pair, *ring_first(attn_pair, unit_mask)]
        quad, shards = lax.optimization_barrier((quad, shards))
        quad.append(ring_last(quad[2], unit_mask))
        if groups > 4:
            quad = [q for quads in gather_ring(jnp.stack(quad), 4 * unit_mask, groups // 4) for q in quads]
    else:
        quad = gather_ring(attn_pair, unit_mask, groups)
    order = ring_order(groups)
    turned = [other_way(k) for k in order]
    count = groups if 2 * depth % 128 == 0 else 1
    starts = [group ^ k for k in order] + [group ^ k for k in turned] if count > 1 else [0, 0]

    def both_blocks(own, other):
        return [*own, *other] if count > 1 else [place_groups(own, order), place_groups(other, turned)]

    token = (jnp.arange(rows) // block) ^ side
    positions = ((group * 2 + token) * block + jnp.arange(rows) % block).astype(f32)
    cosine, sine = rope_tables(positions, width)
    at = jnp.stack([column, narrow_at, *starts]).astype(jnp.int32)
    early = [swap(piece, 1) for piece in quad[:3]]
    mlp_pair, gains, quad, early, cosine, sine, at = lax.optimization_barrier(
        (mlp_pair, gains, quad, early, cosine, sine, at)
    )
    attn_weights = both_blocks(quad, [*early, *[swap(piece, 1) for piece in quad[len(early) :]]])
    mlp_quad = [mlp_pair, *ring_first(mlp_pair, unit_mask)] if groups >= 4 else []

    rows_in, grad_rows, normed_one, query, pair = call(
        functools.partial(project, chips, count),
        [((rows, model), bf16)] * 3 + [((rows, width), bf16), ((rows, span), bf16)],
        at, *shards, *attn_weights, gains, cosine, sine,
    )
    out_own = place_groups([after(piece[:, 3 * half :], pair) for piece in quad], order)
    out_own = from_chips(out_own)
    if groups == 4:
        (first, second), mlp_quad, out_own = lax.optimization_barrier((ring_first(pair, unit_mask), mlp_quad, out_own))
        pairs = [pair, first, second, ring_last(second, unit_mask)]
    else:
        pairs = gather_ring(pair, unit_mask, groups)
    pairs, out_own, early = lax.optimization_barrier((pairs, out_own, mlp_quad))
    early = [swap(piece, 1) for piece in early]
    out_own = jnp.stack(out_own)
    out_other = swap(out_own, 1)
    if groups >= 4:
        mlp_quad.append(ring_last(after(mlp_quad[2], pairs), unit_mask))
    context, pairs, total = call(
        functools.partial(attend, len(pairs)),
        [((rows, width), bf16), ((length, span), bf16), ((8, rows), f32)],
        at, query, *pairs,
    )
    contexts = from_chips(context)
    if groups >= 4:
        late = after(mlp_quad.pop(), contexts)
        mlp_quad, early = [*mlp_quad, late], [*early, swap(late, 1)]
        if groups > 4:
            mlp_quad = [q for quads in gather_ring(jnp.stack(mlp_quad), 4 * unit_mask, groups // 4) for q in quads]
            early = [swap(piece, 1) for piece in mlp_quad]
    else:
        mlp_quad = gather_ring(mlp_pair, unit_mask, groups)
        early = [swap(piece, 1) for piece in mlp_quad]
    mlp_weights = both_blocks(mlp_quad, early)
    middle, middle_rows, normed_two, unit, active, mlp_gain_part, grad_two, *sends = call(
        functools.partial(feed, chips, count),
        [((block, span), f32), ((part, model), f32), ((rows, model), bf16), ((2, rows, 2 * hidden), bf16),
         ((2, rows, hidden), bf16), ((1, model), f32), ((part, model), f32)] + [((part, model), bf16)] * (len(chips) - 1),
        at, *contexts, *mlp_weights, out_own, out_other, rows_in, grad_rows, gains,
        scratch=[((rows, model), f32)],
    )
    received = to_chips(sends)
    grad_mlp_own, grad_mlp_other, branch, *branch_sends = call(
        functools.partial(settle, chips, count),
        [((model, lanes), bf16)] * 2 + [((block, span), f32)] + [((block, span), bf16)] * (len(chips) - 1),
        at, *mlp_weights, normed_two, unit, active, grad_rows, middle,
        scratch=[((rows, model), f32)],
    )
    grad_mlp_other = after(grad_mlp_other, received)
    grad_middle, grad_low = call(
        functools.partial(turn), [((part, model), f32), ((part, model), bf16)],
        at, grad_two, *received, middle_rows, grad_rows, gains,
    )
    grad_pieces = from_chips(grad_low)
    grad_mlp = reduce_cores(grad_mlp_own, grad_mlp_other, grad_low)
    mlp_state = scatter_early(grad_mlp)
    grad_attn, grad_query, grad_pairs = call(
        functools.partial(reflect, chips, count),
        [((rows, model), bf16), ((rows, width), f32), ((length, span), f32)],
        at, *grad_pieces, *attn_weights, query, pairs, total,
    )
    if groups >= 4:
        mlp_state, grad_pairs, branch_sends = lax.optimization_barrier((mlp_state, grad_pairs, branch_sends))
    grad_pairs = scatter_ring(list(grad_pairs.reshape(groups, rows, span)), unit_mask)

    branch_received = to_chips(branch_sends)
    grad_pairs, mlp_state, branch_received = lax.optimization_barrier((grad_pairs, mlp_state, branch_received))
    for piece in branch_received:
        branch = branch + piece.astype(f32)
    branch = branch.astype(bf16).reshape(block, 2, width)
    result = place([pick(branch, core, 1)[None], swap(pick(branch, 1 - core, 1), 1)[None]], core, 0)

    grad_mlp = scatter_late(grad_mlp, mlp_state, grad_query)
    grad_projected, attn_gain_part, grad_one, *sends = call(
        functools.partial(unwind, chips, count),
        [((2, rows, 3 * half), bf16), ((1, model), f32), ((part, model), f32)] + [((part, model), bf16)] * (len(chips) - 1),
        at, *attn_weights, grad_query, grad_pairs, cosine, sine, rows_in,
        scratch=[((rows, model), f32)],
    )
    received = to_chips(sends)
    grad_attn_own, grad_attn_other = call(
        functools.partial(repay), [((model, 4 * half), bf16)] * 2,
        at, normed_one, grad_projected, grad_attn, context,
    )
    grad_attn_other, grad_mlp, received = lax.optimization_barrier((grad_attn_other, grad_mlp, received))
    gain_grads = jnp.concatenate([after(attn_gain_part, *received), mlp_gain_part], axis=0).reshape(2, narrow, width)
    gain_total = pick(gain_grads, narrow_at, 1)
    for m in range(1, narrow):
        gain_total = gain_total + swap(pick(gain_grads, narrow_at ^ m, 1), m)
    attn_places = reduce_cores(grad_attn_own, grad_attn_other, gain_total)
    summed = [piece.astype(bf16) for piece in attn_places()[1::2]]
    state = scatter_early(attn_places)
    finished = call(
        functools.partial(finish, narrow), [((part, width), f32)] * narrow,
        at, after(grad_one, *summed), *received, rows_in, grad_middle, gains,
        scratch=[((part, model), f32)],
    )
    sends = [swap(piece, m) for m, piece in enumerate(finished)]
    gain_total = after(gain_total, *summed)
    gain_total = gain_total + swap(gain_total, narrow)
    sends, state, gain_total = lax.optimization_barrier((sends, state, gain_total))
    grad_mlp = after(grad_mlp, *summed)
    grad_mlp = join(reduce_side(grad_mlp)[..., : 3 * hidden].reshape(2, depth, 3, hidden))
    grad_attn_weight = scatter_late(attn_places, state, finished[0])
    gain_total = after(gain_total, grad_attn_weight)
    if groups == 4:
        near, across, far = [swap(gain_total, unit_mask * k) for k in (1, 2, 3)]
        gain_total = (gain_total + near) + (across + far)
    else:
        for mask in ring_masks(groups):
            gain_total = gain_total + swap(gain_total, unit_mask * mask)
    grad_attn_weight = join(reduce_side(grad_attn_weight).reshape(2, depth, 4, half))
    grad_inputs = place(
        [place([sends[2 * k + c] for k in range(columns)], column, 0)[None] for c in range(2)],
        core, 0,
    )
    return (
        result,
        grad_inputs,
        gain_total[0],
        grad_attn_weight[:, :3],
        grad_attn_weight[:, 3].T,
        gain_total[1],
        grad_mlp[:, :2],
        grad_mlp[:, 2].T,
    )


def solution(mesh):
    in_specs = (
        P(None, "wide", "narrow"),
        P("narrow"),
        P("wide", None, "narrow"),
        P("narrow", "wide"),
        P("narrow"),
        P("wide", None, "narrow"),
        P("narrow", "wide"),
        P(None, "wide", "narrow"),
    )
    out_specs = (
        P(None, "wide", "narrow"),
        P(None, "wide", "narrow"),
        P("narrow"),
        P("wide", None, "narrow"),
        P("narrow", "wide"),
        P("narrow"),
        P("wide", None, "narrow"),
        P("narrow", "wide"),
    )
    step = functools.partial(body, mesh.shape["wide"], mesh.shape["narrow"])
    return jax.shard_map(step, mesh=mesh, in_specs=in_specs, out_specs=out_specs, check_vma=False)
```

```python
import functools
import math

import jax
import jax.numpy as jnp
from jax import lax
from jax.experimental import pallas as pl
from jax.experimental.pallas import tpu as pltpu
from jax.sharding import PartitionSpec as P

HEAD_DIM = 64
eps_norm = 1e-05
rope_base = 160000.0
f32 = jnp.float32
bf16 = jnp.bfloat16


def mm(a, b):
    return lax.dot_general(a, b, (((1,), (0,)), ((), ())), preferred_element_type=f32)


def mm_nt(a, b):
    return lax.dot_general(a, b, (((1,), (1,)), ((), ())), preferred_element_type=f32)


def aligned(index, size):
    return pl.ds(pl.multiple_of(index * size, size), size)


def norm_rows(rows):
    width = rows.shape[-1]
    average = jnp.sum(rows, axis=-1, keepdims=True) / width
    variance = jnp.sum(rows * rows, axis=-1, keepdims=True) / width - average * average
    inverse = lax.rsqrt(variance + eps_norm)
    return (rows - average) * inverse, inverse


def norm_backward(grad_normed, centred, inverse, gain):
    width = grad_normed.shape[-1]
    scaled = grad_normed * gain
    row_total = jnp.sum(scaled, axis=-1, keepdims=True)
    row_along = jnp.sum(scaled * centred, axis=-1, keepdims=True)
    return inverse * (scaled - row_total / width - centred * (row_along / width))


def rope_tables(positions, lanes):
    half_dim = HEAD_DIM // 2
    frequency = rope_base ** (-jnp.arange(half_dim).astype(f32) * 2.0 / HEAD_DIM)
    angles = positions[:, None] * frequency[None, :]
    angles = jnp.concatenate([angles, angles] * (lanes // HEAD_DIM), axis=-1)
    return jnp.cos(angles), jnp.sin(angles)


def rotated(tensor):
    lanes, half_dim = tensor.shape[-1], HEAD_DIM // 2
    lane = lax.broadcasted_iota(jnp.int32, tensor.shape, 1)
    up = pltpu.roll(tensor, half_dim, 1)
    down = pltpu.roll(tensor, lanes - half_dim, 1)
    return jnp.where(lane % HEAD_DIM < half_dim, -down, up)


def call(kernel, outs, at, *arrays, scratch=()):
    return pl.pallas_call(
        kernel,
        out_shape=[jax.ShapeDtypeStruct(shape, dtype) for shape, dtype in outs],
        in_specs=[pl.BlockSpec(memory_space=pltpu.SMEM)]
        + [pl.BlockSpec(memory_space=pltpu.VMEM)] * len(arrays),
        out_specs=[pl.BlockSpec(memory_space=pltpu.VMEM)] * len(outs),
        scratch_shapes=[pltpu.VMEM(shape, dtype) for shape, dtype in scratch],
        compiler_params=pltpu.CompilerParams(vmem_limit_bytes=60 * 1024 * 1024),
        name=kernel.func.__name__,
    )(at, *arrays)


def ring_masks(count):
    masks, unit = [], 1
    while unit < count:
        masks += [unit] + ([3 * unit] if 4 * unit <= count else [])
        unit *= 4
    return masks


def pick(array, index, axis=0):
    return lax.dynamic_index_in_dim(array, index, axis=axis, keepdims=False)


def place(pieces, own, axis):
    count = len(pieces)
    if count == 1:
        return pieces[0]
    if count == 2:
        return jnp.where(
            own == 0,
            jnp.concatenate(pieces, axis=axis),
            jnp.concatenate(pieces[::-1], axis=axis),
        )
    size = pieces[0].shape[axis]
    shape = list(pieces[0].shape)
    shape[axis] = size * count
    whole = jnp.zeros(shape, pieces[0].dtype)
    for relative, piece in enumerate(pieces):
        whole = lax.dynamic_update_slice_in_dim(whole, piece, (own ^ relative) * size, axis)
    return whole


def contract(rows_ref, pieces, starts, lanes):
    total = 0.0
    for piece, start in zip(pieces, starts):
        total = total + mm(rows_ref[:, aligned(start, piece.shape[0])], piece[:, lanes])
    return total


def spread(out_ref, array, pieces, starts, lanes):
    for piece, start in zip(pieces, starts):
        out_ref[:, aligned(start, piece.shape[0])] += mm_nt(array, piece[:, lanes])


def both_cores(count, at, refs):
    first = [at[2 + p] for p in range(count)]
    second = [at[2 + count + p] for p in range(count)]
    return ((refs[:count], first), (refs[count : 2 * count], second)), refs[2 * count :]


def project(chips, count, at, *refs):
    shards, refs = refs[: len(chips)], refs[len(chips) :]
    weights, refs = both_cores(count, at, refs)
    gains, cosine, sine, rows_ref, grad_ref, normed_ref, query_ref, pair_ref = refs
    block, span = shards[0].shape[1:]
    half = query_ref.shape[1] // 2
    for (k, s), shard in zip(chips, shards):
        lanes = aligned(at[0] ^ k, span)
        rows_ref[s * block : (s + 1) * block, lanes] = shard[0]
        grad_ref[s * block : (s + 1) * block, lanes] = shard[1]
    centred, _ = norm_rows(rows_ref[...].astype(f32))
    normed_ref[...] = (centred * gains[0:1, :]).astype(bf16)
    queries, keys, values = [], [], []
    for pieces, starts in weights:
        projected = contract(normed_ref, pieces, starts, slice(0, 3 * half))
        queries.append(projected[:, :half])
        keys.append(projected[:, half : 2 * half])
        values.append(projected[:, 2 * half :])
    query, key = jnp.concatenate(queries, axis=1), jnp.concatenate(keys, axis=1)
    cosine, sine = cosine[...], sine[...]
    query = (query * cosine + rotated(query) * sine).astype(bf16)
    key = (key * cosine + rotated(key) * sine).astype(bf16)
    query_ref[...] = query * jnp.asarray(HEAD_DIM**-0.5, bf16)
    pair_ref[:, : 2 * half] = key
    pair_ref[:, 2 * half :] = jnp.concatenate(values, axis=1).astype(bf16)


def attend(parts, at, query_ref, *refs):
    pieces, (context_ref, pairs_ref, total_ref) = refs[:parts], refs[parts:]
    start = 0
    for piece in pieces:
        pairs_ref[start : start + piece.shape[0], :] = piece[...]
        start += piece.shape[0]
    width = query_ref.shape[1]
    values = pairs_ref[:, width:].T
    contexts = []
    for h in range(width // HEAD_DIM):
        lanes = slice(h * HEAD_DIM, (h + 1) * HEAD_DIM)
        scores = mm_nt(pairs_ref[:, lanes], query_ref[:, lanes])
        peak = jnp.max(scores, axis=0, keepdims=True)
        log_total = peak + jnp.log(jnp.sum(jnp.exp(scores - peak), axis=0, keepdims=True))
        probs = jnp.exp(scores - log_total).astype(bf16)
        contexts.append(mm(values[lanes], probs))
        total_ref[h : h + 1, :] = log_total
    context_ref[...] = jnp.concatenate(contexts, axis=0).T.astype(bf16)


def feed(chips, count, at, *refs):
    contexts, refs = refs[: len(chips)], refs[len(chips) :]
    weights, refs = both_cores(count, at, refs)
    (out_own, out_other, rows_ref, grad_ref, gains), refs = refs[:5], refs[5:]
    (middle_ref, middle_rows_ref, normed_ref, unit_ref, active_ref, gain_ref, total_ref), refs = refs[:7], refs[7:]
    pieces, scratch = refs[:-1], refs[-1]
    hidden = active_ref.shape[2]
    block, span = middle_ref.shape
    part = total_ref.shape[0]
    middle = rows_ref[...].astype(f32)
    for p, (k, s) in enumerate(chips):
        context = contexts[p][...]
        if s:
            context = jnp.concatenate([context[block:], context[:block]], axis=0)
        middle = middle + mm_nt(context, jnp.concatenate([out_own[p], out_other[p]], axis=1))
    scratch[...] = middle
    middle_ref[...] = scratch[:block, aligned(at[0], span)]
    middle_rows_ref[...] = scratch[aligned(at[0], part), :]
    centred, _ = norm_rows(middle)
    normed_ref[...] = (centred * gains[1:2, :]).astype(bf16)
    scratch[...] = jnp.zeros_like(scratch)
    for b, (weight, starts) in enumerate(weights):
        gate_up = contract(normed_ref, weight, starts, slice(0, 2 * hidden))
        gate, lift = gate_up[:, :hidden], gate_up[:, hidden:]
        share = 0.5 + 0.5 * lax.erf(gate * math.sqrt(0.5))
        bent = gate * share
        active_ref[b] = (bent * lift).astype(bf16)
        slope = share + gate * jnp.exp(-0.5 * gate * gate) * (1.0 / math.sqrt(2.0 * math.pi))
        back = contract(grad_ref, weight, starts, slice(2 * hidden, 3 * hidden))
        unit = jnp.concatenate([back * lift * slope, back * bent], axis=1).astype(bf16)
        unit_ref[b] = unit
        spread(scratch, unit, weight, starts, slice(0, 2 * hidden))
    gain_ref[...] = jnp.sum(scratch[...] * centred, axis=0, keepdims=True)
    cut_rows(chips, at, scratch, total_ref, pieces)


def cut_rows(chips, at, scratch, total_ref, pieces):
    part = total_ref.shape[0]
    columns = scratch.shape[0] // (2 * part)
    for p, (k, s) in enumerate(chips):
        rows = scratch[aligned(s * columns + (at[0] ^ k), part), :]
        if p:
            pieces[p - 1][...] = rows.astype(bf16)
        else:
            total_ref[...] = rows


def turn(at, total_ref, *refs):
    pieces, (middle_ref, grad_ref, gains, grad_middle_ref, low_ref) = refs[:-5], refs[-5:]
    part = total_ref.shape[0]
    total = total_ref[...]
    for piece in pieces:
        total = total + piece[...].astype(f32)
    centred, inverse = norm_rows(middle_ref[...])
    grad = grad_ref[aligned(at[0], part), :].astype(f32)
    grad = grad + norm_backward(total, centred, inverse, gains[1:2, :])
    grad_middle_ref[...] = grad
    low_ref[...] = grad.astype(bf16)


def settle(chips, count, at, *refs):
    weights, refs = both_cores(count, at, refs)
    (normed_ref, unit_ref, active_ref, grad_ref, middle_ref), refs = refs[:5], refs[5:]
    (own_ref, other_ref, total_ref), refs = refs[:3], refs[3:]
    pieces, scratch = refs[:-1], refs[-1]
    hidden = active_ref.shape[2]
    block, span = total_ref.shape
    normed, grad = normed_ref[...].T, grad_ref[...].T
    for b, out in enumerate((other_ref, own_ref)):
        out[:, : 2 * hidden] = mm(normed, unit_ref[1 - b]).astype(bf16)
        out[:, 2 * hidden : 3 * hidden] = mm(grad, active_ref[1 - b]).astype(bf16)
        if out.shape[1] > 3 * hidden:
            out[:, 3 * hidden :] = jnp.zeros((out.shape[0], out.shape[1] - 3 * hidden), bf16)
    scratch[...] = jnp.zeros_like(scratch)
    for b, (weight, starts) in enumerate(weights):
        spread(scratch, active_ref[b], weight, starts, slice(2 * hidden, 3 * hidden))
    for p, (k, s) in enumerate(chips):
        piece = scratch[s * block : (s + 1) * block, aligned(at[0] ^ k, span)]
        if p:
            pieces[p - 1][...] = piece.astype(bf16)
        else:
            total_ref[...] = piece + middle_ref[...]


def reflect(chips, count, at, *refs):
    pieces, refs = refs[: len(chips)], refs[len(chips) :]
    weights, refs = both_cores(count, at, refs)
    query_ref, pairs_ref, total_ref, grad_attn_ref, grad_query_ref, grad_pairs_ref = refs
    part = pieces[0].shape[0]
    rows, width = query_ref.shape
    columns = rows // (2 * part)
    half = width // 2
    for (k, s), piece in zip(chips, pieces):
        grad_attn_ref[aligned(s * columns + (at[0] ^ k), part), :] = piece[...]
    grad_context = jnp.concatenate(
        [contract(grad_attn_ref, weight, starts, slice(3 * half, 4 * half)) for weight, starts in weights],
        axis=1,
    ).astype(bf16)
    keys = pairs_ref[:, :width].T
    grad_queries = []
    for h in range(width // HEAD_DIM):
        lanes = slice(h * HEAD_DIM, (h + 1) * HEAD_DIM)
        query = query_ref[:, lanes]
        grad = grad_context[:, lanes]
        probs = jnp.exp(mm_nt(pairs_ref[:, lanes], query) - total_ref[h : h + 1, :])
        value_lanes = slice(width + h * HEAD_DIM, width + (h + 1) * HEAD_DIM)
        grad_probs = mm_nt(pairs_ref[:, value_lanes], grad)
        delta = jnp.sum(probs * grad_probs, axis=0, keepdims=True)
        grad_scores = (probs * (grad_probs - delta)).astype(bf16)
        grad_pairs_ref[:, lanes] = mm(grad_scores, query).astype(bf16)
        grad_pairs_ref[:, value_lanes] = mm(probs.astype(bf16), grad).astype(bf16)
        grad_queries.append(mm(keys[lanes], grad_scores))
    grad_query_ref[...] = jnp.concatenate(grad_queries, axis=0).T * HEAD_DIM**-0.5


def unwind(chips, count, at, *refs):
    weights, refs = both_cores(count, at, refs)
    (grad_query_ref, grad_pairs_ref, cosine, sine, rows_ref), refs = refs[:5], refs[5:]
    (grad_projected_ref, gain_ref, total_ref), refs = refs[:3], refs[3:]
    pieces, scratch = refs[:-1], refs[-1]
    width = grad_query_ref.shape[1]
    half = width // 2
    cosine, sine = cosine[...], sine[...]
    grad_query, grad_key = grad_query_ref[...], grad_pairs_ref[:, :width]
    grad_query = (grad_query * cosine - rotated(grad_query * sine)).astype(bf16)
    grad_key = (grad_key * cosine - rotated(grad_key * sine)).astype(bf16)
    grad_value = grad_pairs_ref[:, width:].astype(bf16)
    scratch[...] = jnp.zeros_like(scratch)
    for b, (weight, starts) in enumerate(weights):
        lanes = slice(b * half, (b + 1) * half)
        grad = jnp.concatenate([grad_query[:, lanes], grad_key[:, lanes], grad_value[:, lanes]], axis=1)
        grad_projected_ref[b] = grad
        spread(scratch, grad, weight, starts, slice(0, 3 * half))
    centred, _ = norm_rows(rows_ref[...].astype(f32))
    gain_ref[...] = jnp.sum(scratch[...] * centred, axis=0, keepdims=True)
    cut_rows(chips, at, scratch, total_ref, pieces)


def repay(at, normed_ref, grad_projected_ref, grad_attn_ref, context_ref, own_ref, other_ref):
    half = context_ref.shape[1] // 2
    normed, grad_attn = normed_ref[...].T, grad_attn_ref[...].T
    for b, out in ((1, other_ref), (0, own_ref)):
        out[:, : 3 * half] = mm(normed, grad_projected_ref[b]).astype(bf16)
        out[:, 3 * half :] = mm(grad_attn, context_ref[:, b * half : (b + 1) * half]).astype(bf16)


def finish(narrow, at, total_ref, *refs):
    pieces, (rows_ref, grad_middle_ref, gains), outs, scratch = refs[: -narrow - 4], refs[-narrow - 4 : -narrow - 1], refs[-narrow - 1 : -1], refs[-1]
    part = total_ref.shape[0]
    width = outs[0].shape[1]
    total = total_ref[...]
    for piece in pieces:
        total = total + piece[...].astype(f32)
    centred, inverse = norm_rows(rows_ref[aligned(at[0], part), :].astype(f32))
    scratch[...] = grad_middle_ref[...] + norm_backward(total, centred, inverse, gains[0:1, :])
    for m, out in enumerate(outs):
        out[...] = scratch[:, aligned(at[1] ^ m, width)]


def body(
    wide,
    narrow,
    inputs,
    attn_gain,
    query_key_value_weight,
    attention_out_weight,
    mlp_gain,
    feedforward_in_weight,
    feedforward_out_weight,
    grad_out,
):
    groups, columns = wide // 2, narrow // 2
    _, block, width = inputs.shape
    model = width * narrow
    depth = query_key_value_weight.shape[0]
    hidden = feedforward_out_weight.shape[0] // 2
    half, span = width // 2, 2 * width
    part = block // columns
    rows = 2 * block
    length = groups * rows
    wide_at, narrow_at = lax.axis_index("wide"), lax.axis_index("narrow")
    group, side = wide_at // 2, wide_at % 2
    column, core = narrow_at // 2, narrow_at % 2
    chips = [(k, s) for s in range(2) for k in range(columns)]

    unit_mask = 2 * narrow

    def swap(array, mask):
        if mask == 0:
            return array
        return lax.ppermute(
            array, ("wide", "narrow"), [(i, i ^ mask) for i in range(wide * narrow)]
        )

    def over_chips(column_rel, side_rel):
        return 2 * column_rel + narrow * side_rel

    def over_groups(group_rel):
        return 2 * narrow * group_rel

    def after(array, *others):
        return lax.optimization_barrier((array, *others))[0]

    def swap_ways(array, even, odd):
        pairs = [(i, i ^ (odd if i % 2 else even)) for i in range(wide * narrow)]
        return lax.ppermute(array, ("wide", "narrow"), pairs)

    def ring_order(count):
        if count < 4:
            return list(range(count))
        quad = [0, 1 + 2 * core, 3 - 2 * core, 2]
        return [low + 4 * high for high in ring_order(count // 4) for low in quad]

    def other_way(relative):
        turned, unit = relative, 1
        while 4 * unit <= groups:
            turned, unit = turned ^ (2 * unit * ((relative // unit) % 2)), 4 * unit
        return turned

    def ring_first(array, unit):
        return swap_ways(array, unit, 3 * unit), swap_ways(array, 3 * unit, unit)

    def ring_last(second, unit):
        return swap_ways(second, unit, 3 * unit)

    def gather_ring(array, unit, count):
        if count < 4:
            return [swap(array, unit * k) for k in range(count)]
        first, second = ring_first(array, unit)
        quad = [array, first, second, ring_last(second, unit)]
        if count == 4:
            return quad
        return [q for quads in gather_ring(jnp.stack(quad), 4 * unit, count // 4) for q in quads]

    def scatter_first(pieces, unit):
        count = len(pieces)
        if count < 4:
            return pieces, None
        if count > 4:
            stacked = [jnp.stack(pieces[k : k + 4]) for k in range(0, count, 4)]
            pieces = list(scatter_ring(stacked, 4 * unit))
        own, first, second, across = pieces
        passing = swap_ways(across.astype(bf16), unit, 3 * unit)
        arrived = swap_ways(first.astype(bf16), unit, 3 * unit)
        return own, (second, passing, arrived)

    def scatter_last(own, state, unit):
        if state is None:
            total = own[0].astype(f32)
            for k in range(1, len(own)):
                total = total + swap(own[k].astype(bf16), unit * k).astype(f32)
            return total
        second, passing, arrived = state
        second = (second.astype(f32) + passing.astype(f32)).astype(bf16)
        return own.astype(f32) + arrived.astype(f32) + swap_ways(second, 3 * unit, unit).astype(f32)

    def scatter_ring(pieces, unit):
        return scatter_last(*scatter_first(pieces, unit), unit)

    def place_groups(pieces, order):
        size = pieces[0].shape[0]
        whole = jnp.zeros((size * groups, pieces[0].shape[1]), pieces[0].dtype)
        for relative, piece in zip(order, pieces):
            whole = lax.dynamic_update_slice_in_dim(whole, piece, (group ^ relative) * size, 0)
        return whole

    def fetch_side(bundle):
        received = swap(pick(bundle, 1 - side), narrow)
        return place([pick(bundle, side), received], side, 0)

    def halves(array):
        return array.reshape(depth, -1, 2, array.shape[-1] // 2).transpose(2, 0, 1, 3)

    def from_chips(array):
        return [swap(array, over_chips(k, s)) for k, s in chips]

    def to_chips(pieces):
        return [swap(piece, over_chips(k, s)) for (k, s), piece in zip(chips[1:], pieces)]

    def reduce_cores(own, other, *others):
        received = after(swap(other, 1), *others)

        def places(*later):
            blocks = []
            for place_at, k in enumerate(ring_order(groups)):
                pair = (own, received)
                if later and place_at % 2 == 0:
                    pair = lax.optimization_barrier((own, received, *later))[:2]
                pair = [pick(array.reshape(groups, 2 * depth, -1), group ^ k).astype(f32) for array in pair]
                blocks.append(pair[0] + pair[1])
            return blocks

        return places

    def scatter_early(places, joined=False):
        if groups != 4:
            return scatter_first(places(), unit_mask)
        _, first, _, across = places()
        if joined:
            both_ways = jnp.stack([across.astype(bf16), first.astype(bf16)])
            both_ways = swap_ways(both_ways, unit_mask, 3 * unit_mask)
            return both_ways[0], both_ways[1]
        return swap_ways(across.astype(bf16), unit_mask, 3 * unit_mask), swap_ways(first.astype(bf16), unit_mask, 3 * unit_mask)

    def scatter_late(places, state, *later):
        if groups != 4:
            return scatter_last(*state, unit_mask)
        own, _, second, _ = places(*later)
        return scatter_last(own, (second, *state), unit_mask)

    def reduce_side(total):
        total = total.reshape(2, depth, -1)
        kept = pick(total, side)
        received = swap(pick(total, 1 - side).astype(bf16), narrow).astype(f32)
        return place([kept[None], received[None]], side, 0)

    def join(array):
        return array.transpose(1, 2, 0, 3).reshape(depth, array.shape[2], -1)

    attn_bundle = jnp.concatenate(
        [halves(query_key_value_weight), halves(attention_out_weight.T[:, None])], axis=2
    ).reshape(2, depth, 4 * half)
    mlp_bundle = jnp.concatenate(
        [halves(feedforward_in_weight), halves(feedforward_out_weight.T[:, None])], axis=2
    ).reshape(2, depth, 3 * hidden)
    lanes = -(-3 * hidden // 128) * 128
    mlp_bundle = jnp.pad(mlp_bundle, ((0, 0), (0, 0), (0, lanes - 3 * hidden)))

    both = jnp.stack([inputs, grad_out])
    received = swap(pick(both, 1 - core, 1), 1)
    features = place([pick(both, core, 1), received], core, 2)
    attn_pair = fetch_side(attn_bundle)
    shards = from_chips(features)
    gains = after(jnp.stack([attn_gain, mlp_gain]), shards)
    gains = place([gains, swap(gains, 1)], core, 1)
    gains = place([swap(gains, 2 * k) for k in range(columns)], column, 1)
    mlp_pair = fetch_side(after(mlp_bundle, attn_pair))
    if groups >= 4:
        quad = [attn_pair, *ring_first(attn_pair, unit_mask)]
        quad, shards, mlp_pair = lax.optimization_barrier((quad, shards, mlp_pair))
        quad.append(ring_last(quad[2], unit_mask))
        if groups > 4:
            quad = [q for quads in gather_ring(jnp.stack(quad), 4 * unit_mask, groups // 4) for q in quads]
    else:
        quad = gather_ring(attn_pair, unit_mask, groups)
    order = ring_order(groups)
    turned = [other_way(k) for k in order]
    count = groups if 2 * depth % 128 == 0 else 1
    starts = [group ^ k for k in order] + [group ^ k for k in turned] if count > 1 else [0, 0]

    def both_blocks(own, other):
        return [*own, *other] if count > 1 else [place_groups(own, order), place_groups(other, turned)]

    token = (jnp.arange(rows) // block) ^ side
    positions = ((group * 2 + token) * block + jnp.arange(rows) % block).astype(f32)
    cosine, sine = rope_tables(positions, width)
    at = jnp.stack([column, narrow_at, *starts]).astype(jnp.int32)
    early = [swap(piece, 1) for piece in quad[:3]]
    gains, quad, early, cosine, sine, at = lax.optimization_barrier((gains, quad, early, cosine, sine, at))
    attn_weights = both_blocks(quad, [*early, *[swap(piece, 1) for piece in quad[len(early) :]]])
    mlp_quad = [mlp_pair, *ring_first(mlp_pair, unit_mask)] if groups >= 4 else []

    if groups >= 4:
        gains, mlp_quad[1] = lax.optimization_barrier((gains, mlp_quad[1]))
    rows_in, grad_rows, normed_one, query, pair = call(
        functools.partial(project, chips, count),
        [((rows, model), bf16)] * 3 + [((rows, width), bf16), ((rows, span), bf16)],
        at, *shards, *attn_weights, gains, cosine, sine,
    )
    out_own = place_groups([after(piece[:, 3 * half :], pair) for piece in quad], order)
    out_own = from_chips(out_own)
    if groups == 4:
        (first, second), mlp_quad, out_own = lax.optimization_barrier((ring_first(pair, unit_mask), mlp_quad, out_own))
        pairs = [pair, first, second, ring_last(second, unit_mask)]
    else:
        pairs = gather_ring(pair, unit_mask, groups)
    pairs, out_own, early = lax.optimization_barrier((pairs, out_own, mlp_quad))
    early = [swap(piece, 1) for piece in early]
    out_own = jnp.stack(out_own)
    out_other = swap(out_own, 1)
    if groups >= 4:
        mlp_quad.append(ring_last(after(mlp_quad[2], pairs), unit_mask))
    context, pairs, total = call(
        functools.partial(attend, len(pairs)),
        [((rows, width), bf16), ((length, span), bf16), ((8, rows), f32)],
        at, query, *pairs,
    )
    contexts = from_chips(context)
    if groups >= 4:
        late = after(mlp_quad.pop(), contexts)
        mlp_quad, early = [*mlp_quad, late], [*early, swap(late, 1)]
        if groups > 4:
            mlp_quad = [q for quads in gather_ring(jnp.stack(mlp_quad), 4 * unit_mask, groups // 4) for q in quads]
            early = [swap(piece, 1) for piece in mlp_quad]
    else:
        mlp_quad = gather_ring(mlp_pair, unit_mask, groups)
        early = [swap(piece, 1) for piece in mlp_quad]
    mlp_weights = both_blocks(mlp_quad, early)
    middle, middle_rows, normed_two, unit, active, mlp_gain_part, grad_two, *sends = call(
        functools.partial(feed, chips, count),
        [((block, span), f32), ((part, model), f32), ((rows, model), bf16), ((2, rows, 2 * hidden), bf16),
         ((2, rows, hidden), bf16), ((1, model), f32), ((part, model), f32)] + [((part, model), bf16)] * (len(chips) - 1),
        at, *contexts, *mlp_weights, out_own, out_other, rows_in, grad_rows, gains,
        scratch=[((rows, model), f32)],
    )
    received = to_chips(sends)
    grad_mlp_own, grad_mlp_other, branch, *branch_sends = call(
        functools.partial(settle, chips, count),
        [((model, lanes), bf16)] * 2 + [((block, span), f32)] + [((block, span), bf16)] * (len(chips) - 1),
        at, *mlp_weights, normed_two, unit, active, grad_rows, middle,
        scratch=[((rows, model), f32)],
    )
    grad_mlp_other = after(grad_mlp_other, received)
    grad_middle, grad_low = call(
        functools.partial(turn), [((part, model), f32), ((part, model), bf16)],
        at, grad_two, *received, middle_rows, grad_rows, gains,
    )
    grad_pieces = from_chips(grad_low)
    grad_mlp = reduce_cores(grad_mlp_own, grad_mlp_other, grad_low)
    mlp_state = scatter_early(grad_mlp)
    grad_attn, grad_query, grad_pairs = call(
        functools.partial(reflect, chips, count),
        [((rows, model), bf16), ((rows, width), f32), ((length, span), bf16)],
        at, *grad_pieces, *attn_weights, query, pairs, total,
    )
    if groups >= 4:
        mlp_state, grad_pairs, branch_sends = lax.optimization_barrier((mlp_state, grad_pairs, branch_sends))
    grad_pairs = scatter_ring(list(grad_pairs.reshape(groups, rows, span)), unit_mask)

    branch_received = to_chips(branch_sends)
    grad_pairs, mlp_state, branch_received = lax.optimization_barrier((grad_pairs, mlp_state, branch_received))
    for piece in branch_received:
        branch = branch + piece.astype(f32)
    branch = branch.astype(bf16).reshape(block, 2, width)
    result = place([pick(branch, core, 1)[None], swap(pick(branch, 1 - core, 1), 1)[None]], core, 0)

    grad_mlp = scatter_late(grad_mlp, mlp_state, grad_query)
    grad_projected, attn_gain_part, grad_one, *sends = call(
        functools.partial(unwind, chips, count),
        [((2, rows, 3 * half), bf16), ((1, model), f32), ((part, model), f32)] + [((part, model), bf16)] * (len(chips) - 1),
        at, *attn_weights, grad_query, grad_pairs, cosine, sine, rows_in,
        scratch=[((rows, model), f32)],
    )
    received = to_chips(sends)
    grad_attn_own, grad_attn_other = call(
        functools.partial(repay), [((model, 4 * half), bf16)] * 2,
        at, normed_one, grad_projected, grad_attn, context,
    )
    grad_attn_other, grad_mlp, received = lax.optimization_barrier((grad_attn_other, grad_mlp, received))
    attn_places = reduce_cores(grad_attn_own, grad_attn_other)
    summed = [piece.astype(bf16) for piece in attn_places()[1::2]]
    state = scatter_early(attn_places, joined=True)
    finished = call(
        functools.partial(finish, narrow), [((part, width), f32)] * narrow,
        at, after(grad_one, *summed), *received, rows_in, grad_middle, gains,
        scratch=[((part, model), f32)],
    )
    sends = [swap(piece, m) for m, piece in enumerate(finished)]
    gain_grads = jnp.concatenate([after(attn_gain_part, finished[0]), mlp_gain_part], axis=0).reshape(2, narrow, width)
    gain_total = pick(gain_grads, narrow_at, 1)
    for m in range(1, narrow):
        gain_total = gain_total + swap(pick(gain_grads, narrow_at ^ m, 1), m)
    gain_total = gain_total + swap(gain_total, narrow)
    sends, state, gain_total = lax.optimization_barrier((sends, state, gain_total))
    grad_mlp = after(grad_mlp, *summed)
    grad_mlp = join(reduce_side(grad_mlp)[..., : 3 * hidden].reshape(2, depth, 3, hidden))
    grad_attn_weight = scatter_late(attn_places, state, finished[0])
    gain_total = after(gain_total, grad_mlp)
    if groups == 4:
        near, across, far = [swap(gain_total, unit_mask * k) for k in (1, 2, 3)]
        gain_total = (gain_total + near) + (across + far)
    else:
        for mask in ring_masks(groups):
            gain_total = gain_total + swap(gain_total, unit_mask * mask)
    grad_attn_weight, gain_total = lax.optimization_barrier((grad_attn_weight, gain_total))
    grad_attn_weight = join(reduce_side(grad_attn_weight).reshape(2, depth, 4, half))
    grad_inputs = place(
        [place([sends[2 * k + c] for k in range(columns)], column, 0)[None] for c in range(2)],
        core, 0,
    )
    return (
        result,
        grad_inputs,
        gain_total[0],
        grad_attn_weight[:, :3],
        grad_attn_weight[:, 3].T,
        gain_total[1],
        grad_mlp[:, :2],
        grad_mlp[:, 2].T,
    )


def solution(mesh):
    in_specs = (
        P(None, "wide", "narrow"),
        P("narrow"),
        P("wide", None, "narrow"),
        P("narrow", "wide"),
        P("narrow"),
        P("wide", None, "narrow"),
        P("narrow", "wide"),
        P(None, "wide", "narrow"),
    )
    out_specs = (
        P(None, "wide", "narrow"),
        P(None, "wide", "narrow"),
        P("narrow"),
        P("wide", None, "narrow"),
        P("narrow", "wide"),
        P("narrow"),
        P("wide", None, "narrow"),
        P("narrow", "wide"),
    )
    step = functools.partial(body, mesh.shape["wide"], mesh.shape["narrow"])
    return jax.shard_map(step, mesh=mesh, in_specs=in_specs, out_specs=out_specs, check_vma=False)
```

```python
import functools
import math

import jax
import jax.numpy as jnp
from jax import lax
from jax.experimental import pallas as pl
from jax.experimental.pallas import tpu as pltpu
from jax.sharding import PartitionSpec as P

HEAD_DIM = 64
eps_norm = 1e-05
rope_base = 160000.0
f32 = jnp.float32
bf16 = jnp.bfloat16


def mm(a, b):
    return lax.dot_general(a, b, (((1,), (0,)), ((), ())), preferred_element_type=f32)


def mm_nt(a, b):
    return lax.dot_general(a, b, (((1,), (1,)), ((), ())), preferred_element_type=f32)


def aligned(index, size):
    return pl.ds(pl.multiple_of(index * size, size), size)


def norm_rows(rows):
    width = rows.shape[-1]
    average = jnp.sum(rows, axis=-1, keepdims=True) / width
    variance = jnp.sum(rows * rows, axis=-1, keepdims=True) / width - average * average
    inverse = lax.rsqrt(variance + eps_norm)
    return (rows - average) * inverse, inverse


def norm_backward(grad_normed, centred, inverse, gain):
    width = grad_normed.shape[-1]
    scaled = grad_normed * gain
    row_total = jnp.sum(scaled, axis=-1, keepdims=True)
    row_along = jnp.sum(scaled * centred, axis=-1, keepdims=True)
    return inverse * (scaled - row_total / width - centred * (row_along / width))


def rope_tables(positions, lanes):
    half_dim = HEAD_DIM // 2
    frequency = rope_base ** (-jnp.arange(half_dim).astype(f32) * 2.0 / HEAD_DIM)
    angles = positions[:, None] * frequency[None, :]
    angles = jnp.concatenate([angles, angles] * (lanes // HEAD_DIM), axis=-1)
    return jnp.cos(angles), jnp.sin(angles)


def rotated(tensor):
    lanes, half_dim = tensor.shape[-1], HEAD_DIM // 2
    lane = lax.broadcasted_iota(jnp.int32, tensor.shape, 1)
    up = pltpu.roll(tensor, half_dim, 1)
    down = pltpu.roll(tensor, lanes - half_dim, 1)
    return jnp.where(lane % HEAD_DIM < half_dim, -down, up)


def call(kernel, outs, at, *arrays, scratch=()):
    return pl.pallas_call(
        kernel,
        out_shape=[jax.ShapeDtypeStruct(shape, dtype) for shape, dtype in outs],
        in_specs=[pl.BlockSpec(memory_space=pltpu.SMEM)]
        + [pl.BlockSpec(memory_space=pltpu.VMEM)] * len(arrays),
        out_specs=[pl.BlockSpec(memory_space=pltpu.VMEM)] * len(outs),
        scratch_shapes=[pltpu.VMEM(shape, dtype) for shape, dtype in scratch],
        compiler_params=pltpu.CompilerParams(vmem_limit_bytes=60 * 1024 * 1024),
        name=kernel.func.__name__,
    )(at, *arrays)


def ring_masks(count):
    masks, unit = [], 1
    while unit < count:
        masks += [unit] + ([3 * unit] if 4 * unit <= count else [])
        unit *= 4
    return masks


def pick(array, index, axis=0):
    return lax.dynamic_index_in_dim(array, index, axis=axis, keepdims=False)


def place(pieces, own, axis):
    count = len(pieces)
    if count == 1:
        return pieces[0]
    if count == 2:
        return jnp.where(
            own == 0,
            jnp.concatenate(pieces, axis=axis),
            jnp.concatenate(pieces[::-1], axis=axis),
        )
    size = pieces[0].shape[axis]
    shape = list(pieces[0].shape)
    shape[axis] = size * count
    whole = jnp.zeros(shape, pieces[0].dtype)
    for relative, piece in enumerate(pieces):
        whole = lax.dynamic_update_slice_in_dim(whole, piece, (own ^ relative) * size, axis)
    return whole


def contract(rows_ref, pieces, starts, lanes):
    total = 0.0
    for piece, start in zip(pieces, starts):
        total = total + mm(rows_ref[:, aligned(start, piece.shape[0])], piece[:, lanes])
    return total


def spread(out_ref, array, pieces, starts, lanes):
    for piece, start in zip(pieces, starts):
        out_ref[:, aligned(start, piece.shape[0])] += mm_nt(array, piece[:, lanes])


def both_cores(count, at, refs):
    first = [at[2 + p] for p in range(count)]
    second = [at[2 + count + p] for p in range(count)]
    return ((refs[:count], first), (refs[count : 2 * count], second)), refs[2 * count :]


def project(chips, count, at, *refs):
    shards, refs = refs[: len(chips)], refs[len(chips) :]
    weights, refs = both_cores(count, at, refs)
    gains, cosine, sine, rows_ref, grad_ref, normed_ref, query_ref, pair_ref = refs
    block, span = shards[0].shape[1:]
    half = query_ref.shape[1] // 2
    for (k, s), shard in zip(chips, shards):
        lanes = aligned(at[0] ^ k, span)
        rows_ref[s * block : (s + 1) * block, lanes] = shard[0]
        grad_ref[s * block : (s + 1) * block, lanes] = shard[1]
    centred, _ = norm_rows(rows_ref[...].astype(f32))
    normed_ref[...] = (centred * gains[0:1, :]).astype(bf16)
    queries, keys, values = [], [], []
    for pieces, starts in weights:
        projected = contract(normed_ref, pieces, starts, slice(0, 3 * half))
        queries.append(projected[:, :half])
        keys.append(projected[:, half : 2 * half])
        values.append(projected[:, 2 * half :])
    query, key = jnp.concatenate(queries, axis=1), jnp.concatenate(keys, axis=1)
    cosine, sine = cosine[...], sine[...]
    query = (query * cosine + rotated(query) * sine).astype(bf16)
    key = (key * cosine + rotated(key) * sine).astype(bf16)
    query_ref[...] = query * jnp.asarray(HEAD_DIM**-0.5, bf16)
    pair_ref[:, : 2 * half] = key
    pair_ref[:, 2 * half :] = jnp.concatenate(values, axis=1).astype(bf16)


def attend(parts, at, query_ref, *refs):
    pieces, (context_ref, pairs_ref, total_ref) = refs[:parts], refs[parts:]
    start = 0
    for piece in pieces:
        pairs_ref[start : start + piece.shape[0], :] = piece[...]
        start += piece.shape[0]
    width = query_ref.shape[1]
    values = pairs_ref[:, width:].T
    contexts = []
    for h in range(width // HEAD_DIM):
        lanes = slice(h * HEAD_DIM, (h + 1) * HEAD_DIM)
        scores = mm_nt(pairs_ref[:, lanes], query_ref[:, lanes])
        peak = jnp.max(scores, axis=0, keepdims=True)
        log_total = peak + jnp.log(jnp.sum(jnp.exp(scores - peak), axis=0, keepdims=True))
        probs = jnp.exp(scores - log_total).astype(bf16)
        contexts.append(mm(values[lanes], probs))
        total_ref[h : h + 1, :] = log_total
    context_ref[...] = jnp.concatenate(contexts, axis=0).T.astype(bf16)


def feed(chips, count, at, *refs):
    contexts, refs = refs[: len(chips)], refs[len(chips) :]
    weights, refs = both_cores(count, at, refs)
    (out_own, out_other, rows_ref, grad_ref, gains), refs = refs[:5], refs[5:]
    (middle_ref, middle_rows_ref, normed_ref, unit_ref, active_ref, gain_ref, total_ref), refs = refs[:7], refs[7:]
    pieces, scratch = refs[:-1], refs[-1]
    hidden = active_ref.shape[2]
    block, span = middle_ref.shape
    part = total_ref.shape[0]
    middle = rows_ref[...].astype(f32)
    for p, (k, s) in enumerate(chips):
        context = contexts[p][...]
        if s:
            context = jnp.concatenate([context[block:], context[:block]], axis=0)
        middle = middle + mm_nt(context, jnp.concatenate([out_own[p], out_other[p]], axis=1))
    scratch[...] = middle
    middle_ref[...] = scratch[:block, aligned(at[0], span)]
    middle_rows_ref[...] = scratch[aligned(at[0], part), :]
    centred, _ = norm_rows(middle)
    normed_ref[...] = (centred * gains[1:2, :]).astype(bf16)
    scratch[...] = jnp.zeros_like(scratch)
    for b, (weight, starts) in enumerate(weights):
        gate_up = contract(normed_ref, weight, starts, slice(0, 2 * hidden))
        gate, lift = gate_up[:, :hidden], gate_up[:, hidden:]
        share = 0.5 + 0.5 * lax.erf(gate * math.sqrt(0.5))
        bent = gate * share
        active_ref[b] = (bent * lift).astype(bf16)
        slope = share + gate * jnp.exp(-0.5 * gate * gate) * (1.0 / math.sqrt(2.0 * math.pi))
        back = contract(grad_ref, weight, starts, slice(2 * hidden, 3 * hidden))
        unit = jnp.concatenate([back * lift * slope, back * bent], axis=1).astype(bf16)
        unit_ref[b] = unit
        spread(scratch, unit, weight, starts, slice(0, 2 * hidden))
    gain_ref[...] = jnp.sum(scratch[...] * centred, axis=0, keepdims=True)
    cut_rows(chips, at, scratch, total_ref, pieces)


def cut_rows(chips, at, scratch, total_ref, pieces):
    part = total_ref.shape[0]
    columns = scratch.shape[0] // (2 * part)
    for p, (k, s) in enumerate(chips):
        rows = scratch[aligned(s * columns + (at[0] ^ k), part), :]
        if p:
            pieces[p - 1][...] = rows.astype(bf16)
        else:
            total_ref[...] = rows


def turn(at, total_ref, *refs):
    pieces, (middle_ref, grad_ref, gains, grad_middle_ref, low_ref) = refs[:-5], refs[-5:]
    part = total_ref.shape[0]
    total = total_ref[...]
    for piece in pieces:
        total = total + piece[...].astype(f32)
    centred, inverse = norm_rows(middle_ref[...])
    grad = grad_ref[aligned(at[0], part), :].astype(f32)
    grad = grad + norm_backward(total, centred, inverse, gains[1:2, :])
    grad_middle_ref[...] = grad
    low_ref[...] = grad.astype(bf16)


def settle(chips, count, at, *refs):
    weights, refs = both_cores(count, at, refs)
    (normed_ref, unit_ref, active_ref, grad_ref, middle_ref), refs = refs[:5], refs[5:]
    (own_ref, other_ref, total_ref), refs = refs[:3], refs[3:]
    pieces, scratch = refs[:-1], refs[-1]
    hidden = active_ref.shape[2]
    block, span = total_ref.shape
    normed, grad = normed_ref[...].T, grad_ref[...].T
    for b, out in enumerate((other_ref, own_ref)):
        out[:, : 2 * hidden] = mm(normed, unit_ref[1 - b]).astype(bf16)
        out[:, 2 * hidden : 3 * hidden] = mm(grad, active_ref[1 - b]).astype(bf16)
        if out.shape[1] > 3 * hidden:
            out[:, 3 * hidden :] = jnp.zeros((out.shape[0], out.shape[1] - 3 * hidden), bf16)
    scratch[...] = jnp.zeros_like(scratch)
    for b, (weight, starts) in enumerate(weights):
        spread(scratch, active_ref[b], weight, starts, slice(2 * hidden, 3 * hidden))
    for p, (k, s) in enumerate(chips):
        piece = scratch[s * block : (s + 1) * block, aligned(at[0] ^ k, span)]
        if p:
            pieces[p - 1][...] = piece.astype(bf16)
        else:
            total_ref[...] = piece + middle_ref[...]


def reflect(chips, count, at, *refs):
    pieces, refs = refs[: len(chips)], refs[len(chips) :]
    weights, refs = both_cores(count, at, refs)
    query_ref, pairs_ref, total_ref, grad_attn_ref, grad_query_ref, grad_pairs_ref = refs
    part = pieces[0].shape[0]
    rows, width = query_ref.shape
    columns = rows // (2 * part)
    half = width // 2
    for (k, s), piece in zip(chips, pieces):
        grad_attn_ref[aligned(s * columns + (at[0] ^ k), part), :] = piece[...]
    grad_context = jnp.concatenate(
        [contract(grad_attn_ref, weight, starts, slice(3 * half, 4 * half)) for weight, starts in weights],
        axis=1,
    ).astype(bf16)
    keys = pairs_ref[:, :width].T
    grad_queries = []
    for h in range(width // HEAD_DIM):
        lanes = slice(h * HEAD_DIM, (h + 1) * HEAD_DIM)
        query = query_ref[:, lanes]
        grad = grad_context[:, lanes]
        probs = jnp.exp(mm_nt(pairs_ref[:, lanes], query) - total_ref[h : h + 1, :])
        value_lanes = slice(width + h * HEAD_DIM, width + (h + 1) * HEAD_DIM)
        grad_probs = mm_nt(pairs_ref[:, value_lanes], grad)
        delta = jnp.sum(probs * grad_probs, axis=0, keepdims=True)
        grad_scores = (probs * (grad_probs - delta)).astype(bf16)
        grad_pairs_ref[:, lanes] = mm(grad_scores, query).astype(bf16)
        grad_pairs_ref[:, value_lanes] = mm(probs.astype(bf16), grad).astype(bf16)
        grad_queries.append(mm(keys[lanes], grad_scores))
    grad_query_ref[...] = jnp.concatenate(grad_queries, axis=0).T * HEAD_DIM**-0.5


def unwind(chips, count, at, *refs):
    weights, refs = both_cores(count, at, refs)
    (grad_query_ref, grad_pairs_ref, cosine, sine, rows_ref), refs = refs[:5], refs[5:]
    (grad_projected_ref, gain_ref, total_ref), refs = refs[:3], refs[3:]
    pieces, scratch = refs[:-1], refs[-1]
    width = grad_query_ref.shape[1]
    half = width // 2
    cosine, sine = cosine[...], sine[...]
    grad_query, grad_key = grad_query_ref[...], grad_pairs_ref[:, :width]
    grad_query = (grad_query * cosine - rotated(grad_query * sine)).astype(bf16)
    grad_key = (grad_key * cosine - rotated(grad_key * sine)).astype(bf16)
    grad_value = grad_pairs_ref[:, width:].astype(bf16)
    scratch[...] = jnp.zeros_like(scratch)
    for b, (weight, starts) in enumerate(weights):
        lanes = slice(b * half, (b + 1) * half)
        grad = jnp.concatenate([grad_query[:, lanes], grad_key[:, lanes], grad_value[:, lanes]], axis=1)
        grad_projected_ref[b] = grad
        spread(scratch, grad, weight, starts, slice(0, 3 * half))
    centred, _ = norm_rows(rows_ref[...].astype(f32))
    gain_ref[...] = jnp.sum(scratch[...] * centred, axis=0, keepdims=True)
    cut_rows(chips, at, scratch, total_ref, pieces)


def repay(at, normed_ref, grad_projected_ref, grad_attn_ref, context_ref, own_ref, other_ref):
    half = context_ref.shape[1] // 2
    normed, grad_attn = normed_ref[...].T, grad_attn_ref[...].T
    for b, out in ((1, other_ref), (0, own_ref)):
        out[:, : 3 * half] = mm(normed, grad_projected_ref[b]).astype(bf16)
        out[:, 3 * half :] = mm(grad_attn, context_ref[:, b * half : (b + 1) * half]).astype(bf16)


def finish(narrow, at, total_ref, *refs):
    pieces, (rows_ref, grad_middle_ref, gains), outs, scratch = refs[: -narrow - 4], refs[-narrow - 4 : -narrow - 1], refs[-narrow - 1 : -1], refs[-1]
    part = total_ref.shape[0]
    width = outs[0].shape[1]
    total = total_ref[...]
    for piece in pieces:
        total = total + piece[...].astype(f32)
    centred, inverse = norm_rows(rows_ref[aligned(at[0], part), :].astype(f32))
    scratch[...] = grad_middle_ref[...] + norm_backward(total, centred, inverse, gains[0:1, :])
    for m, out in enumerate(outs):
        out[...] = scratch[:, aligned(at[1] ^ m, width)]


def body(
    wide,
    narrow,
    inputs,
    attn_gain,
    query_key_value_weight,
    attention_out_weight,
    mlp_gain,
    feedforward_in_weight,
    feedforward_out_weight,
    grad_out,
):
    groups, columns = wide // 2, narrow // 2
    _, block, width = inputs.shape
    model = width * narrow
    depth = query_key_value_weight.shape[0]
    hidden = feedforward_out_weight.shape[0] // 2
    half, span = width // 2, 2 * width
    part = block // columns
    rows = 2 * block
    length = groups * rows
    wide_at, narrow_at = lax.axis_index("wide"), lax.axis_index("narrow")
    group, side = wide_at // 2, wide_at % 2
    column, core = narrow_at // 2, narrow_at % 2
    chips = [(k, s) for s in range(2) for k in range(columns)]

    unit_mask = 2 * narrow

    def swap(array, mask):
        if mask == 0:
            return array
        return lax.ppermute(
            array, ("wide", "narrow"), [(i, i ^ mask) for i in range(wide * narrow)]
        )

    def over_chips(column_rel, side_rel):
        return 2 * column_rel + narrow * side_rel

    def over_groups(group_rel):
        return 2 * narrow * group_rel

    def after(array, *others):
        return lax.optimization_barrier((array, *others))[0]

    def swap_ways(array, even, odd):
        pairs = [(i, i ^ (odd if i % 2 else even)) for i in range(wide * narrow)]
        return lax.ppermute(array, ("wide", "narrow"), pairs)

    def ring_order(count):
        if count < 4:
            return list(range(count))
        quad = [0, 1 + 2 * core, 3 - 2 * core, 2]
        return [low + 4 * high for high in ring_order(count // 4) for low in quad]

    def other_way(relative):
        turned, unit = relative, 1
        while 4 * unit <= groups:
            turned, unit = turned ^ (2 * unit * ((relative // unit) % 2)), 4 * unit
        return turned

    def ring_first(array, unit):
        return swap_ways(array, unit, 3 * unit), swap_ways(array, 3 * unit, unit)

    def ring_last(second, unit):
        return swap_ways(second, unit, 3 * unit)

    def gather_ring(array, unit, count):
        if count < 4:
            return [swap(array, unit * k) for k in range(count)]
        first, second = ring_first(array, unit)
        quad = [array, first, second, ring_last(second, unit)]
        if count == 4:
            return quad
        return [q for quads in gather_ring(jnp.stack(quad), 4 * unit, count // 4) for q in quads]

    def scatter_first(pieces, unit):
        count = len(pieces)
        if count < 4:
            return pieces, None
        if count > 4:
            stacked = [jnp.stack(pieces[k : k + 4]) for k in range(0, count, 4)]
            pieces = list(scatter_ring(stacked, 4 * unit))
        own, first, second, across = pieces
        passing = swap_ways(across.astype(bf16), unit, 3 * unit)
        arrived = swap_ways(first.astype(bf16), unit, 3 * unit)
        return own, (second, passing, arrived)

    def scatter_last(own, state, unit):
        if state is None:
            total = own[0].astype(f32)
            for k in range(1, len(own)):
                total = total + swap(own[k].astype(bf16), unit * k).astype(f32)
            return total
        second, passing, arrived = state
        return own.astype(f32) + arrived.astype(f32) + scatter_message(second, passing, unit).astype(f32)

    def scatter_message(second, passing, unit):
        return swap_ways((second.astype(f32) + passing.astype(f32)).astype(bf16), 3 * unit, unit)

    def scatter_ring(pieces, unit):
        return scatter_last(*scatter_first(pieces, unit), unit)

    def place_groups(pieces, order):
        size = pieces[0].shape[0]
        whole = jnp.zeros((size * groups, pieces[0].shape[1]), pieces[0].dtype)
        for relative, piece in zip(order, pieces):
            whole = lax.dynamic_update_slice_in_dim(whole, piece, (group ^ relative) * size, 0)
        return whole

    def fetch_side(bundle):
        received = swap(pick(bundle, 1 - side), narrow)
        return place([pick(bundle, side), received], side, 0)

    def halves(array):
        return array.reshape(depth, -1, 2, array.shape[-1] // 2).transpose(2, 0, 1, 3)

    def from_chips(array):
        return [swap(array, over_chips(k, s)) for k, s in chips]

    def to_chips(pieces):
        return [swap(piece, over_chips(k, s)) for (k, s), piece in zip(chips[1:], pieces)]

    def reduce_cores(own, other, *others):
        received = after(swap(other, 1), *others)

        def places(*later):
            blocks = []
            for place_at, k in enumerate(ring_order(groups)):
                pair = (own, received)
                if later and place_at % 2 == 0:
                    pair = lax.optimization_barrier((own, received, *later))[:2]
                pair = [pick(array.reshape(groups, 2 * depth, -1), group ^ k).astype(f32) for array in pair]
                blocks.append(pair[0] + pair[1])
            return blocks

        return places

    def scatter_early(places):
        if groups != 4:
            return scatter_first(places(), unit_mask)
        _, first, _, across = places()
        return swap_ways(across.astype(bf16), unit_mask, 3 * unit_mask), swap_ways(first.astype(bf16), unit_mask, 3 * unit_mask)

    def scatter_late(places, state, *later):
        if groups != 4:
            return scatter_last(*state, unit_mask)
        own, _, second, _ = places(*later)
        return scatter_last(own, (second, *state), unit_mask)

    def reduce_side(total):
        total = total.reshape(2, depth, -1)
        kept = pick(total, side)
        received = swap(pick(total, 1 - side).astype(bf16), narrow).astype(f32)
        return place([kept[None], received[None]], side, 0)

    def join(array):
        return array.transpose(1, 2, 0, 3).reshape(depth, array.shape[2], -1)

    attn_bundle = jnp.concatenate(
        [halves(query_key_value_weight), halves(attention_out_weight.T[:, None])], axis=2
    ).reshape(2, depth, 4 * half)
    mlp_bundle = jnp.concatenate(
        [halves(feedforward_in_weight), halves(feedforward_out_weight.T[:, None])], axis=2
    ).reshape(2, depth, 3 * hidden)
    lanes = -(-3 * hidden // 128) * 128
    mlp_bundle = jnp.pad(mlp_bundle, ((0, 0), (0, 0), (0, lanes - 3 * hidden)))

    both = jnp.stack([inputs, grad_out])
    received = swap(pick(both, 1 - core, 1), 1)
    features = place([pick(both, core, 1), received], core, 2)
    attn_pair = fetch_side(attn_bundle)
    shards = from_chips(features)
    gains = after(jnp.stack([attn_gain, mlp_gain]), shards)
    gains = place([gains, swap(gains, 1)], core, 1)
    gains = place([swap(gains, 2 * k) for k in range(columns)], column, 1)
    mlp_pair = fetch_side(after(mlp_bundle, shards))
    if groups >= 4:
        quad = [attn_pair, *ring_first(attn_pair, unit_mask)]
        quad, shards = lax.optimization_barrier((quad, shards))
        quad.append(ring_last(quad[2], unit_mask))
        if groups > 4:
            quad = [q for quads in gather_ring(jnp.stack(quad), 4 * unit_mask, groups // 4) for q in quads]
    else:
        quad = gather_ring(attn_pair, unit_mask, groups)
    order = ring_order(groups)
    turned = [other_way(k) for k in order]
    count = groups if 2 * depth % 128 == 0 else 1
    starts = [group ^ k for k in order] + [group ^ k for k in turned] if count > 1 else [0, 0]

    def both_blocks(own, other):
        return [*own, *other] if count > 1 else [place_groups(own, order), place_groups(other, turned)]

    token = (jnp.arange(rows) // block) ^ side
    positions = ((group * 2 + token) * block + jnp.arange(rows) % block).astype(f32)
    cosine, sine = rope_tables(positions, width)
    at = jnp.stack([column, narrow_at, *starts]).astype(jnp.int32)
    early = [swap(piece, 1) for piece in quad[:3]]
    mlp_pair, gains, quad, early, cosine, sine, at = lax.optimization_barrier(
        (mlp_pair, gains, quad, early, cosine, sine, at)
    )
    attn_weights = both_blocks(quad, [*early, *[swap(piece, 1) for piece in quad[len(early) :]]])
    mlp_quad = [mlp_pair, *ring_first(mlp_pair, unit_mask)] if groups >= 4 else []

    rows_in, grad_rows, normed_one, query, pair = call(
        functools.partial(project, chips, count),
        [((rows, model), bf16)] * 3 + [((rows, width), bf16), ((rows, span), bf16)],
        at, *shards, *attn_weights, gains, cosine, sine,
    )
    out_own = place_groups([after(piece[:, 3 * half :], pair) for piece in quad], order)
    out_own = from_chips(out_own)
    if groups == 4:
        (first, second), mlp_quad, out_own = lax.optimization_barrier((ring_first(pair, unit_mask), mlp_quad, out_own))
        pairs = [pair, first, second, ring_last(second, unit_mask)]
    else:
        pairs = gather_ring(pair, unit_mask, groups)
    pairs, out_own, early = lax.optimization_barrier((pairs, out_own, mlp_quad))
    early = [swap(piece, 1) for piece in early]
    out_own = jnp.stack(out_own)
    out_other = swap(out_own, 1)
    if groups >= 4:
        mlp_quad.append(ring_last(after(mlp_quad[2], pairs), unit_mask))
    context, pairs, total = call(
        functools.partial(attend, len(pairs)),
        [((rows, width), bf16), ((length, span), bf16), ((8, rows), f32)],
        at, query, *pairs,
    )
    contexts = from_chips(context)
    if groups >= 4:
        late = after(mlp_quad.pop(), contexts)
        mlp_quad, early = [*mlp_quad, late], [*early, swap(late, 1)]
        if groups > 4:
            mlp_quad = [q for quads in gather_ring(jnp.stack(mlp_quad), 4 * unit_mask, groups // 4) for q in quads]
            early = [swap(piece, 1) for piece in mlp_quad]
    else:
        mlp_quad = gather_ring(mlp_pair, unit_mask, groups)
        early = [swap(piece, 1) for piece in mlp_quad]
    mlp_weights = both_blocks(mlp_quad, early)
    middle, middle_rows, normed_two, unit, active, mlp_gain_part, grad_two, *sends = call(
        functools.partial(feed, chips, count),
        [((block, span), f32), ((part, model), f32), ((rows, model), bf16), ((2, rows, 2 * hidden), bf16),
         ((2, rows, hidden), bf16), ((1, model), f32), ((part, model), f32)] + [((part, model), bf16)] * (len(chips) - 1),
        at, *contexts, *mlp_weights, out_own, out_other, rows_in, grad_rows, gains,
        scratch=[((rows, model), f32)],
    )
    received = to_chips(sends)
    grad_mlp_own, grad_mlp_other, branch, *branch_sends = call(
        functools.partial(settle, chips, count),
        [((model, lanes), bf16)] * 2 + [((block, span), f32)] + [((block, span), bf16)] * (len(chips) - 1),
        at, *mlp_weights, normed_two, unit, active, grad_rows, middle,
        scratch=[((rows, model), f32)],
    )
    grad_mlp_other = after(grad_mlp_other, received)
    grad_middle, grad_low = call(
        functools.partial(turn), [((part, model), f32), ((part, model), bf16)],
        at, grad_two, *received, middle_rows, grad_rows, gains,
    )
    grad_pieces = from_chips(grad_low)
    grad_mlp = reduce_cores(grad_mlp_own, grad_mlp_other, grad_low)
    mlp_state = scatter_early(grad_mlp)
    grad_attn, grad_query, grad_pairs = call(
        functools.partial(reflect, chips, count),
        [((rows, model), bf16), ((rows, width), f32), ((length, span), bf16)],
        at, *grad_pieces, *attn_weights, query, pairs, total,
    )
    if groups >= 4:
        mlp_state, grad_pairs, branch_sends = lax.optimization_barrier((mlp_state, grad_pairs, branch_sends))
    grad_pairs = scatter_ring(list(grad_pairs.reshape(groups, rows, span)), unit_mask)

    branch_received = to_chips(branch_sends)
    grad_pairs, mlp_state, branch_received = lax.optimization_barrier((grad_pairs, mlp_state, branch_received))
    for piece in branch_received:
        branch = branch + piece.astype(f32)
    branch = branch.astype(bf16).reshape(block, 2, width)
    result = place([pick(branch, core, 1)[None], swap(pick(branch, 1 - core, 1), 1)[None]], core, 0)

    mlp_places = grad_mlp
    if groups == 4:
        mlp_own, _, mlp_second, _ = mlp_places(grad_query)
        grad_mlp = scatter_message(mlp_second, mlp_state[0], unit_mask)
    else:
        grad_mlp = scatter_late(mlp_places, mlp_state)
    grad_projected, attn_gain_part, grad_one, *sends = call(
        functools.partial(unwind, chips, count),
        [((2, rows, 3 * half), bf16), ((1, model), f32), ((part, model), f32)] + [((part, model), bf16)] * (len(chips) - 1),
        at, *attn_weights, grad_query, grad_pairs, cosine, sine, rows_in,
        scratch=[((rows, model), f32)],
    )
    received = to_chips(sends)
    grad_attn_own, grad_attn_other = call(
        functools.partial(repay), [((model, 4 * half), bf16)] * 2,
        at, normed_one, grad_projected, grad_attn, context,
    )
    grad_attn_other, grad_mlp, received = lax.optimization_barrier((grad_attn_other, grad_mlp, received))
    gain_grads = jnp.concatenate([after(attn_gain_part, *received), mlp_gain_part], axis=0).reshape(2, narrow, width)
    gain_total = pick(gain_grads, narrow_at, 1)
    for m in range(1, narrow):
        gain_total = gain_total + swap(pick(gain_grads, narrow_at ^ m, 1), m)
    attn_places = reduce_cores(grad_attn_own, grad_attn_other, gain_total)
    summed = [piece.astype(bf16) for piece in attn_places()[1::2]]
    state = scatter_early(attn_places)
    finished = call(
        functools.partial(finish, narrow), [((part, width), f32)] * narrow,
        at, after(grad_one, *summed), *received, rows_in, grad_middle, gains,
        scratch=[((part, model), f32)],
    )
    sends = [swap(piece, m) for m, piece in enumerate(finished)]
    gain_total = after(gain_total, *summed)
    gain_total = gain_total + swap(gain_total, narrow)
    sends, state, gain_total = lax.optimization_barrier((sends, state, gain_total))
    grad_mlp = after(grad_mlp, *summed)
    if groups == 4:
        grad_mlp = mlp_own + mlp_state[1].astype(f32) + grad_mlp.astype(f32)
    grad_mlp = join(reduce_side(grad_mlp)[..., : 3 * hidden].reshape(2, depth, 3, hidden))
    grad_attn_weight = scatter_late(attn_places, state, finished[0])
    gain_total = after(gain_total, grad_attn_weight)
    if groups == 4:
        near, across, far = [swap(gain_total, unit_mask * k) for k in (1, 2, 3)]
        gain_total = (gain_total + near) + (across + far)
    else:
        for mask in ring_masks(groups):
            gain_total = gain_total + swap(gain_total, unit_mask * mask)
    grad_attn_weight = join(reduce_side(grad_attn_weight).reshape(2, depth, 4, half))
    grad_inputs = place(
        [place([sends[2 * k + c] for k in range(columns)], column, 0)[None] for c in range(2)],
        core, 0,
    )
    return (
        result,
        grad_inputs,
        gain_total[0],
        grad_attn_weight[:, :3],
        grad_attn_weight[:, 3].T,
        gain_total[1],
        grad_mlp[:, :2],
        grad_mlp[:, 2].T,
    )


def solution(mesh):
    in_specs = (
        P(None, "wide", "narrow"),
        P("narrow"),
        P("wide", None, "narrow"),
        P("narrow", "wide"),
        P("narrow"),
        P("wide", None, "narrow"),
        P("narrow", "wide"),
        P(None, "wide", "narrow"),
    )
    out_specs = (
        P(None, "wide", "narrow"),
        P(None, "wide", "narrow"),
        P("narrow"),
        P("wide", None, "narrow"),
        P("narrow", "wide"),
        P("narrow"),
        P("wide", None, "narrow"),
        P("narrow", "wide"),
    )
    step = functools.partial(body, mesh.shape["wide"], mesh.shape["narrow"])
    return jax.shard_map(step, mesh=mesh, in_specs=in_specs, out_specs=out_specs, check_vma=False)
```

```python
import functools
import math

import jax
import jax.numpy as jnp
from jax import lax
from jax.experimental import pallas as pl
from jax.experimental.pallas import tpu as pltpu
from jax.sharding import PartitionSpec as P

HEAD_DIM = 64
eps_norm = 1e-05
rope_base = 160000.0
f32 = jnp.float32
bf16 = jnp.bfloat16


def mm(a, b):
    return lax.dot_general(a, b, (((1,), (0,)), ((), ())), preferred_element_type=f32)


def mm_nt(a, b):
    return lax.dot_general(a, b, (((1,), (1,)), ((), ())), preferred_element_type=f32)


def aligned(index, size):
    return pl.ds(pl.multiple_of(index * size, size), size)


def norm_rows(rows):
    width = rows.shape[-1]
    average = jnp.sum(rows, axis=-1, keepdims=True) / width
    variance = jnp.sum(rows * rows, axis=-1, keepdims=True) / width - average * average
    inverse = lax.rsqrt(variance + eps_norm)
    return (rows - average) * inverse, inverse


def norm_backward(grad_normed, centred, inverse, gain):
    width = grad_normed.shape[-1]
    scaled = grad_normed * gain
    row_total = jnp.sum(scaled, axis=-1, keepdims=True)
    row_along = jnp.sum(scaled * centred, axis=-1, keepdims=True)
    return inverse * (scaled - row_total / width - centred * (row_along / width))


def rope_tables(positions, lanes):
    half_dim = HEAD_DIM // 2
    frequency = rope_base ** (-jnp.arange(half_dim).astype(f32) * 2.0 / HEAD_DIM)
    angles = positions[:, None] * frequency[None, :]
    angles = jnp.concatenate([angles, angles] * (lanes // HEAD_DIM), axis=-1)
    return jnp.cos(angles), jnp.sin(angles)


def rotated(tensor):
    lanes, half_dim = tensor.shape[-1], HEAD_DIM // 2
    lane = lax.broadcasted_iota(jnp.int32, tensor.shape, 1)
    up = pltpu.roll(tensor, half_dim, 1)
    down = pltpu.roll(tensor, lanes - half_dim, 1)
    return jnp.where(lane % HEAD_DIM < half_dim, -down, up)


def call(kernel, outs, at, *arrays, scratch=()):
    return pl.pallas_call(
        kernel,
        out_shape=[jax.ShapeDtypeStruct(shape, dtype) for shape, dtype in outs],
        in_specs=[pl.BlockSpec(memory_space=pltpu.SMEM)]
        + [pl.BlockSpec(memory_space=pltpu.VMEM)] * len(arrays),
        out_specs=[pl.BlockSpec(memory_space=pltpu.VMEM)] * len(outs),
        scratch_shapes=[pltpu.VMEM(shape, dtype) for shape, dtype in scratch],
        compiler_params=pltpu.CompilerParams(vmem_limit_bytes=60 * 1024 * 1024),
        name=kernel.func.__name__,
    )(at, *arrays)


def ring_masks(count):
    masks, unit = [], 1
    while unit < count:
        masks += [unit] + ([3 * unit] if 4 * unit <= count else [])
        unit *= 4
    return masks


def pick(array, index, axis=0):
    return lax.dynamic_index_in_dim(array, index, axis=axis, keepdims=False)


def place(pieces, own, axis):
    count = len(pieces)
    if count == 1:
        return pieces[0]
    if count == 2:
        return jnp.where(
            own == 0,
            jnp.concatenate(pieces, axis=axis),
            jnp.concatenate(pieces[::-1], axis=axis),
        )
    size = pieces[0].shape[axis]
    shape = list(pieces[0].shape)
    shape[axis] = size * count
    whole = jnp.zeros(shape, pieces[0].dtype)
    for relative, piece in enumerate(pieces):
        whole = lax.dynamic_update_slice_in_dim(whole, piece, (own ^ relative) * size, axis)
    return whole


def contract(rows_ref, pieces, starts, lanes):
    total = 0.0
    for piece, start in zip(pieces, starts):
        total = total + mm(rows_ref[:, aligned(start, piece.shape[0])], piece[:, lanes])
    return total


def spread(out_ref, array, pieces, starts, lanes):
    for piece, start in zip(pieces, starts):
        out_ref[:, aligned(start, piece.shape[0])] += mm_nt(array, piece[:, lanes])


def both_cores(count, at, refs):
    first = [at[2 + p] for p in range(count)]
    second = [at[2 + count + p] for p in range(count)]
    return ((refs[:count], first), (refs[count : 2 * count], second)), refs[2 * count :]


def project(chips, count, at, *refs):
    shards, refs = refs[: len(chips)], refs[len(chips) :]
    weights, refs = both_cores(count, at, refs)
    gains, cosine, sine, rows_ref, grad_ref, normed_ref, query_ref, pair_ref = refs
    block, span = shards[0].shape[1:]
    half = query_ref.shape[1] // 2
    for (k, s), shard in zip(chips, shards):
        lanes = aligned(at[0] ^ k, span)
        rows_ref[s * block : (s + 1) * block, lanes] = shard[0]
        grad_ref[s * block : (s + 1) * block, lanes] = shard[1]
    centred, _ = norm_rows(rows_ref[...].astype(f32))
    normed_ref[...] = (centred * gains[0:1, :]).astype(bf16)
    queries, keys, values = [], [], []
    for pieces, starts in weights:
        projected = contract(normed_ref, pieces, starts, slice(0, 3 * half))
        queries.append(projected[:, :half])
        keys.append(projected[:, half : 2 * half])
        values.append(projected[:, 2 * half :])
    query, key = jnp.concatenate(queries, axis=1), jnp.concatenate(keys, axis=1)
    cosine, sine = cosine[...], sine[...]
    query = (query * cosine + rotated(query) * sine).astype(bf16)
    key = (key * cosine + rotated(key) * sine).astype(bf16)
    query_ref[...] = query * jnp.asarray(HEAD_DIM**-0.5, bf16)
    pair_ref[:, : 2 * half] = key
    pair_ref[:, 2 * half :] = jnp.concatenate(values, axis=1).astype(bf16)


def attend(parts, at, query_ref, *refs):
    pieces, (context_ref, pairs_ref, total_ref) = refs[:parts], refs[parts:]
    start = 0
    for piece in pieces:
        pairs_ref[start : start + piece.shape[0], :] = piece[...]
        start += piece.shape[0]
    width = query_ref.shape[1]
    values = pairs_ref[:, width:].T
    contexts = []
    for h in range(width // HEAD_DIM):
        lanes = slice(h * HEAD_DIM, (h + 1) * HEAD_DIM)
        scores = mm_nt(pairs_ref[:, lanes], query_ref[:, lanes])
        peak = jnp.max(scores, axis=0, keepdims=True)
        log_total = peak + jnp.log(jnp.sum(jnp.exp(scores - peak), axis=0, keepdims=True))
        probs = jnp.exp(scores - log_total).astype(bf16)
        contexts.append(mm(values[lanes], probs))
        total_ref[h : h + 1, :] = log_total
    context_ref[...] = jnp.concatenate(contexts, axis=0).T.astype(bf16)


def feed(chips, count, at, *refs):
    contexts, refs = refs[: len(chips)], refs[len(chips) :]
    weights, refs = both_cores(count, at, refs)
    (out_own, out_other, rows_ref, grad_ref, gains), refs = refs[:5], refs[5:]
    (middle_ref, middle_rows_ref, normed_ref, unit_ref, active_ref, gain_ref, total_ref), refs = refs[:7], refs[7:]
    pieces, scratch = refs[:-1], refs[-1]
    hidden = active_ref.shape[2]
    block, span = middle_ref.shape
    part = total_ref.shape[0]
    middle = rows_ref[...].astype(f32)
    for p, (k, s) in enumerate(chips):
        context = contexts[p][...]
        if s:
            context = jnp.concatenate([context[block:], context[:block]], axis=0)
        middle = middle + mm_nt(context, jnp.concatenate([out_own[p], out_other[p]], axis=1))
    scratch[...] = middle
    middle_ref[...] = scratch[:block, aligned(at[0], span)]
    middle_rows_ref[...] = scratch[aligned(at[0], part), :]
    centred, _ = norm_rows(middle)
    normed_ref[...] = (centred * gains[1:2, :]).astype(bf16)
    scratch[...] = jnp.zeros_like(scratch)
    for b, (weight, starts) in enumerate(weights):
        gate_up = contract(normed_ref, weight, starts, slice(0, 2 * hidden))
        gate, lift = gate_up[:, :hidden], gate_up[:, hidden:]
        share = 0.5 + 0.5 * lax.erf(gate * math.sqrt(0.5))
        bent = gate * share
        active_ref[b] = (bent * lift).astype(bf16)
        slope = share + gate * jnp.exp(-0.5 * gate * gate) * (1.0 / math.sqrt(2.0 * math.pi))
        back = contract(grad_ref, weight, starts, slice(2 * hidden, 3 * hidden))
        unit = jnp.concatenate([back * lift * slope, back * bent], axis=1).astype(bf16)
        unit_ref[b] = unit
        spread(scratch, unit, weight, starts, slice(0, 2 * hidden))
    gain_ref[...] = jnp.sum(scratch[...] * centred, axis=0, keepdims=True)
    cut_rows(chips, at, scratch, total_ref, pieces)


def cut_rows(chips, at, scratch, total_ref, pieces):
    part = total_ref.shape[0]
    columns = scratch.shape[0] // (2 * part)
    for p, (k, s) in enumerate(chips):
        rows = scratch[aligned(s * columns + (at[0] ^ k), part), :]
        if p:
            pieces[p - 1][...] = rows.astype(bf16)
        else:
            total_ref[...] = rows


def turn(at, total_ref, *refs):
    pieces, (middle_ref, grad_ref, gains, grad_middle_ref, low_ref) = refs[:-5], refs[-5:]
    part = total_ref.shape[0]
    total = total_ref[...]
    for piece in pieces:
        total = total + piece[...].astype(f32)
    centred, inverse = norm_rows(middle_ref[...])
    grad = grad_ref[aligned(at[0], part), :].astype(f32)
    grad = grad + norm_backward(total, centred, inverse, gains[1:2, :])
    grad_middle_ref[...] = grad
    low_ref[...] = grad.astype(bf16)


def settle(chips, count, at, *refs):
    weights, refs = both_cores(count, at, refs)
    (normed_ref, unit_ref, active_ref, grad_ref, middle_ref), refs = refs[:5], refs[5:]
    (own_ref, other_ref, total_ref), refs = refs[:3], refs[3:]
    pieces, scratch = refs[:-1], refs[-1]
    hidden = active_ref.shape[2]
    block, span = total_ref.shape
    normed, grad = normed_ref[...].T, grad_ref[...].T
    for b, out in enumerate((other_ref, own_ref)):
        out[:, : 2 * hidden] = mm(normed, unit_ref[1 - b]).astype(bf16)
        out[:, 2 * hidden : 3 * hidden] = mm(grad, active_ref[1 - b]).astype(bf16)
        if out.shape[1] > 3 * hidden:
            out[:, 3 * hidden :] = jnp.zeros((out.shape[0], out.shape[1] - 3 * hidden), bf16)
    scratch[...] = jnp.zeros_like(scratch)
    for b, (weight, starts) in enumerate(weights):
        spread(scratch, active_ref[b], weight, starts, slice(2 * hidden, 3 * hidden))
    for p, (k, s) in enumerate(chips):
        piece = scratch[s * block : (s + 1) * block, aligned(at[0] ^ k, span)]
        if p:
            pieces[p - 1][...] = piece.astype(bf16)
        else:
            total_ref[...] = piece + middle_ref[...]


def reflect(chips, count, at, *refs):
    pieces, refs = refs[: len(chips)], refs[len(chips) :]
    weights, refs = both_cores(count, at, refs)
    query_ref, pairs_ref, total_ref, grad_attn_ref, grad_query_ref, grad_pairs_ref = refs
    part = pieces[0].shape[0]
    rows, width = query_ref.shape
    columns = rows // (2 * part)
    half = width // 2
    for (k, s), piece in zip(chips, pieces):
        grad_attn_ref[aligned(s * columns + (at[0] ^ k), part), :] = piece[...]
    grad_context = jnp.concatenate(
        [contract(grad_attn_ref, weight, starts, slice(3 * half, 4 * half)) for weight, starts in weights],
        axis=1,
    ).astype(bf16)
    keys = pairs_ref[:, :width].T
    grad_queries = []
    for h in range(width // HEAD_DIM):
        lanes = slice(h * HEAD_DIM, (h + 1) * HEAD_DIM)
        query = query_ref[:, lanes]
        grad = grad_context[:, lanes]
        probs = jnp.exp(mm_nt(pairs_ref[:, lanes], query) - total_ref[h : h + 1, :])
        value_lanes = slice(width + h * HEAD_DIM, width + (h + 1) * HEAD_DIM)
        grad_probs = mm_nt(pairs_ref[:, value_lanes], grad)
        delta = jnp.sum(probs * grad_probs, axis=0, keepdims=True)
        grad_scores = (probs * (grad_probs - delta)).astype(bf16)
        grad_pairs_ref[:, lanes] = mm(grad_scores, query)
        grad_pairs_ref[:, value_lanes] = mm(probs.astype(bf16), grad)
        grad_queries.append(mm(keys[lanes], grad_scores))
    grad_query_ref[...] = jnp.concatenate(grad_queries, axis=0).T * HEAD_DIM**-0.5


def unwind(chips, count, at, *refs):
    weights, refs = both_cores(count, at, refs)
    (grad_query_ref, grad_pairs_ref, cosine, sine, rows_ref), refs = refs[:5], refs[5:]
    (grad_projected_ref, gain_ref, total_ref), refs = refs[:3], refs[3:]
    pieces, scratch = refs[:-1], refs[-1]
    width = grad_query_ref.shape[1]
    half = width // 2
    cosine, sine = cosine[...], sine[...]
    grad_query, grad_key = grad_query_ref[...], grad_pairs_ref[:, :width]
    grad_query = (grad_query * cosine - rotated(grad_query * sine)).astype(bf16)
    grad_key = (grad_key * cosine - rotated(grad_key * sine)).astype(bf16)
    grad_value = grad_pairs_ref[:, width:].astype(bf16)
    scratch[...] = jnp.zeros_like(scratch)
    for b, (weight, starts) in enumerate(weights):
        lanes = slice(b * half, (b + 1) * half)
        grad = jnp.concatenate([grad_query[:, lanes], grad_key[:, lanes], grad_value[:, lanes]], axis=1)
        grad_projected_ref[b] = grad
        spread(scratch, grad, weight, starts, slice(0, 3 * half))
    centred, _ = norm_rows(rows_ref[...].astype(f32))
    gain_ref[...] = jnp.sum(scratch[...] * centred, axis=0, keepdims=True)
    cut_rows(chips, at, scratch, total_ref, pieces)


def repay(at, normed_ref, grad_projected_ref, grad_attn_ref, context_ref, own_ref, other_ref):
    half = context_ref.shape[1] // 2
    normed, grad_attn = normed_ref[...].T, grad_attn_ref[...].T
    for b, out in ((1, other_ref), (0, own_ref)):
        out[:, : 3 * half] = mm(normed, grad_projected_ref[b]).astype(bf16)
        out[:, 3 * half :] = mm(grad_attn, context_ref[:, b * half : (b + 1) * half]).astype(bf16)


def finish(narrow, at, total_ref, *refs):
    pieces, (rows_ref, grad_middle_ref, gains), outs, scratch = refs[: -narrow - 4], refs[-narrow - 4 : -narrow - 1], refs[-narrow - 1 : -1], refs[-1]
    part = total_ref.shape[0]
    width = outs[0].shape[1]
    total = total_ref[...]
    for piece in pieces:
        total = total + piece[...].astype(f32)
    centred, inverse = norm_rows(rows_ref[aligned(at[0], part), :].astype(f32))
    scratch[...] = grad_middle_ref[...] + norm_backward(total, centred, inverse, gains[0:1, :])
    for m, out in enumerate(outs):
        out[...] = scratch[:, aligned(at[1] ^ m, width)]


def body(
    wide,
    narrow,
    inputs,
    attn_gain,
    query_key_value_weight,
    attention_out_weight,
    mlp_gain,
    feedforward_in_weight,
    feedforward_out_weight,
    grad_out,
):
    groups, columns = wide // 2, narrow // 2
    _, block, width = inputs.shape
    model = width * narrow
    depth = query_key_value_weight.shape[0]
    hidden = feedforward_out_weight.shape[0] // 2
    half, span = width // 2, 2 * width
    part = block // columns
    rows = 2 * block
    length = groups * rows
    wide_at, narrow_at = lax.axis_index("wide"), lax.axis_index("narrow")
    group, side = wide_at // 2, wide_at % 2
    column, core = narrow_at // 2, narrow_at % 2
    chips = [(k, s) for s in range(2) for k in range(columns)]

    unit_mask = 2 * narrow

    def swap(array, mask):
        if mask == 0:
            return array
        return lax.ppermute(
            array, ("wide", "narrow"), [(i, i ^ mask) for i in range(wide * narrow)]
        )

    def over_chips(column_rel, side_rel):
        return 2 * column_rel + narrow * side_rel

    def over_groups(group_rel):
        return 2 * narrow * group_rel

    def after(array, *others):
        return lax.optimization_barrier((array, *others))[0]

    def swap_ways(array, even, odd):
        pairs = [(i, i ^ (odd if i % 2 else even)) for i in range(wide * narrow)]
        return lax.ppermute(array, ("wide", "narrow"), pairs)

    def ring_order(count):
        if count < 4:
            return list(range(count))
        quad = [0, 1 + 2 * core, 3 - 2 * core, 2]
        return [low + 4 * high for high in ring_order(count // 4) for low in quad]

    def ring_first(array, unit):
        return swap(array, unit), swap(array, 3 * unit)

    def ring_last(second, unit):
        return swap(second, unit)

    def gather_order(count):
        if count < 4:
            return list(range(count))
        return [low + 4 * high for high in gather_order(count // 4) for low in (0, 1, 3, 2)]

    def gather_ring(array, unit, count):
        if count < 4:
            return [swap(array, unit * k) for k in range(count)]
        first, second = ring_first(array, unit)
        quad = [array, first, second, ring_last(second, unit)]
        if count == 4:
            return quad
        return [q for quads in gather_ring(jnp.stack(quad), 4 * unit, count // 4) for q in quads]

    def scatter_first(pieces, unit, turn_odd=True):
        count = len(pieces)
        if count < 4:
            return pieces, None
        if count > 4:
            stacked = [jnp.stack(pieces[k : k + 4]) for k in range(0, count, 4)]
            pieces = list(scatter_ring(stacked, 4 * unit, turn_odd))
        own, first, second, across = pieces
        odd = 3 * unit if turn_odd else unit
        passing = swap_ways(across.astype(bf16), unit, odd)
        arrived = swap_ways(first.astype(bf16), unit, odd)
        return own, (second, passing, arrived)

    def scatter_last(own, state, unit, turn_odd=True):
        if state is None:
            total = own[0].astype(f32)
            for k in range(1, len(own)):
                total = total + swap(own[k].astype(bf16), unit * k).astype(f32)
            return total
        second, passing, arrived = state
        second = (second.astype(f32) + passing.astype(f32)).astype(bf16)
        return own.astype(f32) + arrived.astype(f32) + swap_ways(second, 3 * unit, unit if turn_odd else 3 * unit).astype(f32)

    def scatter_ring(pieces, unit, turn_odd):
        return scatter_last(*scatter_first(pieces, unit, turn_odd), unit, turn_odd)

    def place_groups(pieces, order):
        size = pieces[0].shape[0]
        whole = jnp.zeros((size * groups, pieces[0].shape[1]), pieces[0].dtype)
        for relative, piece in zip(order, pieces):
            whole = lax.dynamic_update_slice_in_dim(whole, piece, (group ^ relative) * size, 0)
        return whole

    def fetch_side(bundle):
        received = swap(pick(bundle, 1 - side), narrow)
        return place([pick(bundle, side), received], side, 0)

    def halves(array):
        return array.reshape(depth, -1, 2, array.shape[-1] // 2).transpose(2, 0, 1, 3)

    def from_chips(array):
        return [swap(array, over_chips(k, s)) for k, s in chips]

    def to_chips(pieces):
        return [swap(piece, over_chips(k, s)) for (k, s), piece in zip(chips[1:], pieces)]

    def reduce_cores(own, other, *others):
        received = after(swap(other, 1), *others)

        def places(*later):
            blocks = []
            for place_at, k in enumerate(ring_order(groups)):
                pair = (own, received)
                if later and place_at % 2 == 0:
                    pair = lax.optimization_barrier((own, received, *later))[:2]
                pair = [pick(array.reshape(groups, 2 * depth, -1), group ^ k).astype(f32) for array in pair]
                blocks.append(pair[0] + pair[1])
            return blocks

        return places

    def scatter_early(places):
        if groups != 4:
            return scatter_first(places(), unit_mask)
        _, first, _, across = places()
        return swap_ways(across.astype(bf16), unit_mask, 3 * unit_mask), swap_ways(first.astype(bf16), unit_mask, 3 * unit_mask)

    def scatter_late(places, state, *later):
        if groups != 4:
            return scatter_last(*state, unit_mask)
        own, _, second, _ = places(*later)
        return scatter_last(own, (second, *state), unit_mask)

    def reduce_side(total):
        total = total.reshape(2, depth, -1)
        kept = pick(total, side)
        received = swap(pick(total, 1 - side).astype(bf16), narrow).astype(f32)
        return place([kept[None], received[None]], side, 0)

    def join(array):
        return array.transpose(1, 2, 0, 3).reshape(depth, array.shape[2], -1)

    attn_bundle = jnp.concatenate(
        [halves(query_key_value_weight), halves(attention_out_weight.T[:, None])], axis=2
    ).reshape(2, depth, 4 * half)
    mlp_bundle = jnp.concatenate(
        [halves(feedforward_in_weight), halves(feedforward_out_weight.T[:, None])], axis=2
    ).reshape(2, depth, 3 * hidden)
    lanes = -(-3 * hidden // 128) * 128
    mlp_bundle = jnp.pad(mlp_bundle, ((0, 0), (0, 0), (0, lanes - 3 * hidden)))

    both = jnp.stack([inputs, grad_out])
    received = swap(pick(both, 1 - core, 1), 1)
    features = place([pick(both, core, 1), received], core, 2)
    attn_pair = fetch_side(attn_bundle)
    shards = from_chips(features)
    gains = after(jnp.stack([attn_gain, mlp_gain]), shards)
    gains = place([gains, swap(gains, 1)], core, 1)
    gains = place([swap(gains, 2 * k) for k in range(columns)], column, 1)
    mlp_pair = fetch_side(after(mlp_bundle, shards))
    if groups >= 4:
        quad = [attn_pair, *ring_first(attn_pair, unit_mask)]
        quad, shards = lax.optimization_barrier((quad, shards))
        quad.append(ring_last(quad[2], unit_mask))
        if groups > 4:
            quad = [q for quads in gather_ring(jnp.stack(quad), 4 * unit_mask, groups // 4) for q in quads]
    else:
        quad = gather_ring(attn_pair, unit_mask, groups)
    order = turned = gather_order(groups)
    count = groups if 2 * depth % 128 == 0 else 1
    starts = [group ^ k for k in order] + [group ^ k for k in turned] if count > 1 else [0, 0]

    def both_blocks(own, other):
        return [*own, *other] if count > 1 else [place_groups(own, order), place_groups(other, turned)]

    token = (jnp.arange(rows) // block) ^ side
    positions = ((group * 2 + token) * block + jnp.arange(rows) % block).astype(f32)
    cosine, sine = rope_tables(positions, width)
    at = jnp.stack([column, narrow_at, *starts]).astype(jnp.int32)
    early = [swap(piece, 1) for piece in quad[:3]]
    mlp_pair, gains, quad, early, cosine, sine, at = lax.optimization_barrier(
        (mlp_pair, gains, quad, early, cosine, sine, at)
    )
    attn_weights = both_blocks(quad, [*early, *[swap(piece, 1) for piece in quad[len(early) :]]])
    mlp_quad = [mlp_pair, *ring_first(mlp_pair, unit_mask)] if groups >= 4 else []

    rows_in, grad_rows, normed_one, query, pair = call(
        functools.partial(project, chips, count),
        [((rows, model), bf16)] * 3 + [((rows, width), bf16), ((rows, span), bf16)],
        at, *shards, *attn_weights, gains, cosine, sine,
    )
    out_own = place_groups([after(piece[:, 3 * half :], pair) for piece in quad], order)
    out_own = from_chips(out_own)
    if groups == 4:
        (first, second), mlp_quad, out_own = lax.optimization_barrier((ring_first(pair, unit_mask), mlp_quad, out_own))
        pairs = [pair, first, second, ring_last(second, unit_mask)]
    else:
        pairs = gather_ring(pair, unit_mask, groups)
    pairs, out_own, early = lax.optimization_barrier((pairs, out_own, mlp_quad))
    early = [swap(piece, 1) for piece in early]
    out_own = jnp.stack(out_own)
    out_other = swap(out_own, 1)
    if groups >= 4:
        mlp_quad.append(ring_last(after(mlp_quad[2], pairs), unit_mask))
    context, pairs, total = call(
        functools.partial(attend, len(pairs)),
        [((rows, width), bf16), ((length, span), bf16), ((8, rows), f32)],
        at, query, *pairs,
    )
    contexts = from_chips(context)
    if groups >= 4:
        late = after(mlp_quad.pop(), contexts)
        mlp_quad, early = [*mlp_quad, late], [*early, swap(late, 1)]
        if groups > 4:
            mlp_quad = [q for quads in gather_ring(jnp.stack(mlp_quad), 4 * unit_mask, groups // 4) for q in quads]
            early = [swap(piece, 1) for piece in mlp_quad]
    else:
        mlp_quad = gather_ring(mlp_pair, unit_mask, groups)
        early = [swap(piece, 1) for piece in mlp_quad]
    mlp_weights = both_blocks(mlp_quad, early)
    middle, middle_rows, normed_two, unit, active, mlp_gain_part, grad_two, *sends = call(
        functools.partial(feed, chips, count),
        [((block, span), f32), ((part, model), f32), ((rows, model), bf16), ((2, rows, 2 * hidden), bf16),
         ((2, rows, hidden), bf16), ((1, model), f32), ((part, model), f32)] + [((part, model), bf16)] * (len(chips) - 1),
        at, *contexts, *mlp_weights, out_own, out_other, rows_in, grad_rows, gains,
        scratch=[((rows, model), f32)],
    )
    received = to_chips(sends)
    grad_mlp_own, grad_mlp_other, branch, *branch_sends = call(
        functools.partial(settle, chips, count),
        [((model, lanes), bf16)] * 2 + [((block, span), f32)] + [((block, span), bf16)] * (len(chips) - 1),
        at, *mlp_weights, normed_two, unit, active, grad_rows, middle,
        scratch=[((rows, model), f32)],
    )
    grad_mlp_other = after(grad_mlp_other, received)
    grad_middle, grad_low = call(
        functools.partial(turn), [((part, model), f32), ((part, model), bf16)],
        at, grad_two, *received, middle_rows, grad_rows, gains,
    )
    grad_pieces = from_chips(grad_low)
    grad_mlp = reduce_cores(grad_mlp_own, grad_mlp_other, grad_low)
    mlp_state = scatter_early(grad_mlp)
    grad_attn, grad_query, grad_pairs = call(
        functools.partial(reflect, chips, count),
        [((rows, model), bf16), ((rows, width), f32), ((length, span), f32)],
        at, *grad_pieces, *attn_weights, query, pairs, total,
    )
    if groups >= 4:
        mlp_state, grad_pairs, branch_sends = lax.optimization_barrier((mlp_state, grad_pairs, branch_sends))
    grad_pairs = scatter_ring(list(grad_pairs.reshape(groups, rows, span)), unit_mask, False)

    branch_received = to_chips(branch_sends)
    grad_pairs, mlp_state, branch_received = lax.optimization_barrier((grad_pairs, mlp_state, branch_received))
    for piece in branch_received:
        branch = branch + piece.astype(f32)
    branch = branch.astype(bf16).reshape(block, 2, width)
    result = place([pick(branch, core, 1)[None], swap(pick(branch, 1 - core, 1), 1)[None]], core, 0)

    grad_mlp = scatter_late(grad_mlp, mlp_state, grad_query)
    grad_projected, attn_gain_part, grad_one, *sends = call(
        functools.partial(unwind, chips, count),
        [((2, rows, 3 * half), bf16), ((1, model), f32), ((part, model), f32)] + [((part, model), bf16)] * (len(chips) - 1),
        at, *attn_weights, grad_query, grad_pairs, cosine, sine, rows_in,
        scratch=[((rows, model), f32)],
    )
    received = to_chips(sends)
    grad_attn_own, grad_attn_other = call(
        functools.partial(repay), [((model, 4 * half), bf16)] * 2,
        at, normed_one, grad_projected, grad_attn, context,
    )
    grad_attn_other, grad_mlp, received = lax.optimization_barrier((grad_attn_other, grad_mlp, received))
    gain_grads = jnp.concatenate([after(attn_gain_part, *received), mlp_gain_part], axis=0).reshape(2, narrow, width)
    gain_total = pick(gain_grads, narrow_at, 1)
    for m in range(1, narrow):
        gain_total = gain_total + swap(pick(gain_grads, narrow_at ^ m, 1), m)
    attn_places = reduce_cores(grad_attn_own, grad_attn_other, gain_total)
    summed = [piece.astype(bf16) for piece in attn_places()[1::2]]
    state = scatter_early(attn_places)
    finished = call(
        functools.partial(finish, narrow), [((part, width), f32)] * narrow,
        at, after(grad_one, *summed), *received, rows_in, grad_middle, gains,
        scratch=[((part, model), f32)],
    )
    sends = [swap(piece, m) for m, piece in enumerate(finished)]
    gain_total = after(gain_total, *summed)
    gain_total = gain_total + swap(gain_total, narrow)
    sends, state, gain_total = lax.optimization_barrier((sends, state, gain_total))
    grad_mlp = after(grad_mlp, *summed)
    grad_mlp = join(reduce_side(grad_mlp)[..., : 3 * hidden].reshape(2, depth, 3, hidden))
    grad_attn_weight = scatter_late(attn_places, state, finished[0])
    gain_total = after(gain_total, grad_attn_weight)
    if groups == 4:
        near, across, far = [swap(gain_total, unit_mask * k) for k in (1, 2, 3)]
        gain_total = (gain_total + near) + (across + far)
    else:
        for mask in ring_masks(groups):
            gain_total = gain_total + swap(gain_total, unit_mask * mask)
    grad_attn_weight = join(reduce_side(grad_attn_weight).reshape(2, depth, 4, half))
    grad_inputs = place(
        [place([sends[2 * k + c] for k in range(columns)], column, 0)[None] for c in range(2)],
        core, 0,
    )
    return (
        result,
        grad_inputs,
        gain_total[0],
        grad_attn_weight[:, :3],
        grad_attn_weight[:, 3].T,
        gain_total[1],
        grad_mlp[:, :2],
        grad_mlp[:, 2].T,
    )


def solution(mesh):
    in_specs = (
        P(None, "wide", "narrow"),
        P("narrow"),
        P("wide", None, "narrow"),
        P("narrow", "wide"),
        P("narrow"),
        P("wide", None, "narrow"),
        P("narrow", "wide"),
        P(None, "wide", "narrow"),
    )
    out_specs = (
        P(None, "wide", "narrow"),
        P(None, "wide", "narrow"),
        P("narrow"),
        P("wide", None, "narrow"),
        P("narrow", "wide"),
        P("narrow"),
        P("wide", None, "narrow"),
        P("narrow", "wide"),
    )
    step = functools.partial(body, mesh.shape["wide"], mesh.shape["narrow"])
    return jax.shard_map(step, mesh=mesh, in_specs=in_specs, out_specs=out_specs, check_vma=False)
```

```python
import functools
import math

import jax
import jax.numpy as jnp
from jax import lax
from jax.experimental import pallas as pl
from jax.experimental.pallas import tpu as pltpu
from jax.sharding import PartitionSpec as P

HEAD_DIM = 64
eps_norm = 1e-05
rope_base = 160000.0
f32 = jnp.float32
bf16 = jnp.bfloat16


def mm(a, b):
    return lax.dot_general(a, b, (((1,), (0,)), ((), ())), preferred_element_type=f32)


def mm_nt(a, b):
    return lax.dot_general(a, b, (((1,), (1,)), ((), ())), preferred_element_type=f32)


def aligned(index, size):
    return pl.ds(pl.multiple_of(index * size, size), size)


def norm_rows(rows):
    width = rows.shape[-1]
    average = jnp.sum(rows, axis=-1, keepdims=True) / width
    variance = jnp.sum(rows * rows, axis=-1, keepdims=True) / width - average * average
    inverse = lax.rsqrt(variance + eps_norm)
    return (rows - average) * inverse, inverse


def norm_backward(grad_normed, centred, inverse, gain):
    width = grad_normed.shape[-1]
    scaled = grad_normed * gain
    row_total = jnp.sum(scaled, axis=-1, keepdims=True)
    row_along = jnp.sum(scaled * centred, axis=-1, keepdims=True)
    return inverse * (scaled - row_total / width - centred * (row_along / width))


def rope_tables(positions, lanes):
    half_dim = HEAD_DIM // 2
    frequency = rope_base ** (-jnp.arange(half_dim).astype(f32) * 2.0 / HEAD_DIM)
    angles = positions[:, None] * frequency[None, :]
    angles = jnp.concatenate([angles, angles] * (lanes // HEAD_DIM), axis=-1)
    return jnp.cos(angles), jnp.sin(angles)


def rotated(tensor):
    lanes, half_dim = tensor.shape[-1], HEAD_DIM // 2
    lane = lax.broadcasted_iota(jnp.int32, tensor.shape, 1)
    up = pltpu.roll(tensor, half_dim, 1)
    down = pltpu.roll(tensor, lanes - half_dim, 1)
    return jnp.where(lane % HEAD_DIM < half_dim, -down, up)


def call(kernel, outs, at, *arrays, scratch=()):
    return pl.pallas_call(
        kernel,
        out_shape=[jax.ShapeDtypeStruct(shape, dtype) for shape, dtype in outs],
        in_specs=[pl.BlockSpec(memory_space=pltpu.SMEM)]
        + [pl.BlockSpec(memory_space=pltpu.VMEM)] * len(arrays),
        out_specs=[pl.BlockSpec(memory_space=pltpu.VMEM)] * len(outs),
        scratch_shapes=[pltpu.VMEM(shape, dtype) for shape, dtype in scratch],
        compiler_params=pltpu.CompilerParams(vmem_limit_bytes=60 * 1024 * 1024),
        name=kernel.func.__name__,
    )(at, *arrays)


def ring_masks(count):
    masks, unit = [], 1
    while unit < count:
        masks += [unit] + ([3 * unit] if 4 * unit <= count else [])
        unit *= 4
    return masks


def pick(array, index, axis=0):
    return lax.dynamic_index_in_dim(array, index, axis=axis, keepdims=False)


def place(pieces, own, axis):
    count = len(pieces)
    if count == 1:
        return pieces[0]
    if count == 2:
        return jnp.where(
            own == 0,
            jnp.concatenate(pieces, axis=axis),
            jnp.concatenate(pieces[::-1], axis=axis),
        )
    size = pieces[0].shape[axis]
    shape = list(pieces[0].shape)
    shape[axis] = size * count
    whole = jnp.zeros(shape, pieces[0].dtype)
    for relative, piece in enumerate(pieces):
        whole = lax.dynamic_update_slice_in_dim(whole, piece, (own ^ relative) * size, axis)
    return whole


def contract(rows_ref, pieces, starts, lanes):
    total = 0.0
    for piece, start in zip(pieces, starts):
        total = total + mm(rows_ref[:, aligned(start, piece.shape[0])], piece[:, lanes])
    return total


def spread(out_ref, array, pieces, starts, lanes):
    for piece, start in zip(pieces, starts):
        out_ref[:, aligned(start, piece.shape[0])] += mm_nt(array, piece[:, lanes])


def both_cores(count, at, refs):
    first = [at[2 + p] for p in range(count)]
    second = [at[2 + count + p] for p in range(count)]
    return ((refs[:count], first), (refs[count : 2 * count], second)), refs[2 * count :]


def project(chips, count, at, *refs):
    shards, refs = refs[: len(chips)], refs[len(chips) :]
    weights, refs = both_cores(count, at, refs)
    gains, cosine, sine, rows_ref, grad_ref, normed_ref, query_ref, pair_ref = refs
    block, span = shards[0].shape[1:]
    half = query_ref.shape[1] // 2
    for (k, s), shard in zip(chips, shards):
        lanes = aligned(at[0] ^ k, span)
        rows_ref[s * block : (s + 1) * block, lanes] = shard[0]
        grad_ref[s * block : (s + 1) * block, lanes] = shard[1]
    centred, _ = norm_rows(rows_ref[...].astype(f32))
    normed_ref[...] = (centred * gains[0:1, :]).astype(bf16)
    queries, keys, values = [], [], []
    for pieces, starts in weights:
        projected = contract(normed_ref, pieces, starts, slice(0, 3 * half))
        queries.append(projected[:, :half])
        keys.append(projected[:, half : 2 * half])
        values.append(projected[:, 2 * half :])
    query, key = jnp.concatenate(queries, axis=1), jnp.concatenate(keys, axis=1)
    cosine, sine = cosine[...], sine[...]
    query = (query * cosine + rotated(query) * sine).astype(bf16)
    key = (key * cosine + rotated(key) * sine).astype(bf16)
    query_ref[...] = query * jnp.asarray(HEAD_DIM**-0.5, bf16)
    pair_ref[:, : 2 * half] = key
    pair_ref[:, 2 * half :] = jnp.concatenate(values, axis=1).astype(bf16)


def attend(parts, at, query_ref, *refs):
    pieces, (context_ref, pairs_ref, total_ref) = refs[:parts], refs[parts:]
    start = 0
    for piece in pieces:
        pairs_ref[start : start + piece.shape[0], :] = piece[...]
        start += piece.shape[0]
    width = query_ref.shape[1]
    values = pairs_ref[:, width:].T
    contexts = []
    for h in range(width // HEAD_DIM):
        lanes = slice(h * HEAD_DIM, (h + 1) * HEAD_DIM)
        scores = mm_nt(pairs_ref[:, lanes], query_ref[:, lanes])
        peak = jnp.max(scores, axis=0, keepdims=True)
        log_total = peak + jnp.log(jnp.sum(jnp.exp(scores - peak), axis=0, keepdims=True))
        probs = jnp.exp(scores - log_total).astype(bf16)
        contexts.append(mm(values[lanes], probs))
        total_ref[h : h + 1, :] = log_total
    context_ref[...] = jnp.concatenate(contexts, axis=0).T.astype(bf16)


def feed(chips, count, at, *refs):
    contexts, refs = refs[: len(chips)], refs[len(chips) :]
    weights, refs = both_cores(count, at, refs)
    (out_own, out_other, rows_ref, grad_ref, gains), refs = refs[:5], refs[5:]
    (middle_ref, middle_rows_ref, normed_ref, unit_ref, active_ref, gain_ref, total_ref), refs = refs[:7], refs[7:]
    pieces, scratch = refs[:-1], refs[-1]
    hidden = active_ref.shape[2]
    block, span = middle_ref.shape
    part = total_ref.shape[0]
    middle = rows_ref[...].astype(f32)
    for p, (k, s) in enumerate(chips):
        context = contexts[p][...]
        if s:
            context = jnp.concatenate([context[block:], context[:block]], axis=0)
        middle = middle + mm_nt(context, jnp.concatenate([out_own[p], out_other[p]], axis=1))
    scratch[...] = middle
    middle_ref[...] = scratch[:block, aligned(at[0], span)]
    middle_rows_ref[...] = scratch[aligned(at[0], part), :]
    centred, _ = norm_rows(middle)
    normed_ref[...] = (centred * gains[1:2, :]).astype(bf16)
    scratch[...] = jnp.zeros_like(scratch)
    for b, (weight, starts) in enumerate(weights):
        gate_up = contract(normed_ref, weight, starts, slice(0, 2 * hidden))
        gate, lift = gate_up[:, :hidden], gate_up[:, hidden:]
        share = 0.5 + 0.5 * lax.erf(gate * math.sqrt(0.5))
        bent = gate * share
        active_ref[b] = (bent * lift).astype(bf16)
        slope = share + gate * jnp.exp(-0.5 * gate * gate) * (1.0 / math.sqrt(2.0 * math.pi))
        back = contract(grad_ref, weight, starts, slice(2 * hidden, 3 * hidden))
        unit = jnp.concatenate([back * lift * slope, back * bent], axis=1).astype(bf16)
        unit_ref[b] = unit
        spread(scratch, unit, weight, starts, slice(0, 2 * hidden))
    gain_ref[...] = jnp.sum(scratch[...] * centred, axis=0, keepdims=True)
    cut_rows(chips, at, scratch, total_ref, pieces)


def cut_rows(chips, at, scratch, total_ref, pieces):
    part = total_ref.shape[0]
    columns = scratch.shape[0] // (2 * part)
    for p, (k, s) in enumerate(chips):
        rows = scratch[aligned(s * columns + (at[0] ^ k), part), :]
        if p:
            pieces[p - 1][...] = rows.astype(bf16)
        else:
            total_ref[...] = rows


def turn(at, total_ref, *refs):
    pieces, (middle_ref, grad_ref, gains, grad_middle_ref, low_ref) = refs[:-5], refs[-5:]
    part = total_ref.shape[0]
    total = total_ref[...]
    for piece in pieces:
        total = total + piece[...].astype(f32)
    centred, inverse = norm_rows(middle_ref[...])
    grad = grad_ref[aligned(at[0], part), :].astype(f32)
    grad = grad + norm_backward(total, centred, inverse, gains[1:2, :])
    grad_middle_ref[...] = grad
    low_ref[...] = grad.astype(bf16)


def settle(chips, count, at, *refs):
    weights, refs = both_cores(count, at, refs)
    (normed_ref, unit_ref, active_ref, grad_ref, middle_ref), refs = refs[:5], refs[5:]
    (own_ref, other_ref, total_ref), refs = refs[:3], refs[3:]
    pieces, scratch = refs[:-1], refs[-1]
    hidden = active_ref.shape[2]
    block, span = total_ref.shape
    normed, grad = normed_ref[...].T, grad_ref[...].T
    for b, out in enumerate((other_ref, own_ref)):
        out[:, : 2 * hidden] = mm(normed, unit_ref[1 - b]).astype(bf16)
        out[:, 2 * hidden : 3 * hidden] = mm(grad, active_ref[1 - b]).astype(bf16)
        if out.shape[1] > 3 * hidden:
            out[:, 3 * hidden :] = jnp.zeros((out.shape[0], out.shape[1] - 3 * hidden), bf16)
    scratch[...] = jnp.zeros_like(scratch)
    for b, (weight, starts) in enumerate(weights):
        spread(scratch, active_ref[b], weight, starts, slice(2 * hidden, 3 * hidden))
    for p, (k, s) in enumerate(chips):
        piece = scratch[s * block : (s + 1) * block, aligned(at[0] ^ k, span)]
        if p:
            pieces[p - 1][...] = piece.astype(bf16)
        else:
            total_ref[...] = piece + middle_ref[...]


def reflect(chips, count, at, *refs):
    pieces, refs = refs[: len(chips)], refs[len(chips) :]
    weights, refs = both_cores(count, at, refs)
    query_ref, pairs_ref, total_ref, grad_attn_ref, grad_query_ref, grad_pairs_ref = refs
    part = pieces[0].shape[0]
    rows, width = query_ref.shape
    columns = rows // (2 * part)
    half = width // 2
    for (k, s), piece in zip(chips, pieces):
        grad_attn_ref[aligned(s * columns + (at[0] ^ k), part), :] = piece[...]
    grad_context = jnp.concatenate(
        [contract(grad_attn_ref, weight, starts, slice(3 * half, 4 * half)) for weight, starts in weights],
        axis=1,
    ).astype(bf16)
    keys = pairs_ref[:, :width].T
    grad_queries = []
    for h in range(width // HEAD_DIM):
        lanes = slice(h * HEAD_DIM, (h + 1) * HEAD_DIM)
        query = query_ref[:, lanes]
        grad = grad_context[:, lanes]
        probs = jnp.exp(mm_nt(pairs_ref[:, lanes], query) - total_ref[h : h + 1, :])
        value_lanes = slice(width + h * HEAD_DIM, width + (h + 1) * HEAD_DIM)
        grad_probs = mm_nt(pairs_ref[:, value_lanes], grad)
        delta = jnp.sum(probs * grad_probs, axis=0, keepdims=True)
        grad_scores = (probs * (grad_probs - delta)).astype(bf16)
        grad_pairs_ref[:, lanes] = mm(grad_scores, query).astype(bf16)
        grad_pairs_ref[:, value_lanes] = mm(probs.astype(bf16), grad).astype(bf16)
        grad_queries.append(mm(keys[lanes], grad_scores))
    grad_query_ref[...] = jnp.concatenate(grad_queries, axis=0).T * HEAD_DIM**-0.5


def unwind(chips, count, at, *refs):
    weights, refs = both_cores(count, at, refs)
    (grad_query_ref, grad_pairs_ref, cosine, sine, rows_ref), refs = refs[:5], refs[5:]
    (grad_projected_ref, gain_ref, total_ref), refs = refs[:3], refs[3:]
    pieces, scratch = refs[:-1], refs[-1]
    width = grad_query_ref.shape[1]
    half = width // 2
    cosine, sine = cosine[...], sine[...]
    grad_query, grad_key = grad_query_ref[...], grad_pairs_ref[:, :width]
    grad_query = (grad_query * cosine - rotated(grad_query * sine)).astype(bf16)
    grad_key = (grad_key * cosine - rotated(grad_key * sine)).astype(bf16)
    grad_value = grad_pairs_ref[:, width:].astype(bf16)
    scratch[...] = jnp.zeros_like(scratch)
    for b, (weight, starts) in enumerate(weights):
        lanes = slice(b * half, (b + 1) * half)
        grad = jnp.concatenate([grad_query[:, lanes], grad_key[:, lanes], grad_value[:, lanes]], axis=1)
        grad_projected_ref[b] = grad
        spread(scratch, grad, weight, starts, slice(0, 3 * half))
    centred, _ = norm_rows(rows_ref[...].astype(f32))
    gain_ref[...] = jnp.sum(scratch[...] * centred, axis=0, keepdims=True)
    cut_rows(chips, at, scratch, total_ref, pieces)


def repay(at, normed_ref, grad_projected_ref, grad_attn_ref, context_ref, own_ref, other_ref):
    half = context_ref.shape[1] // 2
    normed, grad_attn = normed_ref[...].T, grad_attn_ref[...].T
    for b, out in ((1, other_ref), (0, own_ref)):
        out[:, : 3 * half] = mm(normed, grad_projected_ref[b]).astype(bf16)
        out[:, 3 * half :] = mm(grad_attn, context_ref[:, b * half : (b + 1) * half]).astype(bf16)


def finish(narrow, at, total_ref, *refs):
    pieces, (rows_ref, grad_middle_ref, gains), outs, scratch = refs[: -narrow - 4], refs[-narrow - 4 : -narrow - 1], refs[-narrow - 1 : -1], refs[-1]
    part = total_ref.shape[0]
    width = outs[0].shape[1]
    total = total_ref[...]
    for piece in pieces:
        total = total + piece[...].astype(f32)
    centred, inverse = norm_rows(rows_ref[aligned(at[0], part), :].astype(f32))
    scratch[...] = grad_middle_ref[...] + norm_backward(total, centred, inverse, gains[0:1, :])
    for m, out in enumerate(outs):
        out[...] = scratch[:, aligned(at[1] ^ m, width)]


def body(
    wide,
    narrow,
    inputs,
    attn_gain,
    query_key_value_weight,
    attention_out_weight,
    mlp_gain,
    feedforward_in_weight,
    feedforward_out_weight,
    grad_out,
):
    groups, columns = wide // 2, narrow // 2
    _, block, width = inputs.shape
    model = width * narrow
    depth = query_key_value_weight.shape[0]
    hidden = feedforward_out_weight.shape[0] // 2
    half, span = width // 2, 2 * width
    part = block // columns
    rows = 2 * block
    length = groups * rows
    wide_at, narrow_at = lax.axis_index("wide"), lax.axis_index("narrow")
    group, side = wide_at // 2, wide_at % 2
    column, core = narrow_at // 2, narrow_at % 2
    chips = [(k, s) for s in range(2) for k in range(columns)]

    unit_mask = 2 * narrow

    def swap(array, mask):
        if mask == 0:
            return array
        return lax.ppermute(
            array, ("wide", "narrow"), [(i, i ^ mask) for i in range(wide * narrow)]
        )

    def over_chips(column_rel, side_rel):
        return 2 * column_rel + narrow * side_rel

    def over_groups(group_rel):
        return 2 * narrow * group_rel

    def after(array, *others):
        return lax.optimization_barrier((array, *others))[0]

    def swap_ways(array, even, odd):
        pairs = [(i, i ^ (odd if i % 2 else even)) for i in range(wide * narrow)]
        return lax.ppermute(array, ("wide", "narrow"), pairs)

    def ring_order(count):
        if count < 4:
            return list(range(count))
        quad = [0, 1 + 2 * core, 3 - 2 * core, 2]
        return [low + 4 * high for high in ring_order(count // 4) for low in quad]

    def ring_first(array, unit):
        return swap(array, unit), swap(array, 3 * unit)

    def ring_last(second, unit):
        return swap(second, unit)

    def gather_order(count):
        if count < 4:
            return list(range(count))
        return [low + 4 * high for high in gather_order(count // 4) for low in (0, 1, 3, 2)]

    def gather_ring(array, unit, count):
        if count < 4:
            return [swap(array, unit * k) for k in range(count)]
        first, second = ring_first(array, unit)
        quad = [array, first, second, ring_last(second, unit)]
        if count == 4:
            return quad
        return [q for quads in gather_ring(jnp.stack(quad), 4 * unit, count // 4) for q in quads]

    def scatter_first(pieces, unit, turn_odd=True):
        count = len(pieces)
        if count < 4:
            return pieces, None
        if count > 4:
            stacked = [jnp.stack(pieces[k : k + 4]) for k in range(0, count, 4)]
            pieces = list(scatter_ring(stacked, 4 * unit, turn_odd))
        own, first, second, across = pieces
        odd = 3 * unit if turn_odd else unit
        passing = swap_ways(across.astype(bf16), unit, odd)
        arrived = swap_ways(first.astype(bf16), unit, odd)
        return own, (second, passing, arrived)

    def scatter_last(own, state, unit, turn_odd=True):
        if state is None:
            total = own[0].astype(f32)
            for k in range(1, len(own)):
                total = total + swap(own[k].astype(bf16), unit * k).astype(f32)
            return total
        second, passing, arrived = state
        second = (second.astype(f32) + passing.astype(f32)).astype(bf16)
        return own.astype(f32) + arrived.astype(f32) + swap_ways(second, 3 * unit, unit if turn_odd else 3 * unit).astype(f32)

    def scatter_ring(pieces, unit, turn_odd):
        return scatter_last(*scatter_first(pieces, unit, turn_odd), unit, turn_odd)

    def place_groups(pieces, order):
        size = pieces[0].shape[0]
        whole = jnp.zeros((size * groups, pieces[0].shape[1]), pieces[0].dtype)
        for relative, piece in zip(order, pieces):
            whole = lax.dynamic_update_slice_in_dim(whole, piece, (group ^ relative) * size, 0)
        return whole

    def fetch_side(bundle):
        received = swap(pick(bundle, 1 - side), narrow)
        return place([pick(bundle, side), received], side, 0)

    def halves(array):
        return array.reshape(depth, -1, 2, array.shape[-1] // 2).transpose(2, 0, 1, 3)

    def from_chips(array):
        return [swap(array, over_chips(k, s)) for k, s in chips]

    def to_chips(pieces):
        return [swap(piece, over_chips(k, s)) for (k, s), piece in zip(chips[1:], pieces)]

    def reduce_cores(own, other, *others):
        received = after(swap(other, 1), *others)

        def places(*later):
            blocks = []
            for place_at, k in enumerate(ring_order(groups)):
                pair = (own, received)
                if later and place_at % 2 == 0:
                    pair = lax.optimization_barrier((own, received, *later))[:2]
                pair = [pick(array.reshape(groups, 2 * depth, -1), group ^ k).astype(f32) for array in pair]
                blocks.append(pair[0] + pair[1])
            return blocks

        return places

    def scatter_early(places):
        if groups != 4:
            return scatter_first(places(), unit_mask)
        _, first, _, across = places()
        return swap_ways(across.astype(bf16), unit_mask, 3 * unit_mask), swap_ways(first.astype(bf16), unit_mask, 3 * unit_mask)

    def scatter_late(places, state, *later):
        if groups != 4:
            return scatter_last(*state, unit_mask)
        own, _, second, _ = places(*later)
        return scatter_last(own, (second, *state), unit_mask)

    def reduce_side(total):
        total = total.reshape(2, depth, -1)
        kept = pick(total, side)
        received = swap(pick(total, 1 - side).astype(bf16), narrow).astype(f32)
        return place([kept[None], received[None]], side, 0)

    def join(array):
        return array.transpose(1, 2, 0, 3).reshape(depth, array.shape[2], -1)

    attn_bundle = jnp.concatenate(
        [halves(query_key_value_weight), halves(attention_out_weight.T[:, None])], axis=2
    ).reshape(2, depth, 4 * half)
    mlp_bundle = jnp.concatenate(
        [halves(feedforward_in_weight), halves(feedforward_out_weight.T[:, None])], axis=2
    ).reshape(2, depth, 3 * hidden)
    lanes = -(-3 * hidden // 128) * 128
    mlp_bundle = jnp.pad(mlp_bundle, ((0, 0), (0, 0), (0, lanes - 3 * hidden)))

    both = jnp.stack([inputs, grad_out])
    received = swap(pick(both, 1 - core, 1), 1)
    features = place([pick(both, core, 1), received], core, 2)
    attn_pair = fetch_side(attn_bundle)
    shards = from_chips(features)
    gains = after(jnp.stack([attn_gain, mlp_gain]), shards)
    gains = place([gains, swap(gains, 1)], core, 1)
    gains = place([swap(gains, 2 * k) for k in range(columns)], column, 1)
    mlp_pair = fetch_side(after(mlp_bundle, shards))
    if groups >= 4:
        quad = [attn_pair, *ring_first(attn_pair, unit_mask)]
        quad, shards = lax.optimization_barrier((quad, shards))
        quad.append(ring_last(quad[2], unit_mask))
        if groups > 4:
            quad = [q for quads in gather_ring(jnp.stack(quad), 4 * unit_mask, groups // 4) for q in quads]
    else:
        quad = gather_ring(attn_pair, unit_mask, groups)
    order = turned = gather_order(groups)
    count = groups if 2 * depth % 128 == 0 else 1
    starts = [group ^ k for k in order] + [group ^ k for k in turned] if count > 1 else [0, 0]

    def both_blocks(own, other):
        return [*own, *other] if count > 1 else [place_groups(own, order), place_groups(other, turned)]

    token = (jnp.arange(rows) // block) ^ side
    positions = ((group * 2 + token) * block + jnp.arange(rows) % block).astype(f32)
    cosine, sine = rope_tables(positions, width)
    at = jnp.stack([column, narrow_at, *starts]).astype(jnp.int32)
    early = [swap(piece, 1) for piece in quad[:3]]
    mlp_pair, gains, quad, early, cosine, sine, at = lax.optimization_barrier(
        (mlp_pair, gains, quad, early, cosine, sine, at)
    )
    attn_weights = both_blocks(quad, [*early, *[swap(piece, 1) for piece in quad[len(early) :]]])
    mlp_quad = [mlp_pair, *ring_first(mlp_pair, unit_mask)] if groups >= 4 else []

    rows_in, grad_rows, normed_one, query, pair = call(
        functools.partial(project, chips, count),
        [((rows, model), bf16)] * 3 + [((rows, width), bf16), ((rows, span), bf16)],
        at, *shards, *attn_weights, gains, cosine, sine,
    )
    out_own = place_groups([after(piece[:, 3 * half :], pair) for piece in quad], order)
    out_own = from_chips(out_own)
    if groups == 4:
        (first, second), mlp_quad, out_own = lax.optimization_barrier((ring_first(pair, unit_mask), mlp_quad, out_own))
        pairs = [pair, first, second, ring_last(second, unit_mask)]
    else:
        pairs = gather_ring(pair, unit_mask, groups)
    pairs, out_own, early = lax.optimization_barrier((pairs, out_own, mlp_quad))
    early = [swap(piece, 1) for piece in early]
    out_own = jnp.stack(out_own)
    out_other = swap(out_own, 1)
    if groups >= 4:
        mlp_quad.append(ring_last(after(mlp_quad[2], pairs), unit_mask))
    context, pairs, total = call(
        functools.partial(attend, len(pairs)),
        [((rows, width), bf16), ((length, span), bf16), ((8, rows), f32)],
        at, query, *pairs,
    )
    contexts = from_chips(context)
    if groups >= 4:
        late = after(mlp_quad.pop(), contexts)
        mlp_quad, early = [*mlp_quad, late], [*early, swap(late, 1)]
        if groups > 4:
            mlp_quad = [q for quads in gather_ring(jnp.stack(mlp_quad), 4 * unit_mask, groups // 4) for q in quads]
            early = [swap(piece, 1) for piece in mlp_quad]
    else:
        mlp_quad = gather_ring(mlp_pair, unit_mask, groups)
        early = [swap(piece, 1) for piece in mlp_quad]
    mlp_weights = both_blocks(mlp_quad, early)
    middle, middle_rows, normed_two, unit, active, mlp_gain_part, grad_two, *sends = call(
        functools.partial(feed, chips, count),
        [((block, span), f32), ((part, model), f32), ((rows, model), bf16), ((2, rows, 2 * hidden), bf16),
         ((2, rows, hidden), bf16), ((1, model), f32), ((part, model), f32)] + [((part, model), bf16)] * (len(chips) - 1),
        at, *contexts, *mlp_weights, out_own, out_other, rows_in, grad_rows, gains,
        scratch=[((rows, model), f32)],
    )
    received = to_chips(sends)
    grad_mlp_own, grad_mlp_other, branch, *branch_sends = call(
        functools.partial(settle, chips, count),
        [((model, lanes), bf16)] * 2 + [((block, span), f32)] + [((block, span), bf16)] * (len(chips) - 1),
        at, *mlp_weights, normed_two, unit, active, grad_rows, middle,
        scratch=[((rows, model), f32)],
    )
    grad_mlp_other = after(grad_mlp_other, received)
    grad_middle, grad_low = call(
        functools.partial(turn), [((part, model), f32), ((part, model), bf16)],
        at, grad_two, *received, middle_rows, grad_rows, gains,
    )
    grad_pieces = from_chips(grad_low)
    grad_mlp = reduce_cores(grad_mlp_own, grad_mlp_other, grad_low)
    mlp_state = scatter_early(grad_mlp)
    grad_attn, grad_query, grad_pairs = call(
        functools.partial(reflect, chips, count),
        [((rows, model), bf16), ((rows, width), f32), ((length, span), bf16)],
        at, *grad_pieces, *attn_weights, query, pairs, total,
    )
    if groups >= 4:
        mlp_state, grad_pairs, branch_sends = lax.optimization_barrier((mlp_state, grad_pairs, branch_sends))
    grad_pairs = scatter_ring(list(grad_pairs.reshape(groups, rows, span)), unit_mask, False)

    branch_received = to_chips(branch_sends)
    grad_pairs, mlp_state, branch_received = lax.optimization_barrier((grad_pairs, mlp_state, branch_received))
    for piece in branch_received:
        branch = branch + piece.astype(f32)
    branch = branch.astype(bf16).reshape(block, 2, width)
    result = place([pick(branch, core, 1)[None], swap(pick(branch, 1 - core, 1), 1)[None]], core, 0)

    grad_mlp = scatter_late(grad_mlp, mlp_state, grad_query)
    grad_projected, attn_gain_part, grad_one, *sends = call(
        functools.partial(unwind, chips, count),
        [((2, rows, 3 * half), bf16), ((1, model), f32), ((part, model), f32)] + [((part, model), bf16)] * (len(chips) - 1),
        at, *attn_weights, grad_query, grad_pairs, cosine, sine, rows_in,
        scratch=[((rows, model), f32)],
    )
    received = to_chips(sends)
    grad_attn_own, grad_attn_other = call(
        functools.partial(repay), [((model, 4 * half), bf16)] * 2,
        at, normed_one, grad_projected, grad_attn, context,
    )
    grad_attn_other, grad_mlp, received = lax.optimization_barrier((grad_attn_other, grad_mlp, received))
    gain_grads = jnp.concatenate([after(attn_gain_part, *received), mlp_gain_part], axis=0).reshape(2, narrow, width)
    gain_total = pick(gain_grads, narrow_at, 1)
    for m in range(1, narrow):
        gain_total = gain_total + swap(pick(gain_grads, narrow_at ^ m, 1), m)
    attn_places = reduce_cores(grad_attn_own, grad_attn_other, gain_total)
    summed = [piece.astype(bf16) for piece in attn_places()[1::2]]
    state = scatter_early(attn_places)
    finished = call(
        functools.partial(finish, narrow), [((part, width), f32)] * narrow,
        at, after(grad_one, *summed), *received, rows_in, grad_middle, gains,
        scratch=[((part, model), f32)],
    )
    sends = [swap(piece, m) for m, piece in enumerate(finished)]
    gain_total = after(gain_total, *summed)
    gain_total = gain_total + swap(gain_total, narrow)
    sends, state, gain_total = lax.optimization_barrier((sends, state, gain_total))
    grad_mlp = after(grad_mlp, *summed)
    grad_mlp = join(reduce_side(grad_mlp)[..., : 3 * hidden].reshape(2, depth, 3, hidden))
    grad_attn_weight = scatter_late(attn_places, state, finished[0])
    gain_total = after(gain_total, grad_attn_weight)
    if groups == 4:
        near, across, far = [swap(gain_total, unit_mask * k) for k in (1, 2, 3)]
        gain_total = (gain_total + near) + (across + far)
    else:
        for mask in ring_masks(groups):
            gain_total = gain_total + swap(gain_total, unit_mask * mask)
    grad_attn_weight = join(reduce_side(grad_attn_weight).reshape(2, depth, 4, half))
    grad_inputs = place(
        [place([sends[2 * k + c] for k in range(columns)], column, 0)[None] for c in range(2)],
        core, 0,
    )
    return (
        result,
        grad_inputs,
        gain_total[0],
        grad_attn_weight[:, :3],
        grad_attn_weight[:, 3].T,
        gain_total[1],
        grad_mlp[:, :2],
        grad_mlp[:, 2].T,
    )


def solution(mesh):
    in_specs = (
        P(None, "wide", "narrow"),
        P("narrow"),
        P("wide", None, "narrow"),
        P("narrow", "wide"),
        P("narrow"),
        P("wide", None, "narrow"),
        P("narrow", "wide"),
        P(None, "wide", "narrow"),
    )
    out_specs = (
        P(None, "wide", "narrow"),
        P(None, "wide", "narrow"),
        P("narrow"),
        P("wide", None, "narrow"),
        P("narrow", "wide"),
        P("narrow"),
        P("wide", None, "narrow"),
        P("narrow", "wide"),
    )
    step = functools.partial(body, mesh.shape["wide"], mesh.shape["narrow"])
    return jax.shard_map(step, mesh=mesh, in_specs=in_specs, out_specs=out_specs, check_vma=False)
```
